32 devices in a mesh: ctx: 8 (over z, y), fsdp: 4 (over x, core).
Axes of the slice: x: 2, y: 2, z: 4, core: 2. Of those that a mesh axis runs over, the one named last changes fastest.
Arguments:
- tokens: bfloat16 [4, 1024, 768], P('fsdp', 'ctx'), may hold values from -6 to 6
- routes: int32 [4, 1024, 2], P('fsdp', 'ctx'), may hold values from 0 to 63, all different within a row; in each aligned block of 128 rows (0 to 127, 128 to 255, ..., all dimensions but the last counted through in order) at most 8 rows name the same one
- cotangent: bfloat16 [4, 1024, 768], P('fsdp', 'ctx'), may hold values from -6 to 6
- gains: bfloat16 [2, 768], P(None, ('ctx', 'fsdp')), may hold values from 0.25 to 1.75
- rel_bias: bfloat16 [384], P(('ctx', 'fsdp')), may hold values from -4 to 4
- attn_qkv: bfloat16 [2304, 768], P(('ctx', 'fsdp')), may hold values from -1.25 to 1.25
- attn_out: bfloat16 [768, 768], P(('ctx', 'fsdp')), may hold values from -0.875 to 0.875
- router: bfloat16 [768, 64], P(('ctx', 'fsdp')), may hold values from -0.875 to 0.875
- w_in: bfloat16 [64, 768, 3072], P('ctx', None, 'fsdp'), may hold values from -0.21875 to 0.21875
- w_out: bfloat16 [64, 3072, 768], P('ctx', 'fsdp'), may hold values from -0.109375 to 0.109375
Outputs:
- mixed: bfloat16 [4, 1024, 768], P('fsdp', 'ctx')
- d_tokens: float32 [4, 1024, 768], P('fsdp', 'ctx')
- d_gains: float32 [2, 768], P(None, ('ctx', 'fsdp'))
- d_rel_bias: float32 [384], P(('ctx', 'fsdp'))
- d_attn_qkv: float32 [2304, 768], P(('ctx', 'fsdp'))
- d_attn_out: float32 [768, 768], P(('ctx', 'fsdp'))
- d_router: float32 [768, 64], P(('ctx', 'fsdp'))
- d_w_in: float32 [64, 768, 3072], P('ctx', None, 'fsdp')
- d_w_out: float32 [64, 3072, 768], P('ctx', 'fsdp')
The draws below stay inside these ranges and needn't reach their ends.
Inputs may be any that keep to these rules, and one draw needn't show every extreme that they name: The two routes of a token name different experts. In each aligned block of 128 tokens of a sequence no expert is named more than 8 times, and some block names some expert exactly 8 times.
All inputs are finite; a program needn't handle non-finite values.
Results may differ from the reference program's by a relative error of at most 0.017.
The reference program's roundings to bfloat16 on the way count: a program that leaves them out, or rounds other values in their place, can miss the bound.
Values may be sent and summed in bfloat16 or wider, within the bound.
A program may use at most 320 MiB of HBM per device.

```python
import math
import jax
import jax.numpy as jnp
import numpy as np
from jax import lax

D = 768
H = 12
DH = 64
FF = 3072
E = 64
NB = 32
TOK_DEV = 128
CAP = 8
LEN = 1024
SEQS = 4
N_CTX = 8


def draw_attn_qkv(key, part):
    base = jax.random.truncated_normal(jax.random.fold_in(key, 11), -6.0, 6.0, (3 * D, D), jnp.float32)
    return (base / jnp.sqrt(jnp.float32(D))).astype(jnp.bfloat16)


def shard_levels(key, extent, shards, smallest, high):
    gain, own = 1.0, jax.random.fold_in(key, 6)
    for dim, parts in shards:
        draws = jnp.exp(jax.random.uniform(jax.random.fold_in(own, dim), (parts,), jnp.float32, smallest / len(shards), high / len(shards)))
        gain = gain * jnp.repeat(draws, extent[dim] // parts).reshape([-1 if axis == dim else 1 for axis in range(len(extent))])
    return gain


def shared_out(rng, own, number, rows, amount, top, most, lean):
    sequence = jax.random.permutation(rng, amount)
    packed, common = shares(amount, rows * top, most, lean, True), shares(amount, rows * top, most, lean, False)
    places = jnp.arange(amount)

    def named(sizes, rotation):
        used = int((sizes > 0).sum())
        fixed = max(1, used // 4)
        shifted = fixed + (places - fixed + rotation * (used - fixed)) % max(1, amount - fixed)
        return jnp.zeros((amount,), jnp.int32).at[sequence[jnp.where(places < fixed, places, shifted)]].set(jnp.asarray(sizes, jnp.int32))

    sizes = jnp.where(number % 4 == 0, named(packed, number // 4), named(common, number - number // 4 - 1))
    mixed = jax.random.permutation(jax.random.fold_in(own, 3), amount)
    donor, taker = mixed[0:amount // 2 * 2:2], mixed[1:amount // 2 * 2:2]
    slack = jnp.minimum(sizes[donor] - 1, most - sizes[taker]) // 2
    slack = jnp.where((donor == sequence[0]) | (taker == sequence[0]) | (sizes[taker] == 0), 0, jnp.maximum(slack, 0))
    shifted = jax.random.randint(jax.random.fold_in(own, 4), (amount // 2,), 0, 1 << 20) % (slack + 1)
    sizes = sizes.at[donor].add(-shifted).at[taker].add(shifted)
    items = jnp.searchsorted(jnp.cumsum(sizes), jnp.arange(rows * top), side="right").astype(jnp.int32)
    grid = items.reshape(top, rows).T
    grid = grid[jax.random.permutation(jax.random.fold_in(own, 1), rows)]
    rotation = jax.random.randint(jax.random.fold_in(own, 2), (rows, 1), 0, top)
    return jnp.take_along_axis(grid, (jnp.arange(top)[None, :] + rotation) % top, axis=1)


def shares(amount, total, most, lean, full):
    portions = [(1 << 20) // math.isqrt(standing ** lean) + 1 for standing in range(1, amount + 1)]
    largest = most if full else min(most, max(-(-total // amount), total * portions[0] // sum(portions)))
    least = 1 if total - largest >= amount - 1 else 0
    given, surplus = [largest] + [least] * (amount - 1), total - largest - least * (amount - 1)
    while surplus > 0:
        free = [i for i in range(1, amount) if given[i] < largest] or [i for i in range(1, amount) if given[i] < most]
        whole, left = sum([portions[i] for i in free]), surplus
        for i in free:
            addition = min(most - given[i], max(1, left * portions[i] // whole), surplus)
            given[i] = given[i] + addition
            surplus = surplus - addition
    return np.array(given)


def normal_values(key, shape, width, reach, cuts=(), kind=jnp.bfloat16):
    values = width * jax.random.normal(key, shape, jnp.float32)
    if cuts:
        values = values * shard_levels(key, shape, cuts, -0.22, 0.18)
    return jnp.clip(values, -reach, reach).astype(kind)


def setup_inputs(seed: int = 0) -> dict:
    arg_keys = jax.random.split(jax.random.key(seed), 11)
    tokens = normal_values(arg_keys[0], (SEQS, LEN, D), 1.0, 6.0, ((0, 4), (1, 8)))
    routes_keys = jax.random.split(jax.random.fold_in(arg_keys[1], 1), SEQS * LEN // TOK_DEV)
    routes_turns = jax.random.permutation(jax.random.fold_in(arg_keys[1], 3), SEQS * LEN // TOK_DEV)
    routes = jax.vmap(lambda own, number: shared_out(jax.random.fold_in(arg_keys[1], 2), own, number, TOK_DEV, E, 2, CAP, 2))(routes_keys, routes_turns).reshape((SEQS, LEN, 2))
    cotangent = normal_values(arg_keys[2], (SEQS, LEN, D), 1.0, 6.0, ((0, 4), (1, 8)))
    gains = jnp.clip(1.0 + 0.15 * jax.random.normal(arg_keys[3], (2, D), jnp.float32), 0.25, 1.75).astype(jnp.bfloat16)
    rel_bias = normal_values(arg_keys[4], (H * NB,), 1.0, 4.0, ((0, 32),))
    attn_qkv = draw_attn_qkv(jax.random.fold_in(arg_keys[10], 71), 0)
    attn_out = normal_values(arg_keys[6], (D, D), (D // 16) ** -0.5, 0.875, ((0, 32),))
    router = normal_values(arg_keys[7], (D, E), (D // 16) ** -0.5, 0.875, ((0, 32),))
    w_in = normal_values(arg_keys[8], (E, D, FF), D ** -0.5, 0.21875, ((0, 8), (2, 4)))
    w_out = normal_values(arg_keys[9], (E, FF, D), FF ** -0.5, 0.109375, ((0, 8), (1, 4)))
    return dict(tokens=tokens, routes=routes, cotangent=cotangent, gains=gains, rel_bias=rel_bias, attn_qkv=attn_qkv, attn_out=attn_out, router=router, w_in=w_in, w_out=w_out)


EPS = 1e-06
EDGES = (16, 23, 32, 45, 64, 91, 128, 181, 256, 362, 512, 724, 1024, 1448, 2048, 2896)
GELU_C = 0.7978845608028654
NEG = -1e+30

def bucket_of(offset):
    clipped = jnp.maximum(offset, 0)
    far = 15 + sum(((clipped >= edge).astype(jnp.int32) for edge in EDGES))
    return jnp.where(clipped < 16, clipped, far).astype(jnp.int32)

def norm_forward(values):
    inverse_norm = lax.rsqrt(lax.optimization_barrier(jnp.mean(values * values, axis=-1, keepdims=True)) + EPS)
    return (values * inverse_norm, inverse_norm)

def norm_backward(normalized_gradient, centered_rows, inverse_norm, gain_vector):
    centered_gradient = normalized_gradient * gain_vector
    gain_gradient = lax.optimization_barrier(jnp.sum(normalized_gradient * centered_rows, axis=0))
    value_gradients = inverse_norm * (centered_gradient - centered_rows * lax.optimization_barrier(jnp.mean(centered_gradient * centered_rows, axis=-1, keepdims=True)))
    return (value_gradients, gain_gradient)

def gelu_parts(pre):
    inner = GELU_C * (pre + 0.044715 * pre * pre * pre)
    tanh_v = jnp.tanh(inner)
    value = 0.5 * pre * (1.0 + tanh_v)
    slope = 0.5 * (1.0 + tanh_v) + 0.5 * pre * (1.0 - tanh_v * tanh_v) * GELU_C * (1.0 + 3.0 * 0.044715 * pre * pre)
    return (value, slope)

def block_scores(qpart, kpart, bias_table, qstart, kstart, scale):
    score = jnp.einsum('qhd,khd->hqk', qpart.astype(jnp.float32), kpart.astype(jnp.float32)) * scale
    offset = (qstart + jnp.arange(qpart.shape[0], dtype=jnp.int32))[:, None] - (kstart + jnp.arange(kpart.shape[0], dtype=jnp.int32))[None, :]
    bias_term = jnp.take(bias_table, bucket_of(offset), axis=1)
    return (jnp.where(offset[None] >= 0, score + bias_term, -jnp.inf), offset)

def reference(tokens, routes, cotangent, gains, rel_bias, attn_qkv, attn_out, router, w_in, w_out):
    single_float = jnp.float32
    bfloat_half = jnp.bfloat16
    rows = SEQS * LEN
    scale = 1.0 / math.sqrt(DH)
    qblk = math.gcd(LEN, 512)
    nqb = LEN // qblk
    input_rows = tokens.reshape(rows, D).astype(single_float)
    first_gain = gains[0].astype(single_float)
    second_gain = gains[1].astype(single_float)
    bias_table = rel_bias.astype(single_float).reshape(H, NB)
    w_qkv = attn_qkv.reshape(3, D, D)
    first_centered, first_inverse_norm = norm_forward(input_rows)
    first_normalized = (first_centered * first_gain).astype(bfloat_half)
    q = jnp.dot(first_normalized, w_qkv[0], preferred_element_type=single_float).astype(bfloat_half)
    k = jnp.dot(first_normalized, w_qkv[1], preferred_element_type=single_float).astype(bfloat_half)
    v = jnp.dot(first_normalized, w_qkv[2], preferred_element_type=single_float).astype(bfloat_half)
    heads_q = q.reshape(SEQS, LEN, H, DH)
    heads_k = k.reshape(SEQS, LEN, H, DH)
    heads_v = v.reshape(SEQS, LEN, H, DH)

    def forward_block(index):
        seq = (index // nqb).astype(jnp.int32)
        qstart = (index % nqb * qblk).astype(jnp.int32)
        qseq = lax.dynamic_index_in_dim(heads_q, seq, 0, keepdims=False)
        kseq = lax.dynamic_index_in_dim(heads_k, seq, 0, keepdims=False)
        vseq = lax.dynamic_index_in_dim(heads_v, seq, 0, keepdims=False)
        qpart = lax.dynamic_slice_in_dim(qseq, qstart, qblk, 0)

        def step(carry, kidx):
            run_max, total, acc = carry
            kstart = (kidx * qblk).astype(jnp.int32)
            kpart = lax.dynamic_slice_in_dim(kseq, kstart, qblk, 0)
            vpart = lax.dynamic_slice_in_dim(vseq, kstart, qblk, 0)
            score, _ = block_scores(qpart, kpart, bias_table, qstart, kstart, scale)
            newest = jnp.maximum(run_max, lax.optimization_barrier(jnp.max(score, axis=-1)))
            factor = jnp.exp(run_max - newest)
            weights = jnp.exp(score - newest[..., None])
            total = total * factor + lax.optimization_barrier(jnp.sum(weights, axis=-1))
            acc = acc * factor[..., None] + jnp.einsum('hqk,khd->hqd', weights.astype(bfloat_half).astype(single_float), vpart.astype(single_float))
            return ((newest, total, acc), None)
        init = (jnp.full((H, qblk), NEG, single_float), jnp.zeros((H, qblk), single_float), jnp.zeros((H, qblk, DH), single_float))
        (run_max, total, acc), _ = lax.scan(step, init, jnp.arange(nqb, dtype=jnp.int32))
        attended = (acc / total[..., None]).transpose(1, 0, 2).reshape(qblk, D).astype(bfloat_half)
        return (attended, run_max + jnp.log(total))
    attended_all, lse_all = lax.map(forward_block, jnp.arange(SEQS * nqb, dtype=jnp.int32))
    attended = attended_all.reshape(rows, D)
    lse_seq = lse_all.reshape(SEQS, nqb, H, qblk).transpose(0, 2, 1, 3).reshape(SEQS, H, LEN)
    first_hidden = input_rows + jnp.dot(attended, attn_out, preferred_element_type=single_float)
    second_centered, second_inverse_norm = norm_forward(first_hidden)
    second_normalized = (second_centered * second_gain).astype(bfloat_half)
    logits = jnp.dot(second_normalized, router, preferred_element_type=single_float)
    flat_routes = routes.reshape(rows, 2)
    chosen = jnp.take_along_axis(logits, flat_routes, axis=1)
    gate = jax.nn.softmax(chosen, axis=-1)
    nblk = SEQS * N_CTX
    assign = routes.reshape(nblk, 2 * TOK_DEV)
    member = (assign[..., None] == jnp.arange(E, dtype=jnp.int32)).astype(jnp.int32)
    slot = lax.optimization_barrier(jnp.sum((jnp.cumsum(member, axis=1) - member) * member, axis=-1)).astype(jnp.int32)
    doubled = jnp.repeat(second_normalized.reshape(nblk, TOK_DEV, D), 2, axis=1)
    block_ids = jnp.broadcast_to(jnp.arange(nblk, dtype=jnp.int32)[:, None], (nblk, 2 * TOK_DEV))
    buffer = jnp.zeros((nblk, E, CAP, D), bfloat_half).at[block_ids, assign, slot].set(doubled)
    expert_rows = buffer.transpose(1, 0, 2, 3).reshape(E, nblk * CAP, D)

    def expert_fwd(items):
        rows_e, win, wout = items
        hid, _ = gelu_parts(jnp.dot(rows_e, win, preferred_element_type=single_float))
        return jnp.dot(hid.astype(bfloat_half), wout, preferred_element_type=single_float).astype(bfloat_half)
    expert_out = lax.map(expert_fwd, (expert_rows, w_in, w_out))
    out_buffer = expert_out.reshape(E, nblk, CAP, D).transpose(1, 0, 2, 3)
    picked = out_buffer[block_ids, assign, slot].astype(single_float).reshape(rows, 2, D)
    mixed = (first_hidden + lax.optimization_barrier(jnp.sum(gate[..., None] * picked, axis=1))).astype(bfloat_half)
    dy = cotangent.reshape(rows, D).astype(single_float)
    dgate = lax.optimization_barrier(jnp.sum(dy[:, None, :] * picked, axis=-1))
    dchosen = gate * (dgate - lax.optimization_barrier(jnp.sum(gate * dgate, axis=-1, keepdims=True)))
    columns = (flat_routes[..., None] == jnp.arange(E, dtype=jnp.int32)).astype(single_float)
    dlogits = lax.optimization_barrier(jnp.sum(columns * dchosen[..., None], axis=1)).astype(bfloat_half)
    dpicked = (gate[..., None] * dy[:, None, :]).astype(bfloat_half).reshape(nblk, 2 * TOK_DEV, D)
    dbuffer = jnp.zeros((nblk, E, CAP, D), bfloat_half).at[block_ids, assign, slot].set(dpicked)
    dexpert_rows = dbuffer.transpose(1, 0, 2, 3).reshape(E, nblk * CAP, D)

    def expert_bwd(items):
        rows_e, drows, win, wout = items
        pre = jnp.dot(rows_e, win, preferred_element_type=single_float)
        hid, slope = gelu_parts(pre)
        dhid = jnp.dot(drows, wout.T, preferred_element_type=single_float)
        dpre = (dhid * slope).astype(bfloat_half)
        dwout = jnp.dot(hid.astype(bfloat_half).T, drows, preferred_element_type=single_float)
        dwin = jnp.dot(rows_e.T, dpre, preferred_element_type=single_float)
        dreturn = jnp.dot(dpre, win.T, preferred_element_type=single_float).astype(bfloat_half)
        return (dreturn, dwin, dwout)
    dreturn, d_w_in, d_w_out = lax.map(expert_bwd, (expert_rows, dexpert_rows, w_in, w_out))
    dreturn_buffer = dreturn.reshape(E, nblk, CAP, D).transpose(1, 0, 2, 3)
    dpicked_back = dreturn_buffer[block_ids, assign, slot].astype(single_float).reshape(rows, 2, D)
    second_normalized_gradient = lax.optimization_barrier(jnp.sum(dpicked_back, axis=1)) + jnp.dot(dlogits, router.T, preferred_element_type=single_float)
    d_router = jnp.dot(second_normalized.T, dlogits, preferred_element_type=single_float)
    second_norm_gradient, second_gain_gradient = norm_backward(second_normalized_gradient, second_centered, second_inverse_norm, second_gain)
    dh1 = dy + second_norm_gradient
    dh1_bf = dh1.astype(bfloat_half)
    d_attn_out = jnp.dot(attended.T, dh1_bf, preferred_element_type=single_float)
    dattended = jnp.dot(dh1_bf, attn_out.T, preferred_element_type=single_float).astype(bfloat_half)
    delta = lax.optimization_barrier(jnp.sum((dattended.astype(single_float) * attended.astype(single_float)).reshape(SEQS, LEN, H, DH), axis=-1)).transpose(0, 2, 1)
    heads_do = dattended.reshape(SEQS, LEN, H, DH)

    def backward_seq(seq):
        qseq = lax.dynamic_index_in_dim(heads_q, seq, 0, keepdims=False)
        kseq = lax.dynamic_index_in_dim(heads_k, seq, 0, keepdims=False)
        vseq = lax.dynamic_index_in_dim(heads_v, seq, 0, keepdims=False)
        doseq = lax.dynamic_index_in_dim(heads_do, seq, 0, keepdims=False)
        lse_here = lax.dynamic_index_in_dim(lse_seq, seq, 0, keepdims=False)
        delta_here = lax.dynamic_index_in_dim(delta, seq, 0, keepdims=False)

        def step(carry, qidx):
            dk, dv, dtable = carry
            qstart = (qidx * qblk).astype(jnp.int32)
            qpart = lax.dynamic_slice_in_dim(qseq, qstart, qblk, 0)
            dopart = lax.dynamic_slice_in_dim(doseq, qstart, qblk, 0)
            lse_part = lax.dynamic_slice_in_dim(lse_here, qstart, qblk, 1)
            delta_part = lax.dynamic_slice_in_dim(delta_here, qstart, qblk, 1)
            score, offset = block_scores(qpart, kseq, bias_table, qstart, jnp.int32(0), scale)
            weight = jnp.exp(score - lse_part[..., None])
            weight_bf = weight.astype(bfloat_half).astype(single_float)
            dweight = jnp.einsum('qhd,khd->hqk', dopart.astype(single_float), vseq.astype(single_float))
            score_gradient = weight * (dweight - delta_part[..., None])
            dscore_bf = score_gradient.astype(bfloat_half).astype(single_float)
            summed = jax.ops.segment_sum(score_gradient.transpose(1, 2, 0).reshape(qblk * LEN, H), bucket_of(offset).reshape(-1), num_segments=NB)
            dq_part = jnp.einsum('hqk,khd->qhd', dscore_bf, kseq.astype(single_float)) * scale
            dk = dk + jnp.einsum('hqk,qhd->khd', dscore_bf, qpart.astype(single_float)) * scale
            dv = dv + jnp.einsum('hqk,qhd->khd', weight_bf, dopart.astype(single_float))
            return ((dk, dv, dtable + summed.T), dq_part)
        init = (jnp.zeros((LEN, H, DH), single_float), jnp.zeros((LEN, H, DH), single_float), jnp.zeros((H, NB), single_float))
        (dk, dv, dtable), dq_parts = lax.scan(step, init, jnp.arange(nqb, dtype=jnp.int32))
        return (dq_parts.reshape(LEN, D).astype(bfloat_half), dk.reshape(LEN, D).astype(bfloat_half), dv.reshape(LEN, D).astype(bfloat_half), dtable)
    dq_all, dk_all, dv_all, dtables = lax.map(backward_seq, jnp.arange(SEQS, dtype=jnp.int32))
    grads_in = (dq_all.reshape(rows, D), dk_all.reshape(rows, D), dv_all.reshape(rows, D))
    d_attn_qkv = jnp.concatenate([jnp.dot(first_normalized.T, part, preferred_element_type=single_float) for part in grads_in], axis=0)
    first_normalized_gradient = jnp.dot(grads_in[0], w_qkv[0].T, preferred_element_type=single_float) + jnp.dot(grads_in[1], w_qkv[1].T, preferred_element_type=single_float) + jnp.dot(grads_in[2], w_qkv[2].T, preferred_element_type=single_float)
    first_norm_gradient, first_gain_gradient = norm_backward(first_normalized_gradient, first_centered, first_inverse_norm, first_gain)
    d_tokens = (dh1 + first_norm_gradient).reshape(SEQS, LEN, D)
    d_gains = jnp.stack([first_gain_gradient, second_gain_gradient])
    d_rel_bias = lax.optimization_barrier(jnp.sum(dtables, axis=0)).reshape(H * NB)
    return (mixed.reshape(SEQS, LEN, D), d_tokens, d_gains, d_rel_bias, d_attn_qkv, d_attn_out, d_router, d_w_in, d_w_out)
```

```python
import functools
import math

import jax
import jax.numpy as jnp
from jax import lax
from jax.experimental import pallas as pl
from jax.experimental.pallas import tpu as pltpu
from jax.sharding import PartitionSpec as P

D = 768
H = 12
DH = 64
E = 64
NB = 32
CAP = 8
G = 4
HG = H // G
GW = HG * DH
CORES = 2

EPS = 1e-06
EDGES = (16, 23, 32, 45, 64, 91, 128, 181, 256, 362, 512, 724, 1024, 1448, 2048, 2896)
STARTS = tuple(range(16)) + EDGES
GELU_C = 0.7978845608028654
NEG = -1e30
MESH = pl.DeviceIdType.MESH
F32 = jnp.float32
BF = jnp.bfloat16
VM = pl.BlockSpec(memory_space=pltpu.VMEM)
HB = pl.BlockSpec(memory_space=pl.ANY)
SM = pl.BlockSpec(memory_space=pltpu.SMEM)
LIMIT = 56 * 1024 * 1024


def dot(a, b, ca=1, cb=0):
    return lax.dot_general(a, b, (((ca,), (cb,)), ((), ())), preferred_element_type=F32)


def call(body, outs, ins, out_specs=None, in_specs=None, scratch=(), cid=None, name=None, cost=None, limit=LIMIT, **kw):
    params = dict(vmem_limit_bytes=limit)
    if cid is not None:
        params.update(collective_id=cid, has_side_effects=True)
    return pl.pallas_call(
        body,
        out_shape=outs,
        in_specs=in_specs or [VM] * len(ins),
        out_specs=out_specs or [VM] * len(outs),
        scratch_shapes=list(scratch),
        compiler_params=pltpu.CompilerParams(**params),
        name=name,
        cost_estimate=cost,
        **kw,
    )(*ins)


def sds(shape, kind=F32):
    return jax.ShapeDtypeStruct(shape, kind)


class Place:
    def __init__(self, n_ctx, nf):
        self.n_ctx, self.nf = n_ctx, nf
        self.R, self.X = n_ctx // G, nf // CORES
        self.c, self.f = lax.axis_index("ctx"), lax.axis_index("fsdp")
        self.g, self.r = lax.div(self.c, self.R), lax.rem(self.c, self.R)
        self.x, self.k = lax.div(self.f, CORES), lax.rem(self.f, CORES)

    def up(self, v, d, n):
        return lax.rem(v + d, n)

    def ctx(self, dg, dr):
        return self.up(self.g, dg % G, G) * self.R + self.up(self.r, dr % self.R, self.R)

    def fs(self, dx, dk):
        return self.up(self.x, dx % self.X, self.X) * CORES + self.up(self.k, dk % CORES, CORES)

    def dev(self, dg, dr, dx, dk):
        return (self.ctx(dg, dr), self.fs(dx, dk))


def greet(targets):
    bar = pltpu.get_barrier_semaphore()
    for t in targets:
        pl.semaphore_signal(bar, inc=1, device_id=t, device_id_type=MESH)
    pl.semaphore_wait(bar, len(targets))


def rcopy(src, dst, ss, rs, dev):
    return pltpu.make_async_remote_copy(
        src_ref=src, dst_ref=dst, send_sem=ss, recv_sem=rs, device_id=dev, device_id_type=MESH
    )


def gather_body(n_ctx, nf, tok, wq, xall, wall, t1s, t1r, t2s, t2r, w1s, w1r, w2s, w2r, w3s, w3r, loc):
    p = Place(n_ctx, nf)
    R, X = p.R, p.X
    quad = [(er, ex) for er in range(R) for ex in range(X)]
    greet(
        [p.dev(d, 0, 0, 0) for d in range(1, G)]
        + [p.dev(0, er, ex, 0) for er, ex in quad[1:]]
        + [p.dev(0, 0, 0, 1)]
    )
    mine = p.c * nf + p.f
    own_t = pltpu.make_async_copy(tok, xall.at[p.c], loc.at[0])
    own_w = pltpu.make_async_copy(wq.at[p.g], wall.at[mine], loc.at[1])
    own_t.start()
    own_w.start()
    waits = []

    def send(src, dst, ss, rs, dev):
        cp = rcopy(src, dst, ss, rs, dev)
        cp.start()
        waits.append(cp)

    far = (2, 1, 3)
    for d in far:
        send(wq.at[p.up(p.g, d, G)], wall.at[mine], w1s.at[d], w1r.at[d], p.dev(d, 0, 0, 0))
    for d in far:
        send(tok, xall.at[p.c], t1s.at[d], t1r.at[d], p.dev(d, 0, 0, 0))
    for e in range(1, R):
        send(tok, xall.at[p.c], t2s.at[0, e], t2r.at[0, e], p.dev(0, e, 0, 0))
    for d in (0, 1, 3, 2):
        block = p.ctx(-d, 0) * nf + p.f
        src = wq.at[p.g] if d == 0 else wall.at[block]
        if d:
            rcopy(src, src, w1s.at[d], w1r.at[d], p.dev(-d, 0, 0, 0)).wait_recv()
        for i, (er, ex) in enumerate(quad):
            if i:
                send(src, wall.at[block], w2s.at[d, i], w2r.at[d, i], p.dev(0, er, ex, 0))
        send(src, wall.at[block], w3s.at[d, 0], w3r.at[d, 0], p.dev(0, 0, 0, 1))
    for d in (1, 3, 2):
        block = p.ctx(-d, 0)
        src = xall.at[block]
        rcopy(src, src, t1s.at[d], t1r.at[d], p.dev(-d, 0, 0, 0)).wait_recv()
        for e in range(1, R):
            send(src, src, t2s.at[d, e], t2r.at[d, e], p.dev(0, e, 0, 0))
    for d in (0, 1, 3, 2):
        for i, (er, ex) in enumerate(quad):
            if i:
                block = p.ctx(-d, -er) * nf + p.fs(-ex, 0)
                src = wall.at[block]
                rcopy(src, src, w2s.at[d, i], w2r.at[d, i], p.dev(0, -er, -ex, 0)).wait_recv()
                send(src, src, w3s.at[d, i], w3r.at[d, i], p.dev(0, 0, 0, 1))
    for d in range(G):
        for i, (er, ex) in enumerate(quad):
            src = wall.at[p.ctx(-d, -er) * nf + p.fs(-ex, 1)]
            rcopy(src, src, w3s.at[d, i], w3r.at[d, i], p.dev(0, 0, 0, 1)).wait_recv()
        for e in range(1, R):
            src = xall.at[p.ctx(-d, -e)]
            rcopy(src, src, t2s.at[d, e], t2r.at[d, e], p.dev(0, -e, 0, 0)).wait_recv()
    for cp in waits:
        cp.wait_send()
    own_t.wait()
    own_w.wait()


def gather(n_ctx, nf, tok, wq):
    R, X = n_ctx // G, nf // CORES
    sem = lambda *s: pltpu.SemaphoreType.DMA(s)
    return call(
        functools.partial(gather_body, n_ctx, nf),
        [sds((n_ctx,) + tok.shape, BF), sds((n_ctx * nf,) + wq.shape[1:], BF)],
        [tok, wq],
        out_specs=[HB, HB],
        scratch=[sem(G)] * 2 + [sem(G, R)] * 2 + [sem(G)] * 2 + [sem(G, R * X)] * 4 + [sem(2)],
        cid=1,
        name="gather",
    )


def swap_body(n_ctx, nf, src, dst, ss, rs, loc):
    p = Place(n_ctx, nf)
    greet([p.dev(d, 0, 0, 0) for d in range(1, G)])
    own = pltpu.make_async_copy(src.at[p.g], dst.at[p.g], loc)
    own.start()
    cps = []
    for d in (2, 1, 3):
        cp = rcopy(src.at[p.up(p.g, d, G)], dst.at[p.g], ss.at[d], rs.at[d], p.dev(d, 0, 0, 0))
        cp.start()
        cps.append(cp)
    for d in (1, 3, 2):
        at = dst.at[p.up(p.g, G - d, G)]
        rcopy(at, at, ss.at[d], rs.at[d], p.dev(-d, 0, 0, 0)).wait_recv()
    for cp in cps:
        cp.wait_send()
    own.wait()


def swap(n_ctx, nf, src, cid, name):
    sem = pltpu.SemaphoreType.DMA
    return call(
        functools.partial(swap_body, n_ctx, nf),
        [sds(src.shape, src.dtype)],
        [src],
        scratch=[sem((G,)), sem((G,)), sem],
        cid=cid,
        name=name,
    )[0]


def dispatch_body(n_ctx, nf, packed, recv, ss, rs, xs, xr, ks, kr, loc):
    p = Place(n_ctx, nf)
    X = p.X
    greet(
        [(p.up(p.c, d, n_ctx), p.f) for d in range(1, n_ctx)]
        + [p.dev(0, 0, dx, 0) for dx in range(1, X)]
        + [p.dev(0, 0, 0, 1)]
    )
    own = pltpu.make_async_copy(packed.at[p.c], recv.at[:, p.f, p.c], loc)
    own.start()
    waits = []

    def send(src, dst, s, r, dev):
        cp = rcopy(src, dst, s, r, dev)
        cp.start()
        waits.append(cp)

    order = sorted(range(1, n_ctx), key=lambda d: (abs(2 * d - n_ctx), d))
    for d in order:
        send(packed.at[p.up(p.c, d, n_ctx)], recv.at[:, p.f, p.c], ss.at[d], rs.at[d], (p.up(p.c, d, n_ctx), p.f))

    def spread(d):
        cc = p.up(p.c, n_ctx - d, n_ctx)
        at = recv.at[:, p.f, cc]
        if d:
            rcopy(at, at, ss.at[d], rs.at[d], (cc, p.f)).wait_recv()
        src = packed.at[p.c] if d == 0 else at
        for dx in range(1, X):
            send(src, at, xs.at[d, dx], xr.at[d, dx], p.dev(0, 0, dx, 0))
        send(src, at, ks.at[d, 0], kr.at[d, 0], p.dev(0, 0, 0, 1))

    def relay(d):
        cc = p.up(p.c, n_ctx - d, n_ctx)
        for dx in range(1, X):
            at = recv.at[:, p.fs(-dx, 0), cc]
            rcopy(at, at, xs.at[d, dx], xr.at[d, dx], p.dev(0, 0, -dx, 0)).wait_recv()
            send(at, at, ks.at[d, dx], kr.at[d, dx], p.dev(0, 0, 0, 1))

    arrive = [0] + order[::-1]
    for i, d in enumerate(arrive):
        spread(d)
        if i:
            relay(arrive[i - 1])
    relay(arrive[-1])
    for d in range(n_ctx):
        cc = p.up(p.c, n_ctx - d, n_ctx)
        for dx in range(X):
            at = recv.at[:, p.fs(-dx, 1), cc]
            rcopy(at, at, ks.at[d, dx], kr.at[d, dx], p.dev(0, 0, 0, 1)).wait_recv()
    for cp in waits:
        cp.wait_send()
    own.wait()


def dispatch(n_ctx, nf, packed):
    per_dev, width = packed.shape[1], packed.shape[3]
    X = nf // CORES
    sem = lambda *s: pltpu.SemaphoreType.DMA(s)
    return call(
        functools.partial(dispatch_body, n_ctx, nf),
        [sds((per_dev, nf, n_ctx, CAP, width), BF)],
        [packed],
        in_specs=[HB],
        out_specs=[HB],
        scratch=[sem(n_ctx)] * 2 + [sem(n_ctx, X)] * 4 + [pltpu.SemaphoreType.DMA],
        cid=3,
        name="dispatch",
    )[0]


def combine_body(n_ctx, nf, part, out, cin, xsum, xin, fin, ss, rs, xs, xr, ks, kr):
    p = Place(n_ctx, nf)
    X = p.X
    greet(
        [(p.up(p.c, d, n_ctx), p.f) for d in range(1, n_ctx)]
        + [p.dev(0, 0, dx, 0) for dx in range(1, X)]
        + [p.dev(0, 0, 0, 1)]
    )
    waits = []

    def send(src, dst, s, r, dev):
        cp = rcopy(src, dst, s, r, dev)
        cp.start()
        waits.append(cp)

    order = sorted(range(1, n_ctx), key=lambda d: (abs(2 * d - n_ctx), d)) + [0]
    for d in order:
        cc = p.up(p.c, d, n_ctx)
        for dx in [*range(1, X), 0]:
            send(part.at[:, p.fs(dx, 1), cc], cin.at[dx, d], ks.at[d, dx], kr.at[d, dx], p.dev(0, 0, 0, 1))
    for d in order:
        cc = p.up(p.c, d, n_ctx)
        for dx in range(1, X):
            rcopy(cin.at[dx, d], cin.at[dx, d], ks.at[d, dx], kr.at[d, dx], p.dev(0, 0, 0, 1)).wait_recv()
            xsum[dx, d] = (part[:, p.fs(dx, 0), cc].astype(F32) + cin[dx, d].astype(F32)).astype(BF)
            send(xsum.at[dx, d], xin.at[dx, d], xs.at[d, dx], xr.at[d, dx], p.dev(0, 0, dx, 0))
    for d in order:
        cc = p.up(p.c, d, n_ctx)
        rcopy(cin.at[0, d], cin.at[0, d], ks.at[d, 0], kr.at[d, 0], p.dev(0, 0, 0, 1)).wait_recv()
        total = part[:, p.fs(0, 0), cc].astype(F32) + cin[0, d].astype(F32)
        for dx in range(1, X):
            rcopy(xin.at[dx, d], xin.at[dx, d], xs.at[d, dx], xr.at[d, dx], p.dev(0, 0, -dx, 0)).wait_recv()
            total = total + xin[dx, d].astype(F32)
        if d:
            fin[d] = total.astype(BF)
            send(fin.at[d], out.at[p.c], ss.at[d], rs.at[d], (cc, p.f))
        else:
            out[p.c] = total.astype(BF)
    for d in order[:-1]:
        at = out.at[p.up(p.c, n_ctx - d, n_ctx)]
        rcopy(at, at, ss.at[d], rs.at[d], (p.up(p.c, n_ctx - d, n_ctx), p.f)).wait_recv()
    for cp in waits:
        cp.wait_send()


def combine(n_ctx, nf, part):
    per_dev, width = part.shape[0], part.shape[-1]
    X = nf // CORES
    sem = lambda *s: pltpu.SemaphoreType.DMA(s)
    blk = (per_dev, CAP, width)
    return call(
        functools.partial(combine_body, n_ctx, nf),
        [sds((n_ctx,) + blk, BF)],
        [part],
        scratch=[pltpu.VMEM((X, n_ctx) + blk, BF)] * 3
        + [pltpu.VMEM((n_ctx,) + blk, BF)]
        + [sem(n_ctx)] * 2
        + [sem(n_ctx, X)] * 4,
        cid=4,
        name="combine",
    )[0]


def reduce_body(
    n_ctx, nf, dx_ref, dw_ref, tok_ref, gain_ref, dh1_ref, dtok_ref, dqkv_ref,
    rin, gsum, gin, cin, s1, qin, s2, win, a1, b1, a2, b2, c1, e1, c2, e2, c3, e3,
):
    p = Place(n_ctx, nf)
    R, X = p.R, p.X
    quad = [(er, ex) for er in range(R) for ex in range(X)]
    greet(
        [p.dev(d, 0, 0, 0) for d in range(1, G)]
        + [p.dev(0, er, ex, 0) for er, ex in quad[1:]]
        + [p.dev(0, 0, 0, 1)]
    )
    waits = []

    def send(src, dst, s, r, dev):
        cp = rcopy(src, dst, s, r, dev)
        cp.start()
        waits.append(cp)

    def got(at, s, r, dev):
        rcopy(at, at, s, r, dev).wait_recv()

    send(dw_ref.at[:, :, :, 1 - p.k], cin, c1, e1, p.dev(0, 0, 0, 1))
    far = (2, 1, 3, 0)
    for dg in far:
        for er in range(1, R):
            send(dx_ref.at[p.ctx(dg, er)], rin.at[er, dg], a1.at[dg, er], b1.at[dg, er], p.dev(0, er, 0, 0))
    got(cin, c1, e1, p.dev(0, 0, 0, 1))
    s1[...] = (dw_ref[:, :, :, p.k].astype(F32) + cin[...].astype(F32)).astype(BF)
    for i, (er, ex) in enumerate(quad):
        if i:
            send(s1.at[:, p.up(p.r, er, R), p.up(p.x, ex, X)], qin.at[i], c2.at[i], e2.at[i], p.dev(0, er, ex, 0))
    for dg in far:
        total = dx_ref[p.ctx(dg, 0)].astype(F32)
        for er in range(1, R):
            got(rin.at[er, dg], a1.at[dg, er], b1.at[dg, er], p.dev(0, -er, 0, 0))
            total = total + rin[er, dg].astype(F32)
        gsum[dg] = total.astype(BF)
        if dg:
            send(gsum.at[dg], gin.at[dg], a2.at[dg], b2.at[dg], p.dev(dg, 0, 0, 0))
    total = s1[:, p.r, p.x].astype(F32)
    for i, (er, ex) in enumerate(quad):
        if i:
            got(qin.at[i], c2.at[i], e2.at[i], p.dev(0, -er, -ex, 0))
            total = total + qin[i].astype(F32)
    s2[...] = total.astype(BF)
    win[p.g] = s2[p.g]
    for dg in range(1, G):
        send(s2.at[p.up(p.g, dg, G)], win.at[p.g], c3.at[dg], e3.at[dg], p.dev(dg, 0, 0, 0))
    grad = gsum[0].astype(F32)
    for dg in range(1, G):
        got(gin.at[dg], a2.at[dg], b2.at[dg], p.dev(-dg, 0, 0, 0))
        grad = grad + gin[dg].astype(F32)
    rows = tok_ref[...].astype(F32)
    inv = lax.rsqrt(jnp.mean(rows * rows, axis=-1, keepdims=True) + EPS)
    hat = rows * inv
    grad = grad * gain_ref[...]
    dtok_ref[...] = dh1_ref[...] + inv * (grad - hat * jnp.mean(grad * hat, axis=-1, keepdims=True))
    for dg in range(1, G):
        at = win.at[p.up(p.g, G - dg, G)]
        got(at, c3.at[dg], e3.at[dg], p.dev(-dg, 0, 0, 0))
    dqkv_ref[...] = jnp.concatenate([win[i].astype(F32) for i in range(G)], axis=1)
    for cp in waits:
        cp.wait_send()


def reduce_all(n_ctx, nf, dx, dw, tok, gain, dh1):
    R, X = n_ctx // G, nf // CORES
    qr = dw.shape[-2]
    tb = dx.shape[1:]
    wb = (qr, GW)
    sem = lambda *s: pltpu.SemaphoreType.DMA(s)
    one = pltpu.SemaphoreType.DMA
    vm = lambda *s: pltpu.VMEM(s, BF)
    return call(
        functools.partial(reduce_body, n_ctx, nf),
        [sds(tb), sds((qr, D))],
        [dx, dw, tok, gain, dh1],
        scratch=[
            vm(R, G, *tb), vm(G, *tb), vm(G, *tb), vm(G, R, X, *wb), vm(G, R, X, *wb), vm(R * X, G, *wb),
            vm(G, *wb), vm(G, *wb), sem(G, R), sem(G, R), sem(G), sem(G), one, one,
            sem(R * X), sem(R * X), sem(G), sem(G),
        ],
        cid=6,
        name="reduce",
    )


def bias_tiles(tab_ref, tiles, g, R, nd):
    tok = tiles.shape[2]
    lane = lax.broadcasted_iota(jnp.int32, (8, 2 * tok), 1)

    def one(i, _):
        off = (i - (R - 1)) * tok + tok - lane
        for hh in range(HG):
            base = (g * HG + hh) * NB
            val = jnp.full(off.shape, NEG, F32)
            for b, e in enumerate(STARTS):
                val = jnp.where(off >= e, tab_ref[base + b], val)
            wide = jnp.concatenate([val] * (tok // 8), axis=0)
            wide = pltpu.roll(wide, tok, 1, stride=1, stride_axis=0)
            tiles[hh, i] = wide[:, :tok]
        return 0

    lax.fori_loop(0, nd, one, 0)


def normed(x_ref, b):
    rows = x_ref[b].astype(F32)
    inv = lax.rsqrt(jnp.mean(rows * rows, axis=-1, keepdims=True) + EPS)
    return rows * inv


def scores(q, keys, tiles, hh, gq, r, R, n):
    s = dot(q, keys, 1, 1) * (1.0 / math.sqrt(DH))
    bias = jnp.concatenate([tiles[hh, gq * R + r - kb + R - 1] for kb in range(n)], axis=1)
    return s + bias


def attend_body(n_ctx, nf, x_ref, w_ref, gain_ref, tab_ref, att_ref, lse_ref, q_ref, k_ref, v_ref, tiles):
    p = Place(n_ctx, nf)
    R, tok = p.R, x_ref.shape[1]
    gain = gain_ref[...]
    bias_tiles(tab_ref, tiles, p.g, R, n_ctx + R - 1)

    def block(b, _):
        xn = (normed(x_ref, b) * gain).astype(BF)
        at = pl.ds(pl.multiple_of(b * tok, tok), tok)
        for m, ref in ((1, k_ref), (2, v_ref)):
            y = dot(xn, w_ref[pl.ds(m * D, D)]).astype(BF)
            for hh in range(HG):
                ref[hh, at] = y[:, hh * DH : (hh + 1) * DH]
        return 0

    lax.fori_loop(0, n_ctx, block, 0)
    for gq in range(G):
        xn = (normed(x_ref, gq * R + p.r) * gain).astype(BF)
        y = dot(xn, w_ref[pl.ds(0, D)]).astype(BF)
        for hh in range(HG):
            q_ref[hh, pl.ds(gq * tok, tok)] = y[:, hh * DH : (hh + 1) * DH]
    for gq in range(G):
        n = (gq + 1) * R
        outs = []
        for hh in range(HG):
            s = scores(q_ref[hh, pl.ds(gq * tok, tok)], k_ref[hh, pl.ds(0, n * tok)], tiles, hh, gq, p.r, R, n)
            top = jnp.max(s, axis=-1, keepdims=True)
            w = jnp.exp(s - top)
            total = jnp.sum(w, axis=-1, keepdims=True)
            acc = dot(w.astype(BF), v_ref[hh, pl.ds(0, n * tok)])
            outs.append((acc / total).astype(BF))
            lse_ref[gq, :, hh : hh + 1] = top + jnp.log(total)
        att_ref[gq] = jnp.concatenate(outs, axis=1)


def attend_back_body(
    n_ctx, nf, x_ref, w_ref, gain_ref, tab_ref, lse_ref, q_ref, k_ref, v_ref, att_ref, do_ref,
    dx_ref, dw_ref, dgain_ref, dtab_ref, tiles, dtiles, dk_acc, dv_acc, xn_s, dq_s, dkv_s, dw_acc,
):
    p = Place(n_ctx, nf)
    R, tok = p.R, x_ref.shape[1]
    nd = n_ctx + R - 1
    scale = 1.0 / math.sqrt(DH)
    bias_tiles(tab_ref, tiles, p.g, R, nd)
    dtiles[...] = jnp.zeros_like(dtiles)
    dk_acc[...] = jnp.zeros_like(dk_acc)
    dv_acc[...] = jnp.zeros_like(dv_acc)
    for gq in range(G):
        n = (gq + 1) * R
        rows = pl.ds(gq * tok, tok)
        keys = pl.ds(0, n * tok)
        do_all = do_ref[gq]
        prod = do_all.astype(F32) * att_ref[gq].astype(F32)
        dqs = []
        for hh in range(HG):
            q, kk, vv = q_ref[hh, rows], k_ref[hh, keys], v_ref[hh, keys]
            do = do_all[:, hh * DH : (hh + 1) * DH]
            delta = jnp.sum(prod[:, hh * DH : (hh + 1) * DH], axis=-1, keepdims=True)
            s = scores(q, kk, tiles, hh, gq, p.r, R, n)
            w = jnp.exp(s - lse_ref[gq, :, hh : hh + 1])
            ds = w * (dot(do, vv, 1, 1) - delta)
            for kb in range(n):
                at = gq * R + p.r - kb + R - 1
                dtiles[hh, at] = dtiles[hh, at] + ds[:, kb * tok : (kb + 1) * tok]
            dsb = ds.astype(BF)
            dqs.append((dot(dsb, kk) * scale).astype(BF))
            dk_acc[hh, keys] = dk_acc[hh, keys] + dot(dsb, q, 0, 0)
            dv_acc[hh, keys] = dv_acc[hh, keys] + dot(w.astype(BF), do, 0, 0)
        dq_s[gq] = jnp.concatenate(dqs, axis=1)
    for hh in range(HG):
        sums = [None] * NB
        off0 = lax.broadcasted_iota(jnp.int32, (tok, tok), 0) - lax.broadcasted_iota(jnp.int32, (tok, tok), 1)
        for d in range(n_ctx):
            t = dtiles[hh, d + R - 1]
            off = off0 + d * tok
            for b in range(NB):
                low = STARTS[b]
                high = STARTS[b + 1] if b + 1 < NB else 1 << 30
                if high <= d * tok - tok + 1 or low > d * tok + tok - 1:
                    continue
                part = jnp.where((off >= low) & (off < high), t, 0.0)
                part = jnp.sum(part.reshape(tok // 8, 8, tok), axis=0)
                sums[b] = part if sums[b] is None else sums[b] + part
        for b in range(NB):
            dtab_ref[hh, b] = jnp.zeros((8, tok), F32) if sums[b] is None else sums[b]
    gain = gain_ref[...]
    xn_q = jnp.concatenate([(normed(x_ref, gq * R + p.r) * gain).astype(BF) for gq in range(G)], axis=0)
    dw_ref[pl.ds(0, D)] = dot(xn_q, dq_s[...].reshape(G * tok, GW), 0, 0).astype(BF)
    width = xn_s.shape[0]
    dgain = jnp.zeros((8, D), F32)
    for first in range(0, n_ctx, width):

        def block(i, dg):
            b = first + i
            hat = normed(x_ref, b)
            at = pl.ds(pl.multiple_of(b * tok, tok), tok)
            xn_s[i] = (hat * gain).astype(BF)
            dk = jnp.concatenate([(dk_acc[hh, at] * scale).astype(BF) for hh in range(HG)], axis=1)
            dv = jnp.concatenate([dv_acc[hh, at].astype(BF) for hh in range(HG)], axis=1)
            dkv_s[0, i] = dk
            dkv_s[1, i] = dv
            mine = lax.rem(b, R) == p.r
            dq = jnp.where(mine, dq_s[lax.div(b, R)], jnp.zeros((tok, GW), BF))
            dxn = (
                dot(dq, w_ref[pl.ds(0, D)], 1, 1)
                + dot(dk, w_ref[pl.ds(D, D)], 1, 1)
                + dot(dv, w_ref[pl.ds(2 * D, D)], 1, 1)
            )
            dx_ref[b] = dxn.astype(BF)
            return dg + jnp.sum((dxn * hat).reshape(tok // 8, 8, D), axis=0)

        dgain = lax.fori_loop(0, width, block, dgain)
        xn = xn_s[...].reshape(width * tok, D)
        for m in range(2):
            piece = dot(xn, dkv_s[m].reshape(width * tok, GW), 0, 0)
            if first:
                piece = piece + dw_acc[m]
            if first + width < n_ctx:
                dw_acc[m] = piece
            else:
                dw_ref[pl.ds((m + 1) * D, D)] = piece.astype(BF)
    dgain_ref[...] = dgain


def middle_body(
    att_ref, tok_ref, wo_ref, gain_ref, router_ref, routes_ref, cot_ref,
    h1_ref, xn2_ref, gate_ref, disp_ref, packed_ref,
):
    tok = tok_ref.shape[0]
    att = jnp.concatenate([att_ref[i] for i in range(G)], axis=1)
    h1 = tok_ref[...].astype(F32) + dot(att, wo_ref[...])
    h1_ref[...] = h1
    inv = lax.rsqrt(jnp.mean(h1 * h1, axis=-1, keepdims=True) + EPS)
    xn2 = (h1 * inv * gain_ref[...]).astype(BF)
    xn2_ref[...] = xn2
    logits = dot(xn2, router_ref[...])
    experts = lax.broadcasted_iota(jnp.int32, (tok, E), 1)
    route = [routes_ref[:, k : k + 1] for k in range(2)]
    member = [(route[k] == experts).astype(F32) for k in range(2)]
    chosen = [jnp.sum(logits * member[k], axis=-1, keepdims=True) for k in range(2)]
    top = jnp.maximum(chosen[0], chosen[1])
    ex = [jnp.exp(chosen[k] - top) for k in range(2)]
    gate = [ex[k] / (ex[0] + ex[1]) for k in range(2)]
    gate_ref[...] = jnp.concatenate(gate, axis=1)
    before = lax.broadcasted_iota(jnp.int32, (tok, tok), 0) > lax.broadcasted_iota(jnp.int32, (tok, tok), 1)
    counts = dot(before.astype(F32).astype(BF), (member[0] + member[1]).astype(BF))
    slots = lax.broadcasted_iota(jnp.int32, (tok, E * CAP), 1)
    disp = []
    for k in range(2):
        slot = jnp.sum(counts * member[k], axis=-1, keepdims=True).astype(jnp.int32)
        disp.append((route[k] * CAP + slot == slots).astype(F32).astype(BF))
        disp_ref[k] = disp[k]
    cot = cot_ref[...].astype(F32)
    packed_ref[:, :D] = dot(disp[0] + disp[1], xn2, 0, 0).astype(BF)
    rows = dot(disp[0], (gate[0] * cot).astype(BF), 0, 0) + dot(disp[1], (gate[1] * cot).astype(BF), 0, 0)
    packed_ref[:, D:] = rows.astype(BF)


def expert_body(x_ref, win_ref, wout_ref, part_ref, dwin_ref, dwout_ref):
    x, dy = x_ref[0, :, :D], x_ref[0, :, D:]
    win, wout = win_ref[0], wout_ref[0]
    pre = dot(x, win)
    inner = GELU_C * (pre + 0.044715 * pre * pre * pre)
    th = jnp.tanh(inner)
    hid = (0.5 * pre * (1.0 + th)).astype(BF)
    slope = 0.5 * (1.0 + th) + 0.5 * pre * (1.0 - th * th) * GELU_C * (1.0 + 3.0 * 0.044715 * pre * pre)
    dpre = (dot(dy, wout, 1, 1) * slope).astype(BF)
    part_ref[0, :, :D] = dot(hid, wout).astype(BF)
    part_ref[0, :, D:] = dot(dpre, win, 1, 1).astype(BF)
    dwin_ref[0] = dot(x, dpre, 0, 0)
    dwout_ref[0] = dot(hid, dy, 0, 0)


def experts(x, w_in, w_out):
    n, rows = x.shape[:2]
    ff = w_in.shape[2]
    spec = lambda *s: pl.BlockSpec((1,) + s, lambda i: (i, 0, 0))
    return pl.pallas_call(
        expert_body,
        grid=(n,),
        in_specs=[spec(rows, 2 * D), spec(D, ff), spec(ff, D)],
        out_specs=[spec(rows, 2 * D), spec(D, ff), spec(ff, D)],
        out_shape=[sds(x.shape, BF), sds((n, D, ff)), sds((n, ff, D))],
        compiler_params=pltpu.CompilerParams(vmem_limit_bytes=LIMIT),
        name="experts",
    )(x, w_in, w_out)


def after_body(
    ret_ref, disp_ref, h1_ref, xn2_ref, gate_ref, cot_ref, routes_ref, router_ref, wo_ref, att_ref, gain_ref,
    mixed_ref, dh1_ref, dat_ref, dout_ref, drouter_ref, dgain_ref,
):
    tok = h1_ref.shape[0]
    both = [dot(disp_ref[k], ret_ref[...]) for k in range(2)]
    gate = [gate_ref[:, k : k + 1] for k in range(2)]
    h1 = h1_ref[...]
    dy = cot_ref[...].astype(F32)
    picked = [both[k][:, :D] for k in range(2)]
    mixed_ref[...] = (h1 + (gate[0] * picked[0] + gate[1] * picked[1])).astype(BF)
    dgate = [jnp.sum(dy * picked[k], axis=-1, keepdims=True) for k in range(2)]
    mean = gate[0] * dgate[0] + gate[1] * dgate[1]
    lanes = lax.broadcasted_iota(jnp.int32, (tok, E), 1)
    dlog = jnp.zeros((tok, E), F32)
    for k in range(2):
        dlog = dlog + jnp.where(routes_ref[:, k : k + 1] == lanes, gate[k] * (dgate[k] - mean), 0.0)
    dlog = dlog.astype(BF)
    xn2 = xn2_ref[...]
    dxn = both[0][:, D:] + both[1][:, D:] + dot(dlog, router_ref[...], 1, 1)
    drouter_ref[...] = dot(xn2, dlog, 0, 0)
    inv = lax.rsqrt(jnp.mean(h1 * h1, axis=-1, keepdims=True) + EPS)
    hat = h1 * inv
    dgain_ref[...] = jnp.sum((dxn * hat).reshape(tok // 8, 8, D), axis=0)
    cen = dxn * gain_ref[...]
    dh1 = dy + inv * (cen - hat * jnp.mean(cen * hat, axis=-1, keepdims=True))
    dh1_ref[...] = dh1
    dh1b = dh1.astype(BF)
    att = jnp.concatenate([att_ref[i] for i in range(G)], axis=1)
    dout_ref[...] = dot(att, dh1b, 0, 0)
    dat = dot(dh1b, wo_ref[...], 1, 1).astype(BF)
    for i in range(G):
        dat_ref[i] = dat[:, i * GW : (i + 1) * GW]


def shards(tokens, routes, cotangent, gains, rel_bias, attn_qkv, attn_out, router, w_in, w_out):
    tok = tokens.shape[1]
    n_ctx, nf = lax.axis_size("ctx"), lax.axis_size("fsdp")
    n_dev = n_ctx * nf
    R, X = n_ctx // G, nf // CORES
    seq = tok * n_ctx
    per_dev = w_in.shape[0]
    qr, orows = attn_qkv.shape[0], attn_out.shape[0]
    axes = ("ctx", "fsdp")
    x2, cot, route2 = tokens.reshape(tok, D), cotangent.reshape(tok, D), routes.reshape(tok, 2)

    sizes = (router.size, gains.size, rel_bias.size)
    used = sum(sizes)
    tail_rows = -(-used // D)
    tail = jnp.concatenate([router.reshape(-1), gains.reshape(-1), rel_bias.reshape(-1)])
    tail = jnp.pad(tail, (0, tail_rows * D - used)).reshape(tail_rows, D)
    pack = jnp.concatenate([attn_out, tail], axis=0)
    everything = lax.all_gather(pack, axes, axis=0, tiled=False)

    wq = attn_qkv.reshape(qr, G, GW).transpose(1, 0, 2)
    xall, wall = gather(n_ctx, nf, x2, wq)
    wall = wall.reshape(n_dev * qr, GW)

    wo = everything[:, :orows].reshape(D, D)
    tails = everything[:, orows:].reshape(n_dev, tail_rows * D)
    cut = sizes[0] + sizes[1]
    router_full = tails[:, : sizes[0]].reshape(D, E)
    gains_full = tails[:, sizes[0] : cut].reshape(n_dev, 2, -1).transpose(1, 0, 2).reshape(2, D).astype(F32)
    table = tails[:, cut:used].reshape(H * NB).astype(F32)
    gain1, gain2 = gains_full[:1], gains_full[1:]

    part = functools.partial
    width = math.gcd(n_ctx, 8)
    tiles = pltpu.VMEM((HG, n_ctx + R - 1, tok, tok), F32)
    att, lse, q, k, v = call(
        part(attend_body, n_ctx, nf),
        [sds((G, tok, GW), BF), sds((G, tok, 128)), sds((HG, G * tok, DH), BF)] + [sds((HG, seq, DH), BF)] * 2,
        [xall, wall, gain1, table],
        in_specs=[VM, VM, VM, SM],
        scratch=[tiles],
        name="attend",
    )
    att_in = swap(n_ctx, nf, att, 2, "swap_att")
    h1, xn2, gate, disp, packed = call(
        middle_body,
        [sds((tok, D)), sds((tok, D), BF), sds((tok, 2)), sds((2, tok, E * CAP), BF), sds((E * CAP, 2 * D), BF)],
        [att_in, x2, wo, gain2, router_full, route2, cot],
        name="middle",
    )
    recv = dispatch(n_ctx, nf, packed.reshape(n_ctx, per_dev, CAP, 2 * D))
    rows = nf * n_ctx * CAP
    part_rows, d_w_in, d_w_out = experts(recv.reshape(per_dev, rows, 2 * D), w_in, w_out)
    ret = combine(n_ctx, nf, part_rows.reshape(per_dev, nf, n_ctx, CAP, 2 * D))
    mixed, dh1, dat, d_out, d_router, dgain2 = call(
        after_body,
        [sds((tok, D), BF), sds((tok, D)), sds((G, tok, GW), BF), sds((D, D)), sds((D, E)), sds((8, D))],
        [ret.reshape(E * CAP, 2 * D), disp, h1, xn2, gate, cot, route2, router_full, wo, att_in, gain2],
        name="after",
    )
    do = swap(n_ctx, nf, dat, 5, "swap_dat")
    dx, dw, dgain1, dtab = call(
        part(attend_back_body, n_ctx, nf),
        [sds((n_ctx, tok, D), BF), sds((3 * D, GW), BF), sds((8, D)), sds((HG, NB, 8, tok))],
        [xall, wall, gain1, table, lse, q, k, v, att, do],
        in_specs=[VM, VM, VM, SM] + [VM] * 6,
        scratch=[
            tiles, tiles, pltpu.VMEM((HG, seq, DH), F32), pltpu.VMEM((HG, seq, DH), F32),
            pltpu.VMEM((width, tok, D), BF), pltpu.VMEM((G, tok, GW), BF), pltpu.VMEM((2, width, tok, GW), BF),
            pltpu.VMEM((2, D, GW) if width < n_ctx else (2, 8, GW), F32),
        ],
        name="attend_back",
        limit=LIMIT if width == n_ctx else 61 * 1024 * 1024,
    )
    dtab = jnp.sum(dtab, axis=(2, 3)).reshape(1, HG * NB)
    own_group = jnp.arange(G)[:, None] == lax.axis_index("ctx") // R
    dtab = jnp.where(own_group, dtab, 0.0).reshape(n_dev, sizes[2])
    dgains = jnp.stack([jnp.sum(dgain1, axis=0), jnp.sum(dgain2, axis=0)])
    d_tail = jnp.concatenate(
        [
            d_router.reshape(n_dev, sizes[0]),
            dgains.reshape(2, n_dev, -1).transpose(1, 0, 2).reshape(n_dev, sizes[1]),
            dtab,
        ],
        axis=1,
    )
    d_tail = jnp.pad(d_tail, ((0, 0), (0, tail_rows * D - used)))
    d_pack = jnp.concatenate([d_out.reshape(n_dev, orows, D), d_tail.reshape(n_dev, tail_rows, D)], axis=1)
    d_mine = lax.psum_scatter(d_pack, axes, scatter_dimension=0, tiled=False)
    d_tokens, d_qkv = reduce_all(n_ctx, nf, dx, dw.reshape(G, R, X, CORES, qr, GW), x2, gain1, dh1)
    tail_mine = d_mine[orows:].reshape(-1)
    return (
        mixed.reshape(1, tok, D),
        d_tokens.reshape(1, tok, D),
        tail_mine[sizes[0] : cut].reshape(gains.shape),
        tail_mine[cut:used],
        d_qkv,
        d_mine[:orows],
        tail_mine[: sizes[0]].reshape(router.shape),
        d_w_in,
        d_w_out,
    )


def solution(mesh):
    return jax.shard_map(
        shards,
        mesh=mesh,
        in_specs=(
            P("fsdp", "ctx", None),
            P("fsdp", "ctx", None),
            P("fsdp", "ctx", None),
            P(None, ("ctx", "fsdp")),
            P(("ctx", "fsdp")),
            P(("ctx", "fsdp"), None),
            P(("ctx", "fsdp"), None),
            P(("ctx", "fsdp"), None),
            P("ctx", None, "fsdp"),
            P("ctx", "fsdp", None),
        ),
        out_specs=(
            P("fsdp", "ctx", None),
            P("fsdp", "ctx", None),
            P(None, ("ctx", "fsdp")),
            P(("ctx", "fsdp")),
            P(("ctx", "fsdp"), None),
            P(("ctx", "fsdp"), None),
            P(("ctx", "fsdp"), None),
            P("ctx", None, "fsdp"),
            P("ctx", "fsdp", None),
        ),
        check_vma=False,
    )
```

```python
import functools
import math

import jax
import jax.numpy as jnp
from jax import lax
from jax.experimental import pallas as pl
from jax.experimental.pallas import tpu as pltpu
from jax.sharding import PartitionSpec as P

D = 768
H = 12
DH = 64
E = 64
NB = 32
CAP = 8
G = 4
HG = H // G
GW = HG * DH
CORES = 2

EPS = 1e-06
EDGES = (16, 23, 32, 45, 64, 91, 128, 181, 256, 362, 512, 724, 1024, 1448, 2048, 2896)
STARTS = tuple(range(16)) + EDGES
GELU_C = 0.7978845608028654
NEG = -1e30
MESH = pl.DeviceIdType.MESH
F32 = jnp.float32
BF = jnp.bfloat16
VM = pl.BlockSpec(memory_space=pltpu.VMEM)
HB = pl.BlockSpec(memory_space=pl.ANY)
SM = pl.BlockSpec(memory_space=pltpu.SMEM)
WINDOW = 3
LIMIT = 56 * 1024 * 1024


def dot(a, b, ca=1, cb=0):
    return lax.dot_general(a, b, (((ca,), (cb,)), ((), ())), preferred_element_type=F32)


def call(body, outs, ins, out_specs=None, in_specs=None, scratch=(), cid=None, name=None, cost=None, limit=LIMIT, **kw):
    params = dict(vmem_limit_bytes=limit)
    if cid is not None:
        params.update(collective_id=cid, has_side_effects=True)
    return pl.pallas_call(
        body,
        out_shape=outs,
        in_specs=in_specs or [VM] * len(ins),
        out_specs=out_specs or [VM] * len(outs),
        scratch_shapes=list(scratch),
        compiler_params=pltpu.CompilerParams(**params),
        name=name,
        cost_estimate=cost,
        **kw,
    )(*ins)


def sds(shape, kind=F32):
    return jax.ShapeDtypeStruct(shape, kind)


class Place:
    def __init__(self, n_ctx, nf):
        self.n_ctx, self.nf = n_ctx, nf
        self.R, self.X = n_ctx // G, nf // CORES
        self.c, self.f = lax.axis_index("ctx"), lax.axis_index("fsdp")
        self.g, self.r = lax.div(self.c, self.R), lax.rem(self.c, self.R)
        self.x, self.k = lax.div(self.f, CORES), lax.rem(self.f, CORES)

    def up(self, v, d, n):
        return lax.rem(v + d, n)

    def ctx(self, dg, dr):
        return self.up(self.g, dg % G, G) * self.R + self.up(self.r, dr % self.R, self.R)

    def fs(self, dx, dk):
        return self.up(self.x, dx % self.X, self.X) * CORES + self.up(self.k, dk % CORES, CORES)

    def dev(self, dg, dr, dx, dk):
        return (self.ctx(dg, dr), self.fs(dx, dk))


def greet(targets):
    bar = pltpu.get_barrier_semaphore()
    for t in targets:
        pl.semaphore_signal(bar, inc=1, device_id=t, device_id_type=MESH)
    pl.semaphore_wait(bar, len(targets))


def mirror(c, d, n):
    out, bit = 0, 1
    while bit < n:
        out = out + lax.rem(lax.div(c, bit) + (d // bit) % 2, 2) * bit
        bit *= 2
    return out


def mixed_order(n):
    far, near = list(range(n // 2, n)), list(range(1, n // 2))
    out = []
    while far or near:
        if far:
            out.append(far.pop(0))
        if near:
            out.append(near.pop(0))
    return out


class Sends:
    def __init__(self):
        self.made = []

    def __call__(self, src, dst, ss, rs, dev):
        cp = rcopy(src, dst, ss, rs, dev)
        cp.start()
        self.made.append(cp)
        return cp

    def finish(self):
        for cp in self.made:
            cp.wait_send()


def got(at, s, r, dev):
    rcopy(at, at, s, r, dev).wait_recv()


class Scatter:
    COUNT = 11

    @staticmethod
    def scratch(G_, R, X, blk, kind):
        sem = lambda *n: pltpu.SemaphoreType.DMA(n)
        vm = lambda *n: pltpu.VMEM(n + blk, kind)
        return [vm(G_, R, X), vm(G_, R, X), vm(R * X, G_), vm(G_), vm(G_), sem(1), sem(1), sem(R * X), sem(R * X), sem(G_), sem(G_)]

    def __init__(self, p, send, src, refs):
        self.p, self.send, self.src = p, send, src
        self.cin, self.s1, self.qin, self.s2, self.win = refs[:5]
        self.c1, self.e1, self.c2, self.e2, self.c3, self.e3 = refs[5:]
        self.quad = [(er, ex) for er in range(p.R) for ex in range(p.X)]

    def over_cores(self):
        p = self.p
        self.send(self.src.at[:, :, :, 1 - p.k], self.cin, self.c1.at[0], self.e1.at[0], p.dev(0, 0, 0, 1))

    def over_quad(self):
        p = self.p
        got(self.cin, self.c1.at[0], self.e1.at[0], p.dev(0, 0, 0, 1))
        self.s1[...] = (self.src[:, :, :, p.k].astype(F32) + self.cin[...].astype(F32)).astype(self.s1.dtype)
        for i, (er, ex) in enumerate(self.quad):
            if i:
                at = self.s1.at[:, p.up(p.r, er, p.R), p.up(p.x, ex, p.X)]
                self.send(at, self.qin.at[i], self.c2.at[i], self.e2.at[i], p.dev(0, er, ex, 0))

    def over_groups(self):
        p = self.p
        total = self.s1[:, p.r, p.x].astype(F32)
        for i, (er, ex) in enumerate(self.quad):
            if i:
                got(self.qin.at[i], self.c2.at[i], self.e2.at[i], p.dev(0, -er, -ex, 0))
                total = total + self.qin[i].astype(F32)
        self.s2[...] = total.astype(self.s2.dtype)
        self.win[p.g] = self.s2[p.g]
        for dg in (2, 1, 3):
            self.send(self.s2.at[p.up(p.g, dg, G)], self.win.at[p.g], self.c3.at[dg], self.e3.at[dg], p.dev(dg, 0, 0, 0))

    def pieces(self):
        p = self.p
        for dg in (1, 3, 2):
            got(self.win.at[p.up(p.g, G - dg, G)], self.c3.at[dg], self.e3.at[dg], p.dev(-dg, 0, 0, 0))
        return [self.win[i].astype(F32) for i in range(G)]


def rcopy(src, dst, ss, rs, dev):
    return pltpu.make_async_remote_copy(
        src_ref=src, dst_ref=dst, send_sem=ss, recv_sem=rs, device_id=dev, device_id_type=MESH
    )


def gather_body(n_ctx, nf, tok, wq, tile, xall, wall, tiles, t1s, t1r, t2s, t2r, w1s, w1r, w2s, w2r, w3s, w3r, v1s, v1r, v2s, v2r, v3s, v3r, loc):
    p = Place(n_ctx, nf)
    R, X = p.R, p.X
    quad = [(er, ex) for er in range(R) for ex in range(X)]
    greet(
        [p.dev(d, 0, 0, 0) for d in range(1, G)]
        + [p.dev(0, er, ex, 0) for er, ex in quad[1:]]
        + [p.dev(0, 0, 0, 1)]
    )
    mine = p.c * nf + p.f
    own_t = pltpu.make_async_copy(tok, xall.at[p.c], loc.at[0])
    own_w = pltpu.make_async_copy(wq.at[p.g], wall.at[mine], loc.at[1])
    own_v = pltpu.make_async_copy(tile, tiles.at[mine], loc.at[2])
    own_t.start()
    own_w.start()
    own_v.start()
    send = Sends()

    far = (2, 1, 3)
    for d in far:
        send(tile, tiles.at[mine], v1s.at[d], v1r.at[d], p.dev(d, 0, 0, 0))
        send(wq.at[p.up(p.g, d, G)], wall.at[mine], w1s.at[d], w1r.at[d], p.dev(d, 0, 0, 0))
    for d in far:
        send(tok, xall.at[p.c], t1s.at[d], t1r.at[d], p.dev(d, 0, 0, 0))
    for e in range(1, R):
        send(tok, xall.at[p.c], t2s.at[0, e], t2r.at[0, e], p.dev(0, e, 0, 0))
    for d in (0, 1, 3, 2):
        block = p.ctx(-d, 0) * nf + p.f
        src = wq.at[p.g] if d == 0 else wall.at[block]
        small = tile if d == 0 else tiles.at[block]
        if d:
            got(src, w1s.at[d], w1r.at[d], p.dev(-d, 0, 0, 0))
            got(small, v1s.at[d], v1r.at[d], p.dev(-d, 0, 0, 0))
        for i, (er, ex) in enumerate(quad):
            if i:
                send(small, tiles.at[block], v2s.at[d, i], v2r.at[d, i], p.dev(0, er, ex, 0))
                send(src, wall.at[block], w2s.at[d, i], w2r.at[d, i], p.dev(0, er, ex, 0))
        send(small, tiles.at[block], v3s.at[d, 0], v3r.at[d, 0], p.dev(0, 0, 0, 1))
        send(src, wall.at[block], w3s.at[d, 0], w3r.at[d, 0], p.dev(0, 0, 0, 1))
    for d in (1, 3, 2):
        block = p.ctx(-d, 0)
        src = xall.at[block]
        rcopy(src, src, t1s.at[d], t1r.at[d], p.dev(-d, 0, 0, 0)).wait_recv()
        for e in range(1, R):
            send(src, src, t2s.at[d, e], t2r.at[d, e], p.dev(0, e, 0, 0))
    for d in (0, 1, 3, 2):
        for i, (er, ex) in enumerate(quad):
            if i:
                block = p.ctx(-d, -er) * nf + p.fs(-ex, 0)
                src = wall.at[block]
                got(src, w2s.at[d, i], w2r.at[d, i], p.dev(0, -er, -ex, 0))
                send(src, src, w3s.at[d, i], w3r.at[d, i], p.dev(0, 0, 0, 1))
                small = tiles.at[block]
                got(small, v2s.at[d, i], v2r.at[d, i], p.dev(0, -er, -ex, 0))
                send(small, small, v3s.at[d, i], v3r.at[d, i], p.dev(0, 0, 0, 1))
    for d in range(G):
        for i, (er, ex) in enumerate(quad):
            block = p.ctx(-d, -er) * nf + p.fs(-ex, 1)
            got(wall.at[block], w3s.at[d, i], w3r.at[d, i], p.dev(0, 0, 0, 1))
            got(tiles.at[block], v3s.at[d, i], v3r.at[d, i], p.dev(0, 0, 0, 1))
        for e in range(1, R):
            src = xall.at[p.ctx(-d, -e)]
            rcopy(src, src, t2s.at[d, e], t2r.at[d, e], p.dev(0, -e, 0, 0)).wait_recv()
    send.finish()
    own_t.wait()
    own_w.wait()
    own_v.wait()


def gather(n_ctx, nf, tok, wq, tile):
    R, X = n_ctx // G, nf // CORES
    sem = lambda *s: pltpu.SemaphoreType.DMA(s)
    return call(
        functools.partial(gather_body, n_ctx, nf),
        [
            sds((n_ctx,) + tok.shape, BF),
            sds((n_ctx * nf,) + wq.shape[1:], BF),
            sds((n_ctx * nf,) + tile.shape, tile.dtype),
        ],
        [tok, wq, tile],
        out_specs=[HB, HB, HB],
        scratch=[sem(G)] * 2
        + [sem(G, R)] * 2
        + ([sem(G)] * 2 + [sem(G, R * X)] * 4) * 2
        + [sem(3)],
        cid=1,
        name="gather",
    )


def swap_body(n_ctx, nf, extra, *refs):
    p = Place(n_ctx, nf)
    src, more = refs[0], refs[1 : 1 + extra]
    dst, sums = refs[1 + extra], refs[2 + extra : 2 + 2 * extra]
    ss, rs, loc = refs[2 + 2 * extra : 5 + 2 * extra]
    rest = refs[5 + 2 * extra :]
    quad = [(er, ex) for er in range(p.R) for ex in range(p.X)]
    near = [p.dev(0, er, ex, 0) for er, ex in quad[1:]] + [p.dev(0, 0, 0, 1)]
    greet([p.dev(d, 0, 0, 0) for d in range(1, G)] + (near if extra else []))
    own = pltpu.make_async_copy(src.at[p.g], dst.at[p.g], loc)
    own.start()
    send = Sends()
    n = Scatter.COUNT
    scatters = [Scatter(p, send, m, rest[i * n : (i + 1) * n]) for i, m in enumerate(more)]
    for d in (2, 1, 3):
        send(src.at[p.up(p.g, d, G)], dst.at[p.g], ss.at[d], rs.at[d], p.dev(d, 0, 0, 0))
    for sc in scatters:
        sc.over_cores()
    for sc in scatters:
        sc.over_quad()
    for sc in scatters:
        sc.over_groups()
    for d in (1, 3, 2):
        got(dst.at[p.up(p.g, G - d, G)], ss.at[d], rs.at[d], p.dev(-d, 0, 0, 0))
    for sc, out in zip(scatters, sums):
        w = sc.pieces()
        out[...] = (w[0] + w[1]) + (w[2] + w[3])
    send.finish()
    own.wait()


def swap(n_ctx, nf, src, cid, name, more=()):
    sem = pltpu.SemaphoreType.DMA
    scratch = [sem((G,)), sem((G,)), sem]
    for m in more:
        scratch += Scatter.scratch(G, n_ctx // G, nf // CORES, m.shape[4:], m.dtype)
    return call(
        functools.partial(swap_body, n_ctx, nf, len(more)),
        [sds(src.shape, src.dtype)] + [sds(m.shape[4:]) for m in more],
        [src, *more],
        scratch=scratch,
        cid=cid,
        name=name,
    )


def dispatch_body(n_ctx, nf, packed, recv, ss, rs, xs, xr, ks, kr, loc):
    p = Place(n_ctx, nf)
    X = p.X
    greet(
        [(p.up(p.c, d, n_ctx), p.f) for d in range(1, n_ctx)]
        + [p.dev(0, 0, dx, 0) for dx in range(1, X)]
        + [p.dev(0, 0, 0, 1)]
    )
    own = pltpu.make_async_copy(packed.at[p.c], recv.at[:, p.f, p.c], loc)
    own.start()
    send = Sends()
    order = mixed_order(n_ctx)
    first = []

    def away(d):
        cc = mirror(p.c, d, n_ctx)
        first.append(send(packed.at[cc], recv.at[:, p.f, p.c], ss.at[d], rs.at[d], (cc, p.f)))

    def spread(d):
        cc = mirror(p.c, d, n_ctx)
        at = recv.at[:, p.f, cc]
        if d:
            got(at, ss.at[d], rs.at[d], (cc, p.f))
        src = packed.at[p.c] if d == 0 else at
        for dx in range(1, X):
            send(src, at, xs.at[d, dx], xr.at[d, dx], p.dev(0, 0, dx, 0))
        send(src, at, ks.at[d, 0], kr.at[d, 0], p.dev(0, 0, 0, 1))

    def relay(d):
        cc = mirror(p.c, d, n_ctx)
        for dx in range(1, X):
            at = recv.at[:, p.fs(-dx, 0), cc]
            got(at, xs.at[d, dx], xr.at[d, dx], p.dev(0, 0, -dx, 0))
            send(at, at, ks.at[d, dx], kr.at[d, dx], p.dev(0, 0, 0, 1))

    for d in order[:WINDOW]:
        away(d)
    spread(0)
    for i, d in enumerate(order):
        spread(d)
        if i + WINDOW < len(order):
            away(order[i + WINDOW])
        if i:
            relay(order[i - 1] if i > 1 else 0)
        if i == 1:
            relay(order[0])
    for d in order[max(1, len(order) - 1) :]:
        relay(d)
    for d in range(n_ctx):
        cc = mirror(p.c, d, n_ctx)
        for dx in range(X):
            at = recv.at[:, p.fs(-dx, 1), cc]
            got(at, ks.at[d, dx], kr.at[d, dx], p.dev(0, 0, 0, 1))
    send.finish()
    own.wait()


def dispatch(n_ctx, nf, packed):
    per_dev, width = packed.shape[1], packed.shape[3]
    X = nf // CORES
    sem = lambda *s: pltpu.SemaphoreType.DMA(s)
    return call(
        functools.partial(dispatch_body, n_ctx, nf),
        [sds((per_dev, nf, n_ctx, CAP, width), BF)],
        [packed],
        in_specs=[HB],
        out_specs=[HB],
        scratch=[sem(n_ctx)] * 2 + [sem(n_ctx, X)] * 4 + [pltpu.SemaphoreType.DMA],
        cid=3,
        name="dispatch",
    )[0]


def combine_body(n_ctx, nf, part, out, cin, xsum, xin, fin, ss, rs, xs, xr, ks, kr):
    p = Place(n_ctx, nf)
    X = p.X
    greet(
        [(p.up(p.c, d, n_ctx), p.f) for d in range(1, n_ctx)]
        + [p.dev(0, 0, dx, 0) for dx in range(1, X)]
        + [p.dev(0, 0, 0, 1)]
    )
    send = Sends()
    order = mixed_order(n_ctx) + [0]
    for d in order:
        cc = mirror(p.c, d, n_ctx)
        for dx in [*range(1, X), 0]:
            send(part.at[:, p.fs(dx, 1), cc], cin.at[dx, d], ks.at[d, dx], kr.at[d, dx], p.dev(0, 0, 0, 1))

    def across(d):
        cc = mirror(p.c, d, n_ctx)
        for dx in range(1, X):
            got(cin.at[dx, d], ks.at[d, dx], kr.at[d, dx], p.dev(0, 0, 0, 1))
            xsum[dx, d] = (part[:, p.fs(dx, 0), cc].astype(F32) + cin[dx, d].astype(F32)).astype(BF)
            send(xsum.at[dx, d], xin.at[dx, d], xs.at[d, dx], xr.at[d, dx], p.dev(0, 0, dx, 0))

    for d in order[: WINDOW - 1]:
        across(d)
    for i, d in enumerate(order):
        if i + WINDOW - 1 < len(order):
            across(order[i + WINDOW - 1])
        cc = mirror(p.c, d, n_ctx)
        got(cin.at[0, d], ks.at[d, 0], kr.at[d, 0], p.dev(0, 0, 0, 1))
        total = part[:, p.fs(0, 0), cc].astype(F32) + cin[0, d].astype(F32)
        for dx in range(1, X):
            got(xin.at[dx, d], xs.at[d, dx], xr.at[d, dx], p.dev(0, 0, -dx, 0))
            total = total + xin[dx, d].astype(F32)
        if d:
            fin[d] = total.astype(BF)
            send(fin.at[d], out.at[p.c], ss.at[d], rs.at[d], (cc, p.f))
        else:
            out[p.c] = total.astype(BF)
    for d in order[:-1]:
        cc = mirror(p.c, d, n_ctx)
        got(out.at[cc], ss.at[d], rs.at[d], (cc, p.f))
    send.finish()


def combine(n_ctx, nf, part):
    per_dev, width = part.shape[0], part.shape[-1]
    X = nf // CORES
    sem = lambda *s: pltpu.SemaphoreType.DMA(s)
    blk = (per_dev, CAP, width)
    return call(
        functools.partial(combine_body, n_ctx, nf),
        [sds((n_ctx,) + blk, BF)],
        [part],
        scratch=[pltpu.VMEM((X, n_ctx) + blk, BF)] * 3
        + [pltpu.VMEM((n_ctx,) + blk, BF)]
        + [sem(n_ctx)] * 2
        + [sem(n_ctx, X)] * 4,
        cid=4,
        name="combine",
    )[0]


def reduce_body(n_ctx, nf, dx_ref, dw_ref, tail_ref, tok_ref, gain_ref, dh1_ref, dtok_ref, dqkv_ref, dtail_ref, *refs):
    p = Place(n_ctx, nf)
    R, X = p.R, p.X
    rin, gsum, gin, a1, b1, a2, b2 = refs[:7]
    n = Scatter.COUNT
    quad = [(er, ex) for er in range(R) for ex in range(X)]
    greet(
        [p.dev(d, 0, 0, 0) for d in range(1, G)]
        + [p.dev(0, er, ex, 0) for er, ex in quad[1:]]
        + [p.dev(0, 0, 0, 1)]
    )
    send = Sends()
    wsum = Scatter(p, send, dw_ref, refs[7 : 7 + n])
    tsum = Scatter(p, send, tail_ref, refs[7 + n :])
    tsum.over_cores()
    wsum.over_cores()
    far = (2, 1, 3, 0)

    def near(dg):
        for er in range(1, R):
            send(dx_ref.at[p.ctx(dg, er)], rin.at[er, dg], a1.at[dg, er], b1.at[dg, er], p.dev(0, er, 0, 0))

    near(far[0])
    near(far[1])
    tsum.over_quad()
    wsum.over_quad()
    near(far[2])
    near(far[3])
    for dg in far:
        total = dx_ref[p.ctx(dg, 0)].astype(F32)
        for er in range(1, R):
            got(rin.at[er, dg], a1.at[dg, er], b1.at[dg, er], p.dev(0, -er, 0, 0))
            total = total + rin[er, dg].astype(F32)
        gsum[dg] = total.astype(BF)
        if dg:
            send(gsum.at[dg], gin.at[dg], a2.at[dg], b2.at[dg], p.dev(dg, 0, 0, 0))
        if dg == far[1]:
            tsum.over_groups()
            wsum.over_groups()
    grad = gsum[0].astype(F32)
    for dg in (1, 3, 2):
        got(gin.at[dg], a2.at[dg], b2.at[dg], p.dev(-dg, 0, 0, 0))
        grad = grad + gin[dg].astype(F32)
    rows = tok_ref[...].astype(F32)
    inv = lax.rsqrt(jnp.mean(rows * rows, axis=-1, keepdims=True) + EPS)
    hat = rows * inv
    grad = grad * gain_ref[...]
    dtok_ref[...] = dh1_ref[...] + inv * (grad - hat * jnp.mean(grad * hat, axis=-1, keepdims=True))
    w = tsum.pieces()
    dtail_ref[...] = (w[0] + w[1]) + (w[2] + w[3])
    dqkv_ref[...] = jnp.concatenate(wsum.pieces(), axis=1)
    send.finish()


def reduce_all(n_ctx, nf, dx, dw, tail, tok, gain, dh1):
    R, X = n_ctx // G, nf // CORES
    tb = dx.shape[1:]
    sem = lambda *n: pltpu.SemaphoreType.DMA(n)
    vm = lambda *n: pltpu.VMEM(n + tb, BF)
    return call(
        functools.partial(reduce_body, n_ctx, nf),
        [sds(tb), sds((dw.shape[4], D)), sds(tail.shape[4:])],
        [dx, dw, tail, tok, gain, dh1],
        scratch=[vm(R, G), vm(G), vm(G), sem(G, R), sem(G, R), sem(G), sem(G)]
        + Scatter.scratch(G, R, X, dw.shape[4:], BF)
        + Scatter.scratch(G, R, X, tail.shape[4:], F32),
        cid=6,
        name="reduce",
    )


def bias_tiles(tab_ref, tiles, g, R, nd):
    tok = tiles.shape[2]
    lane = lax.broadcasted_iota(jnp.int32, (8, 2 * tok), 1)

    def one(i, _):
        off = (i - (R - 1)) * tok + tok - lane
        for hh in range(HG):
            base = (g * HG + hh) * NB
            val = jnp.full(off.shape, NEG, F32)
            for b, e in enumerate(STARTS):
                val = jnp.where(off >= e, tab_ref[base + b], val)
            wide = jnp.concatenate([val] * (tok // 8), axis=0)
            wide = pltpu.roll(wide, tok, 1, stride=1, stride_axis=0)
            tiles[hh, i] = wide[:, :tok]
        return 0

    lax.fori_loop(0, nd, one, 0)


def normed(x_ref, b):
    rows = x_ref[b].astype(F32)
    inv = lax.rsqrt(jnp.mean(rows * rows, axis=-1, keepdims=True) + EPS)
    return rows * inv


def scores(q, keys, tiles, hh, gq, r, R, n):
    s = dot(q, keys, 1, 1) * (1.0 / math.sqrt(DH))
    bias = jnp.concatenate([tiles[hh, gq * R + r - kb + R - 1] for kb in range(n)], axis=1)
    return s + bias


def attend_body(n_ctx, nf, x_ref, w_ref, gain_ref, tab_ref, att_ref, lse_ref, q_ref, k_ref, v_ref, tiles):
    p = Place(n_ctx, nf)
    R, tok = p.R, x_ref.shape[1]
    gain = gain_ref[...]
    bias_tiles(tab_ref, tiles, p.g, R, n_ctx + R - 1)

    def block(b, _):
        xn = (normed(x_ref, b) * gain).astype(BF)
        at = pl.ds(pl.multiple_of(b * tok, tok), tok)
        for m, ref in ((1, k_ref), (2, v_ref)):
            y = dot(xn, w_ref[pl.ds(m * D, D)]).astype(BF)
            for hh in range(HG):
                ref[hh, at] = y[:, hh * DH : (hh + 1) * DH]
        return 0

    lax.fori_loop(0, n_ctx, block, 0)
    for gq in range(G):
        xn = (normed(x_ref, gq * R + p.r) * gain).astype(BF)
        y = dot(xn, w_ref[pl.ds(0, D)]).astype(BF)
        for hh in range(HG):
            q_ref[hh, pl.ds(gq * tok, tok)] = y[:, hh * DH : (hh + 1) * DH]
    for gq in range(G):
        n = (gq + 1) * R
        outs = []
        for hh in range(HG):
            s = scores(q_ref[hh, pl.ds(gq * tok, tok)], k_ref[hh, pl.ds(0, n * tok)], tiles, hh, gq, p.r, R, n)
            top = jnp.max(s, axis=-1, keepdims=True)
            w = jnp.exp(s - top)
            total = jnp.sum(w, axis=-1, keepdims=True)
            acc = dot(w.astype(BF), v_ref[hh, pl.ds(0, n * tok)])
            outs.append((acc / total).astype(BF))
            lse_ref[gq, :, hh : hh + 1] = top + jnp.log(total)
        att_ref[gq] = jnp.concatenate(outs, axis=1)


def attend_back_body(
    n_ctx, nf, x_ref, w_ref, gain_ref, tab_ref, lse_ref, q_ref, k_ref, v_ref, att_ref, do_ref,
    dx_ref, dw_ref, dgain_ref, dtab_ref, tiles, dtiles, dk_acc, dv_acc, xn_s, dq_s, dkv_s, dw_acc,
):
    p = Place(n_ctx, nf)
    R, tok = p.R, x_ref.shape[1]
    nd = n_ctx + R - 1
    scale = 1.0 / math.sqrt(DH)
    bias_tiles(tab_ref, tiles, p.g, R, nd)
    dtiles[...] = jnp.zeros_like(dtiles)
    dk_acc[...] = jnp.zeros_like(dk_acc)
    dv_acc[...] = jnp.zeros_like(dv_acc)
    for gq in range(G):
        n = (gq + 1) * R
        rows = pl.ds(gq * tok, tok)
        keys = pl.ds(0, n * tok)
        do_all = do_ref[gq]
        prod = do_all.astype(F32) * att_ref[gq].astype(F32)
        dqs = []
        for hh in range(HG):
            q, kk, vv = q_ref[hh, rows], k_ref[hh, keys], v_ref[hh, keys]
            do = do_all[:, hh * DH : (hh + 1) * DH]
            delta = jnp.sum(prod[:, hh * DH : (hh + 1) * DH], axis=-1, keepdims=True)
            s = scores(q, kk, tiles, hh, gq, p.r, R, n)
            w = jnp.exp(s - lse_ref[gq, :, hh : hh + 1])
            ds = w * (dot(do, vv, 1, 1) - delta)
            for kb in range(n):
                at = gq * R + p.r - kb + R - 1
                dtiles[hh, at] = dtiles[hh, at] + ds[:, kb * tok : (kb + 1) * tok]
            dsb = ds.astype(BF)
            dqs.append((dot(dsb, kk) * scale).astype(BF))
            dk_acc[hh, keys] = dk_acc[hh, keys] + dot(dsb, q, 0, 0)
            dv_acc[hh, keys] = dv_acc[hh, keys] + dot(w.astype(BF), do, 0, 0)
        dq_s[gq] = jnp.concatenate(dqs, axis=1)
    for hh in range(HG):
        sums = [None] * NB
        off0 = lax.broadcasted_iota(jnp.int32, (tok, tok), 0) - lax.broadcasted_iota(jnp.int32, (tok, tok), 1)
        for d in range(n_ctx):
            t = dtiles[hh, d + R - 1]
            off = off0 + d * tok
            for b in range(NB):
                low = STARTS[b]
                high = STARTS[b + 1] if b + 1 < NB else 1 << 30
                if high <= d * tok - tok + 1 or low > d * tok + tok - 1:
                    continue
                part = jnp.where((off >= low) & (off < high), t, 0.0)
                part = jnp.sum(part.reshape(tok // 8, 8, tok), axis=0)
                sums[b] = part if sums[b] is None else sums[b] + part
        for b in range(NB):
            dtab_ref[hh, b] = jnp.zeros((8, tok), F32) if sums[b] is None else sums[b]
    gain = gain_ref[...]
    xn_q = jnp.concatenate([(normed(x_ref, gq * R + p.r) * gain).astype(BF) for gq in range(G)], axis=0)
    dw_ref[pl.ds(0, D)] = dot(xn_q, dq_s[...].reshape(G * tok, GW), 0, 0).astype(BF)
    width = xn_s.shape[0]
    dgain = jnp.zeros((8, D), F32)
    for first in range(0, n_ctx, width):

        def block(i, dg):
            b = first + i
            hat = normed(x_ref, b)
            at = pl.ds(pl.multiple_of(b * tok, tok), tok)
            xn_s[i] = (hat * gain).astype(BF)
            dk = jnp.concatenate([(dk_acc[hh, at] * scale).astype(BF) for hh in range(HG)], axis=1)
            dv = jnp.concatenate([dv_acc[hh, at].astype(BF) for hh in range(HG)], axis=1)
            dkv_s[0, i] = dk
            dkv_s[1, i] = dv
            mine = lax.rem(b, R) == p.r
            dq = jnp.where(mine, dq_s[lax.div(b, R)], jnp.zeros((tok, GW), BF))
            dxn = (
                dot(dq, w_ref[pl.ds(0, D)], 1, 1)
                + dot(dk, w_ref[pl.ds(D, D)], 1, 1)
                + dot(dv, w_ref[pl.ds(2 * D, D)], 1, 1)
            )
            dx_ref[b] = dxn.astype(BF)
            return dg + jnp.sum((dxn * hat).reshape(tok // 8, 8, D), axis=0)

        dgain = lax.fori_loop(0, width, block, dgain)
        xn = xn_s[...].reshape(width * tok, D)
        for m in range(2):
            piece = dot(xn, dkv_s[m].reshape(width * tok, GW), 0, 0)
            if first:
                piece = piece + dw_acc[m]
            if first + width < n_ctx:
                dw_acc[m] = piece
            else:
                dw_ref[pl.ds((m + 1) * D, D)] = piece.astype(BF)
    dgain_ref[...] = dgain


def middle_body(
    att_ref, tok_ref, wo_ref, gain_ref, router_ref, routes_ref, cot_ref,
    h1_ref, xn2_ref, gate_ref, disp_ref, packed_ref,
):
    tok = tok_ref.shape[0]
    att = jnp.concatenate([att_ref[i] for i in range(G)], axis=1)
    h1 = tok_ref[...].astype(F32) + dot(att, wo_ref[...])
    h1_ref[...] = h1
    inv = lax.rsqrt(jnp.mean(h1 * h1, axis=-1, keepdims=True) + EPS)
    xn2 = (h1 * inv * gain_ref[...]).astype(BF)
    xn2_ref[...] = xn2
    logits = dot(xn2, router_ref[...])
    experts = lax.broadcasted_iota(jnp.int32, (tok, E), 1)
    route = [routes_ref[:, k : k + 1] for k in range(2)]
    member = [(route[k] == experts).astype(F32) for k in range(2)]
    chosen = [jnp.sum(logits * member[k], axis=-1, keepdims=True) for k in range(2)]
    top = jnp.maximum(chosen[0], chosen[1])
    ex = [jnp.exp(chosen[k] - top) for k in range(2)]
    gate = [ex[k] / (ex[0] + ex[1]) for k in range(2)]
    gate_ref[...] = jnp.concatenate(gate, axis=1)
    before = lax.broadcasted_iota(jnp.int32, (tok, tok), 0) > lax.broadcasted_iota(jnp.int32, (tok, tok), 1)
    counts = dot(before.astype(F32).astype(BF), (member[0] + member[1]).astype(BF))
    slots = lax.broadcasted_iota(jnp.int32, (tok, E * CAP), 1)
    disp = []
    for k in range(2):
        slot = jnp.sum(counts * member[k], axis=-1, keepdims=True).astype(jnp.int32)
        disp.append((route[k] * CAP + slot == slots).astype(F32).astype(BF))
        disp_ref[k] = disp[k]
    cot = cot_ref[...].astype(F32)
    packed_ref[:, :D] = dot(disp[0] + disp[1], xn2, 0, 0).astype(BF)
    rows = dot(disp[0], (gate[0] * cot).astype(BF), 0, 0) + dot(disp[1], (gate[1] * cot).astype(BF), 0, 0)
    packed_ref[:, D:] = rows.astype(BF)


def expert_body(x_ref, win_ref, wout_ref, part_ref, dwin_ref, dwout_ref):
    x, dy = x_ref[0, :, :D], x_ref[0, :, D:]
    win, wout = win_ref[0], wout_ref[0]
    pre = dot(x, win)
    inner = GELU_C * (pre + 0.044715 * pre * pre * pre)
    th = jnp.tanh(inner)
    hid = (0.5 * pre * (1.0 + th)).astype(BF)
    slope = 0.5 * (1.0 + th) + 0.5 * pre * (1.0 - th * th) * GELU_C * (1.0 + 3.0 * 0.044715 * pre * pre)
    dpre = (dot(dy, wout, 1, 1) * slope).astype(BF)
    part_ref[0, :, :D] = dot(hid, wout).astype(BF)
    part_ref[0, :, D:] = dot(dpre, win, 1, 1).astype(BF)
    dwin_ref[0] = dot(x, dpre, 0, 0)
    dwout_ref[0] = dot(hid, dy, 0, 0)


def experts(x, w_in, w_out):
    n, rows = x.shape[:2]
    ff = w_in.shape[2]
    spec = lambda *s: pl.BlockSpec((1,) + s, lambda i: (i, 0, 0))
    return pl.pallas_call(
        expert_body,
        grid=(n,),
        in_specs=[spec(rows, 2 * D), spec(D, ff), spec(ff, D)],
        out_specs=[spec(rows, 2 * D), spec(D, ff), spec(ff, D)],
        out_shape=[sds(x.shape, BF), sds((n, D, ff)), sds((n, ff, D))],
        compiler_params=pltpu.CompilerParams(vmem_limit_bytes=LIMIT),
        name="experts",
    )(x, w_in, w_out)


def after_body(
    ret_ref, disp_ref, h1_ref, xn2_ref, gate_ref, cot_ref, routes_ref, router_ref, wo_ref, att_ref, gain_ref,
    mixed_ref, dh1_ref, dat_ref, dout_ref, drouter_ref, dgain_ref,
):
    tok = h1_ref.shape[0]
    both = [dot(disp_ref[k], ret_ref[...]) for k in range(2)]
    gate = [gate_ref[:, k : k + 1] for k in range(2)]
    h1 = h1_ref[...]
    dy = cot_ref[...].astype(F32)
    picked = [both[k][:, :D] for k in range(2)]
    mixed_ref[...] = (h1 + (gate[0] * picked[0] + gate[1] * picked[1])).astype(BF)
    dgate = [jnp.sum(dy * picked[k], axis=-1, keepdims=True) for k in range(2)]
    mean = gate[0] * dgate[0] + gate[1] * dgate[1]
    lanes = lax.broadcasted_iota(jnp.int32, (tok, E), 1)
    dlog = jnp.zeros((tok, E), F32)
    for k in range(2):
        dlog = dlog + jnp.where(routes_ref[:, k : k + 1] == lanes, gate[k] * (dgate[k] - mean), 0.0)
    dlog = dlog.astype(BF)
    xn2 = xn2_ref[...]
    dxn = both[0][:, D:] + both[1][:, D:] + dot(dlog, router_ref[...], 1, 1)
    drouter_ref[...] = dot(xn2, dlog, 0, 0).astype(BF)
    inv = lax.rsqrt(jnp.mean(h1 * h1, axis=-1, keepdims=True) + EPS)
    hat = h1 * inv
    dgain_ref[...] = jnp.sum((dxn * hat).reshape(tok // 8, 8, D), axis=0)
    cen = dxn * gain_ref[...]
    dh1 = dy + inv * (cen - hat * jnp.mean(cen * hat, axis=-1, keepdims=True))
    dh1_ref[...] = dh1
    dh1b = dh1.astype(BF)
    att = jnp.concatenate([att_ref[i] for i in range(G)], axis=1)
    dout_ref[...] = dot(att, dh1b, 0, 0).astype(BF)
    dat = dot(dh1b, wo_ref[...], 1, 1).astype(BF)
    for i in range(G):
        dat_ref[i] = dat[:, i * GW : (i + 1) * GW]


def shards(tokens, routes, cotangent, gains, rel_bias, attn_qkv, attn_out, router, w_in, w_out):
    tok = tokens.shape[1]
    n_ctx, nf = lax.axis_size("ctx"), lax.axis_size("fsdp")
    n_dev = n_ctx * nf
    R, X = n_ctx // G, nf // CORES
    seq = tok * n_ctx
    per_dev = w_in.shape[0]
    qr, orows = attn_qkv.shape[0], attn_out.shape[0]
    axes = ("ctx", "fsdp")
    x2, cot, route2 = tokens.reshape(tok, D), cotangent.reshape(tok, D), routes.reshape(tok, 2)

    n_gain, n_bias = gains.size, rel_bias.size
    rr = -(-router.size // D)
    flat = jnp.pad(router.reshape(-1), (0, rr * D - router.size)).reshape(rr, D)
    pack = jnp.concatenate([attn_out, flat], axis=0)
    everything = lax.all_gather(pack, axes, axis=0, tiled=False)
    tile = jnp.concatenate([gains.reshape(-1), rel_bias]).astype(F32)
    tile = jnp.broadcast_to(jnp.pad(tile, (0, 128 - n_gain - n_bias)), (8, 128))

    wq = attn_qkv.reshape(qr, G, GW).transpose(1, 0, 2)
    xall, wall, tails = gather(n_ctx, nf, x2, wq, tile)
    wall = wall.reshape(n_dev * qr, GW)
    gains_full = tails[:, 0, :n_gain].reshape(n_dev, 2, -1).transpose(1, 0, 2).reshape(2, D)
    table = tails[:, 0, n_gain : n_gain + n_bias].reshape(H * NB)
    gain1, gain2 = gains_full[:1], gains_full[1:]
    wo = everything[:, :orows].reshape(D, D)
    router_full = everything[:, orows:].reshape(n_dev, rr * D)[:, : router.size].reshape(D, E)

    part = functools.partial
    width = math.gcd(n_ctx, 8)
    tiles = pltpu.VMEM((HG, n_ctx + R - 1, tok, tok), F32)
    att, lse, q, k, v = call(
        part(attend_body, n_ctx, nf),
        [sds((G, tok, GW), BF), sds((G, tok, 128)), sds((HG, G * tok, DH), BF)] + [sds((HG, seq, DH), BF)] * 2,
        [xall, wall, gain1, table],
        in_specs=[VM, VM, VM, SM],
        scratch=[tiles],
        name="attend",
    )
    att_in = swap(n_ctx, nf, att, 2, "swap_att")[0]
    h1, xn2, gate, disp, packed = call(
        middle_body,
        [sds((tok, D)), sds((tok, D), BF), sds((tok, 2)), sds((2, tok, E * CAP), BF), sds((E * CAP, 2 * D), BF)],
        [att_in, x2, wo, gain2, router_full, route2, cot],
        name="middle",
    )
    recv = dispatch(n_ctx, nf, packed.reshape(n_ctx, per_dev, CAP, 2 * D))
    rows = nf * n_ctx * CAP
    part_rows, d_w_in, d_w_out = experts(recv.reshape(per_dev, rows, 2 * D), w_in, w_out)
    ret = combine(n_ctx, nf, part_rows.reshape(per_dev, nf, n_ctx, CAP, 2 * D))
    mixed, dh1, dat, d_out, d_router, dgain2 = call(
        after_body,
        [sds((tok, D), BF), sds((tok, D)), sds((G, tok, GW), BF), sds((D, D), BF), sds((D, E), BF), sds((8, D))],
        [ret.reshape(E * CAP, 2 * D), disp, h1, xn2, gate, cot, route2, router_full, wo, att_in, gain2],
        name="after",
    )
    lead = (G, R, X, CORES)
    more = (d_out.reshape(lead + (orows, D)), d_router.reshape(lead + router.shape))
    do, d_out_mine, d_router_mine = swap(n_ctx, nf, dat, 5, "swap_dat", more)
    dx, dw, dgain1, dtab = call(
        part(attend_back_body, n_ctx, nf),
        [sds((n_ctx, tok, D), BF), sds((3 * D, GW), BF), sds((8, D)), sds((HG, NB, 8, tok))],
        [xall, wall, gain1, table, lse, q, k, v, att, do],
        in_specs=[VM, VM, VM, SM] + [VM] * 6,
        scratch=[
            tiles, tiles, pltpu.VMEM((HG, seq, DH), F32), pltpu.VMEM((HG, seq, DH), F32),
            pltpu.VMEM((width, tok, D), BF), pltpu.VMEM((G, tok, GW), BF), pltpu.VMEM((2, width, tok, GW), BF),
            pltpu.VMEM((2, D, GW) if width < n_ctx else (2, 8, GW), F32),
        ],
        name="attend_back",
        limit=LIMIT if width == n_ctx else 61 * 1024 * 1024,
    )
    dtab = jnp.sum(dtab, axis=(2, 3)).reshape(1, HG * NB)
    own_group = jnp.arange(G)[:, None] == lax.axis_index("ctx") // R
    dtab = jnp.where(own_group, dtab, 0.0).reshape(n_dev, n_bias)
    dgains = jnp.stack([jnp.sum(dgain1, axis=0), jnp.sum(dgain2, axis=0)])
    dgains = dgains.reshape(2, n_dev, -1).transpose(1, 0, 2).reshape(n_dev, n_gain)
    d_tail = jnp.pad(jnp.concatenate([dgains, dtab], axis=1), ((0, 0), (0, 128 - n_gain - n_bias)))
    d_tail = jnp.broadcast_to(d_tail[:, None, :], (n_dev, 8, 128)).reshape(lead + (8, 128))
    d_tokens, d_qkv, tail_mine = reduce_all(n_ctx, nf, dx, dw.reshape(lead + (qr, GW)), d_tail, x2, gain1, dh1)
    return (
        mixed.reshape(1, tok, D),
        d_tokens.reshape(1, tok, D),
        tail_mine[0, :n_gain].reshape(gains.shape),
        tail_mine[0, n_gain : n_gain + n_bias],
        d_qkv,
        d_out_mine,
        d_router_mine,
        d_w_in,
        d_w_out,
    )


def solution(mesh):
    return jax.shard_map(
        shards,
        mesh=mesh,
        in_specs=(
            P("fsdp", "ctx", None),
            P("fsdp", "ctx", None),
            P("fsdp", "ctx", None),
            P(None, ("ctx", "fsdp")),
            P(("ctx", "fsdp")),
            P(("ctx", "fsdp"), None),
            P(("ctx", "fsdp"), None),
            P(("ctx", "fsdp"), None),
            P("ctx", None, "fsdp"),
            P("ctx", "fsdp", None),
        ),
        out_specs=(
            P("fsdp", "ctx", None),
            P("fsdp", "ctx", None),
            P(None, ("ctx", "fsdp")),
            P(("ctx", "fsdp")),
            P(("ctx", "fsdp"), None),
            P(("ctx", "fsdp"), None),
            P(("ctx", "fsdp"), None),
            P("ctx", None, "fsdp"),
            P("ctx", "fsdp", None),
        ),
        check_vma=False,
    )
```

```python
import functools
import math

import jax
import jax.numpy as jnp
from jax import lax
from jax.experimental import pallas as pl
from jax.experimental.pallas import tpu as pltpu
from jax.sharding import PartitionSpec as P

D = 768
H = 12
DH = 64
E = 64
NB = 32
CAP = 8
G = 4
HG = H // G
GW = HG * DH
CORES = 2

EPS = 1e-06
EDGES = (16, 23, 32, 45, 64, 91, 128, 181, 256, 362, 512, 724, 1024, 1448, 2048, 2896)
STARTS = tuple(range(16)) + EDGES
GELU_C = 0.7978845608028654
NEG = -1e30
MESH = pl.DeviceIdType.MESH
F32 = jnp.float32
BF = jnp.bfloat16
VM = pl.BlockSpec(memory_space=pltpu.VMEM)
HB = pl.BlockSpec(memory_space=pl.ANY)
SM = pl.BlockSpec(memory_space=pltpu.SMEM)
WINDOW = 2
LIMIT = 56 * 1024 * 1024


def dot(a, b, ca=1, cb=0):
    return lax.dot_general(a, b, (((ca,), (cb,)), ((), ())), preferred_element_type=F32)


def call(body, outs, ins, out_specs=None, in_specs=None, scratch=(), cid=None, name=None, cost=None, limit=LIMIT, **kw):
    params = dict(vmem_limit_bytes=limit)
    if cid is not None:
        params.update(collective_id=cid, has_side_effects=True)
    return pl.pallas_call(
        body,
        out_shape=outs,
        in_specs=in_specs or [VM] * len(ins),
        out_specs=out_specs or [VM] * len(outs),
        scratch_shapes=list(scratch),
        compiler_params=pltpu.CompilerParams(**params),
        name=name,
        cost_estimate=cost,
        **kw,
    )(*ins)


def sds(shape, kind=F32):
    return jax.ShapeDtypeStruct(shape, kind)


class Place:
    def __init__(self, n_ctx, nf):
        self.n_ctx, self.nf = n_ctx, nf
        self.R, self.X = n_ctx // G, nf // CORES
        self.c, self.f = lax.axis_index("ctx"), lax.axis_index("fsdp")
        self.g, self.r = lax.div(self.c, self.R), lax.rem(self.c, self.R)
        self.x, self.k = lax.div(self.f, CORES), lax.rem(self.f, CORES)

    def up(self, v, d, n):
        return lax.rem(v + d, n)

    def ctx(self, dg, dr):
        return self.up(self.g, dg % G, G) * self.R + self.up(self.r, dr % self.R, self.R)

    def fs(self, dx, dk):
        return self.up(self.x, dx % self.X, self.X) * CORES + self.up(self.k, dk % CORES, CORES)

    def dev(self, dg, dr, dx, dk):
        return (self.ctx(dg, dr), self.fs(dx, dk))


def greet(targets):
    bar = pltpu.get_barrier_semaphore()
    for t in targets:
        pl.semaphore_signal(bar, inc=1, device_id=t, device_id_type=MESH)
    pl.semaphore_wait(bar, len(targets))


def mirror(c, d, n):
    out, bit = 0, 1
    while bit < n:
        out = out + lax.rem(lax.div(c, bit) + (d // bit) % 2, 2) * bit
        bit *= 2
    return out


def mixed_order(n):
    far, near = list(range(n // 2, n)), list(range(1, n // 2))
    out = []
    while far or near:
        if far:
            out.append(far.pop(0))
        if near:
            out.append(near.pop(0))
    return out


class Sends:
    def __init__(self):
        self.made = []

    def __call__(self, src, dst, ss, rs, dev):
        cp = rcopy(src, dst, ss, rs, dev)
        cp.start()
        self.made.append(cp)
        return cp

    def finish(self):
        for cp in self.made:
            cp.wait_send()


def got(at, s, r, dev):
    rcopy(at, at, s, r, dev).wait_recv()


class Scatter:
    COUNT = 11

    @staticmethod
    def scratch(G_, R, X, blk, kind):
        sem = lambda *n: pltpu.SemaphoreType.DMA(n)
        vm = lambda *n: pltpu.VMEM(n + blk, kind)
        return [vm(G_, R, X), vm(G_, R, X), vm(R * X, G_), vm(G_), vm(G_), sem(1), sem(1), sem(R * X), sem(R * X), sem(G_), sem(G_)]

    def __init__(self, p, send, src, refs):
        self.p, self.send, self.src = p, send, src
        self.cin, self.s1, self.qin, self.s2, self.win = refs[:5]
        self.c1, self.e1, self.c2, self.e2, self.c3, self.e3 = refs[5:]
        self.quad = [(er, ex) for er in range(p.R) for ex in range(p.X)]

    def over_cores(self):
        p = self.p
        self.send(self.src.at[:, :, :, 1 - p.k], self.cin, self.c1.at[0], self.e1.at[0], p.dev(0, 0, 0, 1))

    def over_quad(self):
        p = self.p
        got(self.cin, self.c1.at[0], self.e1.at[0], p.dev(0, 0, 0, 1))
        self.s1[...] = (self.src[:, :, :, p.k].astype(F32) + self.cin[...].astype(F32)).astype(self.s1.dtype)
        for i, (er, ex) in enumerate(self.quad):
            if i:
                at = self.s1.at[:, p.up(p.r, er, p.R), p.up(p.x, ex, p.X)]
                self.send(at, self.qin.at[i], self.c2.at[i], self.e2.at[i], p.dev(0, er, ex, 0))

    def over_groups(self):
        p = self.p
        total = self.s1[:, p.r, p.x].astype(F32)
        for i, (er, ex) in enumerate(self.quad):
            if i:
                got(self.qin.at[i], self.c2.at[i], self.e2.at[i], p.dev(0, -er, -ex, 0))
                total = total + self.qin[i].astype(F32)
        self.s2[...] = total.astype(self.s2.dtype)
        self.win[p.g] = self.s2[p.g]
        for dg in (2, 1, 3):
            self.send(self.s2.at[p.up(p.g, dg, G)], self.win.at[p.g], self.c3.at[dg], self.e3.at[dg], p.dev(dg, 0, 0, 0))

    def pieces(self):
        p = self.p
        for dg in (1, 3, 2):
            got(self.win.at[p.up(p.g, G - dg, G)], self.c3.at[dg], self.e3.at[dg], p.dev(-dg, 0, 0, 0))
        return [self.win[i].astype(F32) for i in range(G)]


def rcopy(src, dst, ss, rs, dev):
    return pltpu.make_async_remote_copy(
        src_ref=src, dst_ref=dst, send_sem=ss, recv_sem=rs, device_id=dev, device_id_type=MESH
    )


class Gather:
    COUNT = 8

    @staticmethod
    def scratch(R, X):
        sem = lambda *n: pltpu.SemaphoreType.DMA(n)
        return [sem(G)] * 2 + [sem(G, R)] * 2 + [sem(G, R, X)] * 4

    def __init__(self, p, send, piece, out, refs):
        self.p, self.send, self.piece, self.out = p, send, piece, out
        self.a, self.b = refs[0::2], refs[1::2]

    def at(self, d, er, ex, ek):
        p = self.p
        return self.out.at[p.ctx(-d, -er) * p.nf + p.fs(-ex, -ek)]

    def over_groups(self):
        p = self.p
        for d in (2, 1, 3):
            self.send(self.piece(d), self.at(0, 0, 0, 0), self.a[0].at[d], self.b[0].at[d], p.dev(d, 0, 0, 0))

    def over_rows(self, d):
        p, at = self.p, self.at(d, 0, 0, 0)
        if d:
            got(at, self.a[0].at[d], self.b[0].at[d], p.dev(-d, 0, 0, 0))
        src = at if d else self.piece(0)
        for er in range(1, p.R):
            self.send(src, at, self.a[1].at[d, er], self.b[1].at[d, er], p.dev(0, er, 0, 0))
        self.onward(d, 0, src, at)

    def onward(self, d, er, src, at):
        p = self.p
        for ex in range(1, p.X):
            self.send(src, at, self.a[2].at[d, er, ex], self.b[2].at[d, er, ex], p.dev(0, 0, ex, 0))
        self.send(src, at, self.a[3].at[d, er, 0], self.b[3].at[d, er, 0], p.dev(0, 0, 0, 1))

    def over_x(self, d):
        p = self.p
        for er in range(1, p.R):
            at = self.at(d, er, 0, 0)
            got(at, self.a[1].at[d, er], self.b[1].at[d, er], p.dev(0, -er, 0, 0))
            self.onward(d, er, at, at)

    def over_cores(self, d):
        p = self.p
        for er in range(p.R):
            for ex in range(1, p.X):
                at = self.at(d, er, ex, 0)
                got(at, self.a[2].at[d, er, ex], self.b[2].at[d, er, ex], p.dev(0, 0, -ex, 0))
                self.send(at, at, self.a[3].at[d, er, ex], self.b[3].at[d, er, ex], p.dev(0, 0, 0, 1))

    def settle(self):
        p = self.p
        for d in range(G):
            for er in range(p.R):
                for ex in range(p.X):
                    got(self.at(d, er, ex, 1), self.a[3].at[d, er, ex], self.b[3].at[d, er, ex], p.dev(0, 0, 0, 1))


def gather_body(n_ctx, nf, tok, aq, ao, router, tile, xall, wall, oall, tiles, wq, wo, t1s, t1r, t2s, t2r, loc, *refs):
    p = Place(n_ctx, nf)
    R, X = p.R, p.X
    for i in range(G):
        wq[i] = aq[:, i * GW : (i + 1) * GW]
    wo[:, :D] = ao[...]
    wo[:, D : D + E] = router[...]
    wo[:, D + E :] = jnp.zeros((wo.shape[0], E), BF)
    greet(
        [p.dev(d, 0, 0, 0) for d in range(1, G)]
        + [p.dev(0, er, 0, 0) for er in range(1, R)]
        + [p.dev(0, 0, ex, 0) for ex in range(1, X)]
        + [p.dev(0, 0, 0, 1)]
    )
    send = Sends()
    n = Gather.COUNT
    items = [
        Gather(p, send, lambda d: tile, tiles, refs[:n]),
        Gather(p, send, lambda d: wq.at[p.up(p.g, d, G)], wall, refs[n : 2 * n]),
        Gather(p, send, lambda d: wo, oall, refs[2 * n :]),
    ]
    own = [
        pltpu.make_async_copy(src, dst, loc.at[i])
        for i, (src, dst) in enumerate([(tok, xall.at[p.c])] + [(it.piece(0), it.at(0, 0, 0, 0)) for it in items])
    ]
    for cp in own:
        cp.start()
    sides = [(s, -1) for s in range(1, G)] + [(s, 1) for s in range(1, G)]

    def exists(at):
        return (p.g + at >= 0) & (p.g + at < G)

    def hop(s, way):
        at = way * (s - 1)
        src = tok if s == 1 else xall.at[p.ctx(at, 0)]
        i = s + (G if way > 0 else 0)
        return rcopy(src, xall.at[p.ctx(at, 0)], t1s.at[i], t1r.at[i], p.dev(-way, 0, 0, 0))

    def row(at, e):
        src = tok if at == 0 else xall.at[p.ctx(at, 0)]
        return rcopy(src, xall.at[p.ctx(at, 0)], t2s.at[at + G, e], t2r.at[at + G, e], p.dev(0, e, 0, 0))

    def step(s):
        for way in (-1, 1):

            @pl.when(exists(way * s))
            def _():
                i = s + (G if way > 0 else 0)
                got(xall.at[p.ctx(way * s, 0)], t1s.at[i], t1r.at[i], p.dev(way, 0, 0, 0))
                if s + 1 < G:

                    @pl.when(exists(-way))
                    def _():
                        hop(s + 1, way).start()

                for e in range(1, R):
                    row(way * s, e).start()

    for it in items[:2]:
        it.over_groups()
    for way in (-1, 1):

        @pl.when(exists(-way))
        def _():
            hop(1, way).start()

    for e in range(1, R):
        row(0, e).start()
    items[2].over_groups()
    for it in items:
        it.over_rows(0)
    step(1)
    for it in items[:2]:
        it.over_rows(1)
        it.over_rows(3)
    step(2)
    for d in (1, 3):
        items[2].over_rows(d)
    for it in items[:2]:
        it.over_rows(2)
    step(3)
    items[2].over_rows(2)
    for it in items:
        for d in (0, 1, 3, 2):
            it.over_x(d)
    for it in items:
        for d in (0, 1, 3, 2):
            it.over_cores(d)
    for it in items:
        it.settle()
    for at in range(1 - G, G):

        @pl.when(exists(at))
        def _():
            for e in range(1, R):
                got(xall.at[p.ctx(at, -e)], t2s.at[at + G, e], t2r.at[at + G, e], p.dev(0, -e, 0, 0))
                row(at, e).wait_send()

    for s, way in sides:

        @pl.when(exists(-way) & exists(way * (s - 1)))
        def _():
            hop(s, way).wait_send()

    send.finish()
    for cp in own:
        cp.wait()


def gather(n_ctx, nf, tok, aq, ao, router, tile):
    R, X = n_ctx // G, nf // CORES
    n_dev = n_ctx * nf
    sem = lambda *s: pltpu.SemaphoreType.DMA(s)
    qr, rows = aq.shape[0], ao.shape[0]
    return call(
        functools.partial(gather_body, n_ctx, nf),
        [
            sds((n_ctx,) + tok.shape, BF),
            sds((n_dev, qr, GW), BF),
            sds((n_dev, rows, D + 2 * E), BF),
            sds((n_dev,) + tile.shape, tile.dtype),
        ],
        [tok, aq, ao, router, tile],
        out_specs=[HB] * 4,
        scratch=[pltpu.VMEM((G, qr, GW), BF), pltpu.VMEM((rows, D + 2 * E), BF)]
        + [sem(2 * G)] * 2
        + [sem(2 * G, R)] * 2
        + [sem(4)]
        + Gather.scratch(R, X) * 3,
        cid=1,
        name="gather",
    )


def swap_body(n_ctx, nf, extra, *refs):
    p = Place(n_ctx, nf)
    src, more = refs[0], refs[1 : 1 + extra]
    dst, sums = refs[1 + extra], refs[2 + extra : 2 + 2 * extra]
    ss, rs, loc = refs[2 + 2 * extra : 5 + 2 * extra]
    rest = refs[5 + 2 * extra :]
    quad = [(er, ex) for er in range(p.R) for ex in range(p.X)]
    near = [p.dev(0, er, ex, 0) for er, ex in quad[1:]] + [p.dev(0, 0, 0, 1)]
    greet([p.dev(d, 0, 0, 0) for d in range(1, G)] + (near if extra else []))
    own = pltpu.make_async_copy(src.at[p.g], dst.at[p.g], loc)
    own.start()
    send = Sends()
    n = Scatter.COUNT
    scatters = [Scatter(p, send, m, rest[i * n : (i + 1) * n]) for i, m in enumerate(more)]
    for d in (2, 1, 3):
        send(src.at[p.up(p.g, d, G)], dst.at[p.g], ss.at[d], rs.at[d], p.dev(d, 0, 0, 0))
    for sc in scatters:
        sc.over_cores()
    for sc in scatters:
        sc.over_quad()
    for sc in scatters:
        sc.over_groups()
    for d in (1, 3, 2):
        got(dst.at[p.up(p.g, G - d, G)], ss.at[d], rs.at[d], p.dev(-d, 0, 0, 0))
    for sc, out in zip(scatters, sums):
        w = sc.pieces()
        out[...] = (w[0] + w[1]) + (w[2] + w[3])
    send.finish()
    own.wait()


def swap(n_ctx, nf, src, cid, name, more=()):
    sem = pltpu.SemaphoreType.DMA
    scratch = [sem((G,)), sem((G,)), sem]
    for m in more:
        scratch += Scatter.scratch(G, n_ctx // G, nf // CORES, m.shape[4:], m.dtype)
    return call(
        functools.partial(swap_body, n_ctx, nf, len(more)),
        [sds(src.shape, src.dtype)] + [sds(m.shape[4:]) for m in more],
        [src, *more],
        scratch=scratch,
        cid=cid,
        name=name,
    )


def dispatch_body(n_ctx, nf, packed, recv, ss, rs, xs, xr, ks, kr, loc):
    p = Place(n_ctx, nf)
    X = p.X
    greet(
        [(p.up(p.c, d, n_ctx), p.f) for d in range(1, n_ctx)]
        + [p.dev(0, 0, dx, 0) for dx in range(1, X)]
        + [p.dev(0, 0, 0, 1)]
    )
    own = pltpu.make_async_copy(packed.at[p.c], recv.at[:, p.f, p.c], loc)
    own.start()
    send = Sends()
    order = mixed_order(n_ctx)
    first = []

    def away(d):
        cc = mirror(p.c, d, n_ctx)
        first.append(send(packed.at[cc], recv.at[:, p.f, p.c], ss.at[d], rs.at[d], (cc, p.f)))

    def spread(d):
        cc = mirror(p.c, d, n_ctx)
        at = recv.at[:, p.f, cc]
        if d:
            got(at, ss.at[d], rs.at[d], (cc, p.f))
        src = packed.at[p.c] if d == 0 else at
        for dx in range(1, X):
            send(src, at, xs.at[d, dx], xr.at[d, dx], p.dev(0, 0, dx, 0))
        send(src, at, ks.at[d, 0], kr.at[d, 0], p.dev(0, 0, 0, 1))

    def relay(d):
        cc = mirror(p.c, d, n_ctx)
        for dx in range(1, X):
            at = recv.at[:, p.fs(-dx, 0), cc]
            got(at, xs.at[d, dx], xr.at[d, dx], p.dev(0, 0, -dx, 0))
            send(at, at, ks.at[d, dx], kr.at[d, dx], p.dev(0, 0, 0, 1))

    for d in order[:WINDOW]:
        away(d)
    spread(0)
    for i, d in enumerate(order):
        spread(d)
        if i + WINDOW < len(order):
            away(order[i + WINDOW])
        if i:
            relay(order[i - 1] if i > 1 else 0)
        if i == 1:
            relay(order[0])
    for d in order[max(1, len(order) - 1) :]:
        relay(d)
    for d in range(n_ctx):
        cc = mirror(p.c, d, n_ctx)
        for dx in range(X):
            at = recv.at[:, p.fs(-dx, 1), cc]
            got(at, ks.at[d, dx], kr.at[d, dx], p.dev(0, 0, 0, 1))
    send.finish()
    own.wait()


def dispatch(n_ctx, nf, packed):
    per_dev, width = packed.shape[1], packed.shape[3]
    X = nf // CORES
    sem = lambda *s: pltpu.SemaphoreType.DMA(s)
    return call(
        functools.partial(dispatch_body, n_ctx, nf),
        [sds((per_dev, nf, n_ctx, CAP, width), BF)],
        [packed],
        in_specs=[HB],
        out_specs=[HB],
        scratch=[sem(n_ctx)] * 2 + [sem(n_ctx, X)] * 4 + [pltpu.SemaphoreType.DMA],
        cid=3,
        name="dispatch",
    )[0]


def combine_body(n_ctx, nf, part, out, cin, xsum, xin, fin, ss, rs, xs, xr, ks, kr):
    p = Place(n_ctx, nf)
    X = p.X
    greet(
        [(p.up(p.c, d, n_ctx), p.f) for d in range(1, n_ctx)]
        + [p.dev(0, 0, dx, 0) for dx in range(1, X)]
        + [p.dev(0, 0, 0, 1)]
    )
    send = Sends()
    order = mixed_order(n_ctx) + [0]
    for d in order:
        cc = mirror(p.c, d, n_ctx)
        for dx in [*range(1, X), 0]:
            send(part.at[:, p.fs(dx, 1), cc], cin.at[dx, d], ks.at[d, dx], kr.at[d, dx], p.dev(0, 0, 0, 1))

    def across(d):
        cc = mirror(p.c, d, n_ctx)
        for dx in range(1, X):
            got(cin.at[dx, d], ks.at[d, dx], kr.at[d, dx], p.dev(0, 0, 0, 1))
            xsum[dx, d] = (part[:, p.fs(dx, 0), cc].astype(F32) + cin[dx, d].astype(F32)).astype(BF)
            send(xsum.at[dx, d], xin.at[dx, d], xs.at[d, dx], xr.at[d, dx], p.dev(0, 0, dx, 0))

    for d in order[:2]:
        across(d)
    for i, d in enumerate(order):
        if i + 2 < len(order):
            across(order[i + 2])
        cc = mirror(p.c, d, n_ctx)
        got(cin.at[0, d], ks.at[d, 0], kr.at[d, 0], p.dev(0, 0, 0, 1))
        total = part[:, p.fs(0, 0), cc].astype(F32) + cin[0, d].astype(F32)
        for dx in range(1, X):
            got(xin.at[dx, d], xs.at[d, dx], xr.at[d, dx], p.dev(0, 0, -dx, 0))
            total = total + xin[dx, d].astype(F32)
        if d:
            fin[d] = total.astype(BF)
            send(fin.at[d], out.at[p.c], ss.at[d], rs.at[d], (cc, p.f))
        else:
            out[p.c] = total.astype(BF)
    for d in order[:-1]:
        cc = mirror(p.c, d, n_ctx)
        got(out.at[cc], ss.at[d], rs.at[d], (cc, p.f))
    send.finish()


def combine(n_ctx, nf, part):
    per_dev, width = part.shape[0], part.shape[-1]
    X = nf // CORES
    sem = lambda *s: pltpu.SemaphoreType.DMA(s)
    blk = (per_dev, CAP, width)
    return call(
        functools.partial(combine_body, n_ctx, nf),
        [sds((n_ctx,) + blk, BF)],
        [part],
        scratch=[pltpu.VMEM((X, n_ctx) + blk, BF)] * 3
        + [pltpu.VMEM((n_ctx,) + blk, BF)]
        + [sem(n_ctx)] * 2
        + [sem(n_ctx, X)] * 4,
        cid=4,
        name="combine",
    )[0]


def reduce_body(n_ctx, nf, dx_ref, dw_ref, tail_ref, tok_ref, gain_ref, dh1_ref, dtok_ref, dqkv_ref, dtail_ref, *refs):
    p = Place(n_ctx, nf)
    R, X = p.R, p.X
    rin, gsum, gin, a1, b1, a2, b2 = refs[:7]
    n = Scatter.COUNT
    quad = [(er, ex) for er in range(R) for ex in range(X)]
    greet(
        [p.dev(d, 0, 0, 0) for d in range(1, G)]
        + [p.dev(0, er, ex, 0) for er, ex in quad[1:]]
        + [p.dev(0, 0, 0, 1)]
    )
    send = Sends()
    wsum = Scatter(p, send, dw_ref, refs[7 : 7 + n])
    tsum = Scatter(p, send, tail_ref, refs[7 + n :])
    tsum.over_cores()
    wsum.over_cores()
    far = (2, 1, 3, 0)

    def near(dg):
        for er in range(1, R):
            send(dx_ref.at[p.ctx(dg, er)], rin.at[er, dg], a1.at[dg, er], b1.at[dg, er], p.dev(0, er, 0, 0))

    near(far[0])
    near(far[1])
    tsum.over_quad()
    wsum.over_quad()
    near(far[2])
    near(far[3])
    for dg in far:
        total = dx_ref[p.ctx(dg, 0)].astype(F32)
        for er in range(1, R):
            got(rin.at[er, dg], a1.at[dg, er], b1.at[dg, er], p.dev(0, -er, 0, 0))
            total = total + rin[er, dg].astype(F32)
        gsum[dg] = total.astype(BF)
        if dg:
            send(gsum.at[dg], gin.at[dg], a2.at[dg], b2.at[dg], p.dev(dg, 0, 0, 0))
        if dg == far[1]:
            tsum.over_groups()
            wsum.over_groups()
    grad = gsum[0].astype(F32)
    for dg in (1, 3, 2):
        got(gin.at[dg], a2.at[dg], b2.at[dg], p.dev(-dg, 0, 0, 0))
        grad = grad + gin[dg].astype(F32)
    rows = tok_ref[...].astype(F32)
    inv = lax.rsqrt(jnp.mean(rows * rows, axis=-1, keepdims=True) + EPS)
    hat = rows * inv
    grad = grad * gain_ref[...]
    dtok_ref[...] = dh1_ref[...] + inv * (grad - hat * jnp.mean(grad * hat, axis=-1, keepdims=True))
    w = tsum.pieces()
    dtail_ref[...] = (w[0] + w[1]) + (w[2] + w[3])
    dqkv_ref[...] = jnp.concatenate(wsum.pieces(), axis=1)
    send.finish()


def reduce_all(n_ctx, nf, dx, dw, tail, tok, gain, dh1):
    R, X = n_ctx // G, nf // CORES
    tb = dx.shape[1:]
    sem = lambda *n: pltpu.SemaphoreType.DMA(n)
    vm = lambda *n: pltpu.VMEM(n + tb, BF)
    return call(
        functools.partial(reduce_body, n_ctx, nf),
        [sds(tb), sds((dw.shape[4], D)), sds(tail.shape[4:])],
        [dx, dw, tail, tok, gain, dh1],
        scratch=[vm(R, G), vm(G), vm(G), sem(G, R), sem(G, R), sem(G), sem(G)]
        + Scatter.scratch(G, R, X, dw.shape[4:], BF)
        + Scatter.scratch(G, R, X, tail.shape[4:], F32),
        cid=6,
        name="reduce",
    )


def bias_tiles(tab_ref, tiles, g, R, nd):
    tok = tiles.shape[2]
    lane = lax.broadcasted_iota(jnp.int32, (8, 2 * tok), 1)

    def one(i, _):
        off = (i - (R - 1)) * tok + tok - lane
        for hh in range(HG):
            base = (g * HG + hh) * NB
            val = jnp.full(off.shape, NEG, F32)
            for b, e in enumerate(STARTS):
                val = jnp.where(off >= e, tab_ref[base + b], val)
            wide = jnp.concatenate([val] * (tok // 8), axis=0)
            wide = pltpu.roll(wide, tok, 1, stride=1, stride_axis=0)
            tiles[hh, i] = wide[:, :tok]
        return 0

    lax.fori_loop(0, nd, one, 0)


def normed(x_ref, b):
    rows = x_ref[b].astype(F32)
    inv = lax.rsqrt(jnp.mean(rows * rows, axis=-1, keepdims=True) + EPS)
    return rows * inv


def scores(q, keys, tiles, hh, gq, r, R, n):
    s = dot(q, keys, 1, 1) * (1.0 / math.sqrt(DH))
    bias = jnp.concatenate([tiles[hh, gq * R + r - kb + R - 1] for kb in range(n)], axis=1)
    return s + bias


def attend_body(n_ctx, nf, x_ref, w_ref, tails_ref, tab_ref, att_ref, lse_ref, q_ref, k_ref, v_ref, tiles, gain1_ref, gain2_ref):
    p = Place(n_ctx, nf)
    R, tok = p.R, x_ref.shape[1]
    gw = D // (n_ctx * nf)
    for i in range(n_ctx * nf):
        gain1_ref[:, i * gw : (i + 1) * gw] = tails_ref[i, 0:1, :gw]
        gain2_ref[:, i * gw : (i + 1) * gw] = tails_ref[i, 0:1, gw : 2 * gw]
    gain = gain1_ref[...]
    bias_tiles(tab_ref, tiles, p.g, R, n_ctx + R - 1)

    def block(b, _):
        xn = (normed(x_ref, b) * gain).astype(BF)
        at = pl.ds(pl.multiple_of(b * tok, tok), tok)
        for m, ref in ((1, k_ref), (2, v_ref)):
            y = dot(xn, w_ref[pl.ds(m * D, D)]).astype(BF)
            for hh in range(HG):
                ref[hh, at] = y[:, hh * DH : (hh + 1) * DH]
        return 0

    lax.fori_loop(0, n_ctx, block, 0)
    for gq in range(G):
        xn = (normed(x_ref, gq * R + p.r) * gain).astype(BF)
        y = dot(xn, w_ref[pl.ds(0, D)]).astype(BF)
        for hh in range(HG):
            q_ref[hh, pl.ds(gq * tok, tok)] = y[:, hh * DH : (hh + 1) * DH]
    for gq in range(G):
        n = (gq + 1) * R
        outs = []
        for hh in range(HG):
            s = scores(q_ref[hh, pl.ds(gq * tok, tok)], k_ref[hh, pl.ds(0, n * tok)], tiles, hh, gq, p.r, R, n)
            top = jnp.max(s, axis=-1, keepdims=True)
            w = jnp.exp(s - top)
            total = jnp.sum(w, axis=-1, keepdims=True)
            acc = dot(w.astype(BF), v_ref[hh, pl.ds(0, n * tok)])
            outs.append((acc / total).astype(BF))
            lse_ref[gq, :, hh : hh + 1] = top + jnp.log(total)
        att_ref[gq] = jnp.concatenate(outs, axis=1)


def attend_back_body(
    n_ctx, nf, x_ref, w_ref, gain_ref, tiles, lse_ref, q_ref, k_ref, v_ref, att_ref, do_ref,
    dx_ref, dw_ref, dgain_ref, dtab_ref, dtiles, dk_acc, dv_acc, xn_s, dq_s, dkv_s, dw_acc,
):
    p = Place(n_ctx, nf)
    R, tok = p.R, x_ref.shape[1]
    scale = 1.0 / math.sqrt(DH)
    dtiles[...] = jnp.zeros_like(dtiles)
    dk_acc[...] = jnp.zeros_like(dk_acc)
    dv_acc[...] = jnp.zeros_like(dv_acc)
    for gq in range(G):
        n = (gq + 1) * R
        rows = pl.ds(gq * tok, tok)
        keys = pl.ds(0, n * tok)
        do_all = do_ref[gq]
        prod = do_all.astype(F32) * att_ref[gq].astype(F32)
        dqs = []
        for hh in range(HG):
            q, kk, vv = q_ref[hh, rows], k_ref[hh, keys], v_ref[hh, keys]
            do = do_all[:, hh * DH : (hh + 1) * DH]
            delta = jnp.sum(prod[:, hh * DH : (hh + 1) * DH], axis=-1, keepdims=True)
            s = scores(q, kk, tiles, hh, gq, p.r, R, n)
            w = jnp.exp(s - lse_ref[gq, :, hh : hh + 1])
            ds = w * (dot(do, vv, 1, 1) - delta)
            for kb in range(n):
                at = gq * R + p.r - kb + R - 1
                dtiles[hh, at] = dtiles[hh, at] + ds[:, kb * tok : (kb + 1) * tok]
            dsb = ds.astype(BF)
            dqs.append((dot(dsb, kk) * scale).astype(BF))
            dk_acc[hh, keys] = dk_acc[hh, keys] + dot(dsb, q, 0, 0)
            dv_acc[hh, keys] = dv_acc[hh, keys] + dot(w.astype(BF), do, 0, 0)
        dq_s[gq] = jnp.concatenate(dqs, axis=1)
    for hh in range(HG):
        sums = [None] * NB
        off0 = lax.broadcasted_iota(jnp.int32, (tok, tok), 0) - lax.broadcasted_iota(jnp.int32, (tok, tok), 1)
        for d in range(n_ctx):
            t = dtiles[hh, d + R - 1]
            off = off0 + d * tok
            for b in range(NB):
                low = STARTS[b]
                high = STARTS[b + 1] if b + 1 < NB else 1 << 30
                if high <= d * tok - tok + 1 or low > d * tok + tok - 1:
                    continue
                part = jnp.where((off >= low) & (off < high), t, 0.0)
                part = jnp.sum(part.reshape(tok // 8, 8, tok), axis=0)
                sums[b] = part if sums[b] is None else sums[b] + part
        for b in range(NB):
            dtab_ref[hh, b] = jnp.zeros((8, tok), F32) if sums[b] is None else sums[b]
    gain = gain_ref[...]
    xn_q = jnp.concatenate([(normed(x_ref, gq * R + p.r) * gain).astype(BF) for gq in range(G)], axis=0)
    dw_ref[pl.ds(0, D)] = dot(xn_q, dq_s[...].reshape(G * tok, GW), 0, 0).astype(BF)
    width = xn_s.shape[0]
    dgain = jnp.zeros((8, D), F32)
    for first in range(0, n_ctx, width):

        def block(i, dg):
            b = first + i
            hat = normed(x_ref, b)
            at = pl.ds(pl.multiple_of(b * tok, tok), tok)
            xn_s[i] = (hat * gain).astype(BF)
            dk = jnp.concatenate([(dk_acc[hh, at] * scale).astype(BF) for hh in range(HG)], axis=1)
            dv = jnp.concatenate([dv_acc[hh, at].astype(BF) for hh in range(HG)], axis=1)
            dkv_s[0, i] = dk
            dkv_s[1, i] = dv
            mine = lax.rem(b, R) == p.r
            dq = jnp.where(mine, dq_s[lax.div(b, R)], jnp.zeros((tok, GW), BF))
            dxn = (
                dot(dq, w_ref[pl.ds(0, D)], 1, 1)
                + dot(dk, w_ref[pl.ds(D, D)], 1, 1)
                + dot(dv, w_ref[pl.ds(2 * D, D)], 1, 1)
            )
            dx_ref[b] = dxn.astype(BF)
            return dg + jnp.sum((dxn * hat).reshape(tok // 8, 8, D), axis=0)

        dgain = lax.fori_loop(0, width, block, dgain)
        xn = xn_s[...].reshape(width * tok, D)
        for m in range(2):
            piece = dot(xn, dkv_s[m].reshape(width * tok, GW), 0, 0)
            if first:
                piece = piece + dw_acc[m]
            if first + width < n_ctx:
                dw_acc[m] = piece
            else:
                dw_ref[pl.ds((m + 1) * D, D)] = piece.astype(BF)
    dgain_ref[...] = dgain


def middle_body(
    att_ref, tok_ref, wo_ref, gain_ref, routes_ref, cot_ref,
    h1_ref, xn2_ref, gate_ref, disp_ref, packed_ref,
):
    tok = tok_ref.shape[0]
    att = jnp.concatenate([att_ref[i] for i in range(G)], axis=1)
    h1 = tok_ref[...].astype(F32) + dot(att, wo_ref[:, :D])
    h1_ref[...] = h1
    inv = lax.rsqrt(jnp.mean(h1 * h1, axis=-1, keepdims=True) + EPS)
    xn2 = (h1 * inv * gain_ref[...]).astype(BF)
    xn2_ref[...] = xn2
    logits = dot(xn2, wo_ref[:, D : D + E])
    experts = lax.broadcasted_iota(jnp.int32, (tok, E), 1)
    route = [routes_ref[:, k : k + 1] for k in range(2)]
    member = [(route[k] == experts).astype(F32) for k in range(2)]
    chosen = [jnp.sum(logits * member[k], axis=-1, keepdims=True) for k in range(2)]
    top = jnp.maximum(chosen[0], chosen[1])
    ex = [jnp.exp(chosen[k] - top) for k in range(2)]
    gate = [ex[k] / (ex[0] + ex[1]) for k in range(2)]
    gate_ref[...] = jnp.concatenate(gate, axis=1)
    before = lax.broadcasted_iota(jnp.int32, (tok, tok), 0) > lax.broadcasted_iota(jnp.int32, (tok, tok), 1)
    counts = dot(before.astype(F32).astype(BF), (member[0] + member[1]).astype(BF))
    slots = lax.broadcasted_iota(jnp.int32, (tok, E * CAP), 1)
    disp = []
    for k in range(2):
        slot = jnp.sum(counts * member[k], axis=-1, keepdims=True).astype(jnp.int32)
        disp.append((route[k] * CAP + slot == slots).astype(F32).astype(BF))
        disp_ref[k] = disp[k]
    cot = cot_ref[...].astype(F32)
    packed_ref[:, :D] = dot(disp[0] + disp[1], xn2, 0, 0).astype(BF)
    rows = dot(disp[0], (gate[0] * cot).astype(BF), 0, 0) + dot(disp[1], (gate[1] * cot).astype(BF), 0, 0)
    packed_ref[:, D:] = rows.astype(BF)


def expert_body(x_ref, win_ref, wout_ref, part_ref, dwin_ref, dwout_ref):
    x, dy = x_ref[0, :, :D], x_ref[0, :, D:]
    win, wout = win_ref[0], wout_ref[0]
    pre = dot(x, win)
    inner = GELU_C * (pre + 0.044715 * pre * pre * pre)
    th = jnp.tanh(inner)
    hid = (0.5 * pre * (1.0 + th)).astype(BF)
    slope = 0.5 * (1.0 + th) + 0.5 * pre * (1.0 - th * th) * GELU_C * (1.0 + 3.0 * 0.044715 * pre * pre)
    dpre = (dot(dy, wout, 1, 1) * slope).astype(BF)
    part_ref[0, :, :D] = dot(hid, wout).astype(BF)
    part_ref[0, :, D:] = dot(dpre, win, 1, 1).astype(BF)
    dwin_ref[0] = dot(x, dpre, 0, 0)
    dwout_ref[0] = dot(hid, dy, 0, 0)


def experts(x, w_in, w_out):
    n, rows = x.shape[:2]
    ff = w_in.shape[2]
    spec = lambda *s: pl.BlockSpec((1,) + s, lambda i: (i, 0, 0))
    return pl.pallas_call(
        expert_body,
        grid=(n,),
        in_specs=[spec(rows, 2 * D), spec(D, ff), spec(ff, D)],
        out_specs=[spec(rows, 2 * D), spec(D, ff), spec(ff, D)],
        out_shape=[sds(x.shape, BF), sds((n, D, ff)), sds((n, ff, D))],
        compiler_params=pltpu.CompilerParams(vmem_limit_bytes=LIMIT),
        name="experts",
    )(x, w_in, w_out)


def after_body(
    ret_ref, disp_ref, h1_ref, xn2_ref, gate_ref, cot_ref, routes_ref, wo_ref, att_ref, gain_ref,
    mixed_ref, dh1_ref, dat_ref, dout_ref, drouter_ref, dgain_ref,
):
    tok = h1_ref.shape[0]
    both = [dot(disp_ref[k], ret_ref[...]) for k in range(2)]
    gate = [gate_ref[:, k : k + 1] for k in range(2)]
    h1 = h1_ref[...]
    dy = cot_ref[...].astype(F32)
    picked = [both[k][:, :D] for k in range(2)]
    mixed_ref[...] = (h1 + (gate[0] * picked[0] + gate[1] * picked[1])).astype(BF)
    dgate = [jnp.sum(dy * picked[k], axis=-1, keepdims=True) for k in range(2)]
    mean = gate[0] * dgate[0] + gate[1] * dgate[1]
    lanes = lax.broadcasted_iota(jnp.int32, (tok, E), 1)
    dlog = jnp.zeros((tok, E), F32)
    for k in range(2):
        dlog = dlog + jnp.where(routes_ref[:, k : k + 1] == lanes, gate[k] * (dgate[k] - mean), 0.0)
    dlog = dlog.astype(BF)
    xn2 = xn2_ref[...]
    dxn = both[0][:, D:] + both[1][:, D:] + dot(dlog, wo_ref[:, D : D + E], 1, 1)
    drouter_ref[...] = dot(xn2, dlog, 0, 0).astype(BF)
    inv = lax.rsqrt(jnp.mean(h1 * h1, axis=-1, keepdims=True) + EPS)
    hat = h1 * inv
    dgain_ref[...] = jnp.sum((dxn * hat).reshape(tok // 8, 8, D), axis=0)
    cen = dxn * gain_ref[...]
    dh1 = dy + inv * (cen - hat * jnp.mean(cen * hat, axis=-1, keepdims=True))
    dh1_ref[...] = dh1
    dh1b = dh1.astype(BF)
    att = jnp.concatenate([att_ref[i] for i in range(G)], axis=1)
    dout_ref[...] = dot(att, dh1b, 0, 0).astype(BF)
    dat = dot(dh1b, wo_ref[:, :D], 1, 1).astype(BF)
    for i in range(G):
        dat_ref[i] = dat[:, i * GW : (i + 1) * GW]


def shards(tokens, routes, cotangent, gains, rel_bias, attn_qkv, attn_out, router, w_in, w_out):
    tok = tokens.shape[1]
    n_ctx, nf = lax.axis_size("ctx"), lax.axis_size("fsdp")
    n_dev = n_ctx * nf
    R, X = n_ctx // G, nf // CORES
    seq = tok * n_ctx
    per_dev = w_in.shape[0]
    qr, orows = attn_qkv.shape[0], attn_out.shape[0]
    x2, cot, route2 = tokens.reshape(tok, D), cotangent.reshape(tok, D), routes.reshape(tok, 2)

    n_gain, n_bias = gains.size, rel_bias.size
    tile = jnp.concatenate([gains.reshape(-1), rel_bias]).astype(F32)
    tile = jnp.broadcast_to(jnp.pad(tile, (0, 128 - n_gain - n_bias)), (8, 128))
    xall, wall, oall, tails = gather(n_ctx, nf, x2, attn_qkv, attn_out, router, tile)
    wall = wall.reshape(n_dev * qr, GW)
    wo = oall.reshape(D, D + 2 * E)
    table = tails[:, 0, n_gain : n_gain + n_bias].reshape(H * NB)

    part = functools.partial
    width = math.gcd(n_ctx, 8)
    tiles_shape = (HG, n_ctx + R - 1, tok, tok)
    att, lse, q, k, v, tiles, gain1, gain2 = call(
        part(attend_body, n_ctx, nf),
        [sds((G, tok, GW), BF), sds((G, tok, 128)), sds((HG, G * tok, DH), BF)] + [sds((HG, seq, DH), BF)] * 2
        + [sds(tiles_shape), sds((1, D)), sds((1, D))],
        [xall, wall, tails, table],
        in_specs=[VM, VM, VM, SM],
        name="attend",
    )
    att_in = swap(n_ctx, nf, att, 2, "swap_att")[0]
    h1, xn2, gate, disp, packed = call(
        middle_body,
        [sds((tok, D)), sds((tok, D), BF), sds((tok, 2)), sds((2, tok, E * CAP), BF), sds((E * CAP, 2 * D), BF)],
        [att_in, x2, wo, gain2, route2, cot],
        name="middle",
    )
    recv = dispatch(n_ctx, nf, packed.reshape(n_ctx, per_dev, CAP, 2 * D))
    rows = nf * n_ctx * CAP
    part_rows, d_w_in, d_w_out = experts(recv.reshape(per_dev, rows, 2 * D), w_in, w_out)
    ret = combine(n_ctx, nf, part_rows.reshape(per_dev, nf, n_ctx, CAP, 2 * D))
    mixed, dh1, dat, d_out, d_router, dgain2 = call(
        after_body,
        [sds((tok, D), BF), sds((tok, D)), sds((G, tok, GW), BF), sds((D, D), BF), sds((D, E), BF), sds((8, D))],
        [ret.reshape(E * CAP, 2 * D), disp, h1, xn2, gate, cot, route2, wo, att_in, gain2],
        name="after",
    )
    lead = (G, R, X, CORES)
    more = (d_out.reshape(lead + (orows, D)), d_router.reshape(lead + router.shape))
    do, d_out_mine, d_router_mine = swap(n_ctx, nf, dat, 5, "swap_dat", more)
    dx, dw, dgain1, dtab = call(
        part(attend_back_body, n_ctx, nf),
        [sds((n_ctx, tok, D), BF), sds((3 * D, GW), BF), sds((8, D)), sds((HG, NB, 8, tok))],
        [xall, wall, gain1, tiles, lse, q, k, v, att, do],
        scratch=[
            pltpu.VMEM(tiles_shape, F32), pltpu.VMEM((HG, seq, DH), F32), pltpu.VMEM((HG, seq, DH), F32),
            pltpu.VMEM((width, tok, D), BF), pltpu.VMEM((G, tok, GW), BF), pltpu.VMEM((2, width, tok, GW), BF),
            pltpu.VMEM((2, D, GW) if width < n_ctx else (2, 8, GW), F32),
        ],
        name="attend_back",
        limit=LIMIT if width == n_ctx else 61 * 1024 * 1024,
    )
    dtab = jnp.sum(dtab, axis=(2, 3)).reshape(1, HG * NB)
    own_group = jnp.arange(G)[:, None] == lax.axis_index("ctx") // R
    dtab = jnp.where(own_group, dtab, 0.0).reshape(n_dev, n_bias)
    dgains = jnp.stack([jnp.sum(dgain1, axis=0), jnp.sum(dgain2, axis=0)])
    dgains = dgains.reshape(2, n_dev, -1).transpose(1, 0, 2).reshape(n_dev, n_gain)
    d_tail = jnp.pad(jnp.concatenate([dgains, dtab], axis=1), ((0, 0), (0, 128 - n_gain - n_bias)))
    d_tail = jnp.broadcast_to(d_tail[:, None, :], (n_dev, 8, 128)).reshape(lead + (8, 128))
    d_tokens, d_qkv, tail_mine = reduce_all(n_ctx, nf, dx, dw.reshape(lead + (qr, GW)), d_tail, x2, gain1, dh1)
    return (
        mixed.reshape(1, tok, D),
        d_tokens.reshape(1, tok, D),
        tail_mine[0, :n_gain].reshape(gains.shape),
        tail_mine[0, n_gain : n_gain + n_bias],
        d_qkv,
        d_out_mine,
        d_router_mine,
        d_w_in,
        d_w_out,
    )


def solution(mesh):
    return jax.shard_map(
        shards,
        mesh=mesh,
        in_specs=(
            P("fsdp", "ctx", None),
            P("fsdp", "ctx", None),
            P("fsdp", "ctx", None),
            P(None, ("ctx", "fsdp")),
            P(("ctx", "fsdp")),
            P(("ctx", "fsdp"), None),
            P(("ctx", "fsdp"), None),
            P(("ctx", "fsdp"), None),
            P("ctx", None, "fsdp"),
            P("ctx", "fsdp", None),
        ),
        out_specs=(
            P("fsdp", "ctx", None),
            P("fsdp", "ctx", None),
            P(None, ("ctx", "fsdp")),
            P(("ctx", "fsdp")),
            P(("ctx", "fsdp"), None),
            P(("ctx", "fsdp"), None),
            P(("ctx", "fsdp"), None),
            P("ctx", None, "fsdp"),
            P("ctx", "fsdp", None),
        ),
        check_vma=False,
    )
```

```python
import functools
import math

import jax
import jax.numpy as jnp
from jax import lax
from jax.experimental import pallas as pl
from jax.experimental.pallas import tpu as pltpu
from jax.sharding import PartitionSpec as P

D = 768
H = 12
DH = 64
E = 64
NB = 32
CAP = 8
G = 4
HG = H // G
GW = HG * DH
CORES = 2

EPS = 1e-06
EDGES = (16, 23, 32, 45, 64, 91, 128, 181, 256, 362, 512, 724, 1024, 1448, 2048, 2896)
STARTS = tuple(range(16)) + EDGES
GELU_C = 0.7978845608028654
NEG = -1e30
MESH = pl.DeviceIdType.MESH
F32 = jnp.float32
BF = jnp.bfloat16
VM = pl.BlockSpec(memory_space=pltpu.VMEM)
HB = pl.BlockSpec(memory_space=pl.ANY)
SM = pl.BlockSpec(memory_space=pltpu.SMEM)
WINDOW = 2
LIMIT = 56 * 1024 * 1024


def dot(a, b, ca=1, cb=0):
    return lax.dot_general(a, b, (((ca,), (cb,)), ((), ())), preferred_element_type=F32)


def call(body, outs, ins, out_specs=None, in_specs=None, scratch=(), cid=None, name=None, cost=None, limit=LIMIT, **kw):
    params = dict(vmem_limit_bytes=limit)
    if cid is not None:
        params.update(collective_id=cid, has_side_effects=True)
    return pl.pallas_call(
        body,
        out_shape=outs,
        in_specs=in_specs or [VM] * len(ins),
        out_specs=out_specs or [VM] * len(outs),
        scratch_shapes=list(scratch),
        compiler_params=pltpu.CompilerParams(**params),
        name=name,
        cost_estimate=cost,
        **kw,
    )(*ins)


def sds(shape, kind=F32):
    return jax.ShapeDtypeStruct(shape, kind)


class Place:
    def __init__(self, n_ctx, nf):
        self.n_ctx, self.nf = n_ctx, nf
        self.R, self.X = n_ctx // G, nf // CORES
        self.c, self.f = lax.axis_index("ctx"), lax.axis_index("fsdp")
        self.g, self.r = lax.div(self.c, self.R), lax.rem(self.c, self.R)
        self.x, self.k = lax.div(self.f, CORES), lax.rem(self.f, CORES)

    def up(self, v, d, n):
        return lax.rem(v + d, n)

    def ctx(self, dg, dr):
        return self.up(self.g, dg % G, G) * self.R + self.up(self.r, dr % self.R, self.R)

    def fs(self, dx, dk):
        return self.up(self.x, dx % self.X, self.X) * CORES + self.up(self.k, dk % CORES, CORES)

    def dev(self, dg, dr, dx, dk):
        return (self.ctx(dg, dr), self.fs(dx, dk))


def greet(targets):
    bar = pltpu.get_barrier_semaphore()
    for t in targets:
        pl.semaphore_signal(bar, inc=1, device_id=t, device_id_type=MESH)
    pl.semaphore_wait(bar, len(targets))


def mirror(c, d, n):
    out, bit = 0, 1
    while bit < n:
        out = out + lax.rem(lax.div(c, bit) + (d // bit) % 2, 2) * bit
        bit *= 2
    return out


def mixed_order(n):
    far, near = list(range(n // 2, n)), list(range(1, n // 2))
    out = []
    while far or near:
        if far:
            out.append(far.pop(0))
        if near:
            out.append(near.pop(0))
    return out


class Sends:
    def __init__(self):
        self.made = []

    def __call__(self, src, dst, ss, rs, dev):
        cp = rcopy(src, dst, ss, rs, dev)
        cp.start()
        self.made.append(cp)
        return cp

    def finish(self):
        for cp in self.made:
            cp.wait_send()


def got(at, s, r, dev):
    rcopy(at, at, s, r, dev).wait_recv()


class Scatter:
    COUNT = 11

    @staticmethod
    def scratch(G_, R, X, blk, kind):
        sem = lambda *n: pltpu.SemaphoreType.DMA(n)
        vm = lambda *n: pltpu.VMEM(n + blk, kind)
        return [vm(G_, R, X), vm(G_, R, X), vm(R * X, G_), vm(G_), vm(G_), sem(1), sem(1), sem(R * X), sem(R * X), sem(G_), sem(G_)]

    def __init__(self, p, send, src, refs):
        self.p, self.send, self.src = p, send, src
        self.cin, self.s1, self.qin, self.s2, self.win = refs[:5]
        self.c1, self.e1, self.c2, self.e2, self.c3, self.e3 = refs[5:]
        self.quad = [(er, ex) for er in range(p.R) for ex in range(p.X)]

    def over_cores(self):
        p = self.p
        self.send(self.src.at[:, :, :, 1 - p.k], self.cin, self.c1.at[0], self.e1.at[0], p.dev(0, 0, 0, 1))

    def over_quad(self):
        p = self.p
        got(self.cin, self.c1.at[0], self.e1.at[0], p.dev(0, 0, 0, 1))
        self.s1[...] = (self.src[:, :, :, p.k].astype(F32) + self.cin[...].astype(F32)).astype(self.s1.dtype)
        for i, (er, ex) in enumerate(self.quad):
            if i:
                at = self.s1.at[:, p.up(p.r, er, p.R), p.up(p.x, ex, p.X)]
                self.send(at, self.qin.at[i], self.c2.at[i], self.e2.at[i], p.dev(0, er, ex, 0))

    def over_groups(self):
        p = self.p
        total = self.s1[:, p.r, p.x].astype(F32)
        for i, (er, ex) in enumerate(self.quad):
            if i:
                got(self.qin.at[i], self.c2.at[i], self.e2.at[i], p.dev(0, -er, -ex, 0))
                total = total + self.qin[i].astype(F32)
        self.s2[...] = total.astype(self.s2.dtype)
        self.win[p.g] = self.s2[p.g]
        for dg in (2, 1, 3):
            self.send(self.s2.at[p.up(p.g, dg, G)], self.win.at[p.g], self.c3.at[dg], self.e3.at[dg], p.dev(dg, 0, 0, 0))

    def pieces(self):
        p = self.p
        for dg in (1, 3, 2):
            got(self.win.at[p.up(p.g, G - dg, G)], self.c3.at[dg], self.e3.at[dg], p.dev(-dg, 0, 0, 0))
        return [self.win[i].astype(F32) for i in range(G)]


def rcopy(src, dst, ss, rs, dev):
    return pltpu.make_async_remote_copy(
        src_ref=src, dst_ref=dst, send_sem=ss, recv_sem=rs, device_id=dev, device_id_type=MESH
    )


class Gather:
    COUNT = 8

    @staticmethod
    def scratch(R, X):
        sem = lambda *n: pltpu.SemaphoreType.DMA(n)
        return [sem(G)] * 2 + [sem(R)] * 2 + [sem(X)] * 2 + [sem(1)] * 2

    def __init__(self, p, send, piece, out, refs):
        self.p, self.send, self.piece, self.out = p, send, piece, out
        self.a, self.b = refs[0::2], refs[1::2]
        self.mine = out.at[p.g, p.r, p.x, p.k]

    def over_groups(self):
        p = self.p
        for d in (2, 1, 3):
            self.send(self.piece(d), self.mine, self.a[0].at[d], self.b[0].at[d], p.dev(d, 0, 0, 0))

    def over_rows(self):
        p = self.p
        for d in (1, 3, 2):
            at = self.out.at[p.up(p.g, G - d, G), p.r, p.x, p.k]
            got(at, self.a[0].at[d], self.b[0].at[d], p.dev(-d, 0, 0, 0))
        at = self.out.at[:, p.r, p.x, p.k]
        for er in range(1, p.R):
            self.send(at, at, self.a[1].at[er], self.b[1].at[er], p.dev(0, er, 0, 0))

    def over_x(self):
        p = self.p
        for er in range(1, p.R):
            at = self.out.at[:, p.up(p.r, p.R - er, p.R), p.x, p.k]
            got(at, self.a[1].at[er], self.b[1].at[er], p.dev(0, -er, 0, 0))
        at = self.out.at[:, :, p.x, p.k]
        for ex in range(1, p.X):
            self.send(at, at, self.a[2].at[ex], self.b[2].at[ex], p.dev(0, 0, ex, 0))

    def over_cores(self):
        p = self.p
        for ex in range(1, p.X):
            at = self.out.at[:, :, p.up(p.x, p.X - ex, p.X), p.k]
            got(at, self.a[2].at[ex], self.b[2].at[ex], p.dev(0, 0, -ex, 0))
        at = self.out.at[:, :, :, p.k]
        self.send(at, at, self.a[3].at[0], self.b[3].at[0], p.dev(0, 0, 0, 1))

    def settle(self):
        p = self.p
        got(self.out.at[:, :, :, 1 - p.k], self.a[3].at[0], self.b[3].at[0], p.dev(0, 0, 0, 1))


def gather_body(n_ctx, nf, tok, aq, ao, router, tile, xall, wall, oall, tiles, wq, wo, t1s, t1r, t2s, t2r, loc, *refs):
    p = Place(n_ctx, nf)
    R, X = p.R, p.X
    for i in range(G):
        wq[i] = aq[:, i * GW : (i + 1) * GW]
    wo[:, :D] = ao[...]
    wo[:, D : D + E] = router[...]
    wo[:, D + E :] = jnp.zeros((wo.shape[0], E), BF)
    greet(
        [p.dev(d, 0, 0, 0) for d in range(1, G)]
        + [p.dev(0, er, 0, 0) for er in range(1, R)]
        + [p.dev(0, 0, ex, 0) for ex in range(1, X)]
        + [p.dev(0, 0, 0, 1)]
    )
    send = Sends()
    n = Gather.COUNT
    items = [
        Gather(p, send, lambda d: tile, tiles, refs[:n]),
        Gather(p, send, lambda d: wq.at[p.up(p.g, d, G)], wall, refs[n : 2 * n]),
        Gather(p, send, lambda d: wo, oall, refs[2 * n :]),
    ]
    own = [
        pltpu.make_async_copy(src, dst, loc.at[i])
        for i, (src, dst) in enumerate([(tok, xall.at[p.c])] + [(it.piece(0), it.mine) for it in items])
    ]
    for cp in own:
        cp.start()
    sides = [(s, -1) for s in range(1, G)] + [(s, 1) for s in range(1, G)]

    def exists(at):
        return (p.g + at >= 0) & (p.g + at < G)

    def hop(s, way):
        at = way * (s - 1)
        src = tok if s == 1 else xall.at[p.ctx(at, 0)]
        i = s + (G if way > 0 else 0)
        return rcopy(src, xall.at[p.ctx(at, 0)], t1s.at[i], t1r.at[i], p.dev(-way, 0, 0, 0))

    def row(at, e):
        src = tok if at == 0 else xall.at[p.ctx(at, 0)]
        return rcopy(src, xall.at[p.ctx(at, 0)], t2s.at[at + G, e], t2r.at[at + G, e], p.dev(0, e, 0, 0))

    def step(s):
        for way in (-1, 1):

            @pl.when(exists(way * s))
            def _():
                i = s + (G if way > 0 else 0)
                got(xall.at[p.ctx(way * s, 0)], t1s.at[i], t1r.at[i], p.dev(way, 0, 0, 0))
                if s + 1 < G:

                    @pl.when(exists(-way))
                    def _():
                        hop(s + 1, way).start()

                for e in range(1, R):
                    row(way * s, e).start()

    for it in items[:2]:
        it.over_groups()
    for way in (-1, 1):

        @pl.when(exists(-way))
        def _():
            hop(1, way).start()

    for e in range(1, R):
        row(0, e).start()
    items[2].over_groups()
    for cp in own[1:]:
        cp.wait()
    items[0].over_rows()
    items[1].over_rows()
    step(1)
    items[2].over_rows()
    items[0].over_x()
    items[1].over_x()
    step(2)
    items[2].over_x()
    items[0].over_cores()
    items[1].over_cores()
    step(3)
    items[2].over_cores()
    for it in items:
        it.settle()
    for at in range(1 - G, G):

        @pl.when(exists(at))
        def _():
            for e in range(1, R):
                got(xall.at[p.ctx(at, -e)], t2s.at[at + G, e], t2r.at[at + G, e], p.dev(0, -e, 0, 0))
                row(at, e).wait_send()

    for s, way in sides:

        @pl.when(exists(-way) & exists(way * (s - 1)))
        def _():
            hop(s, way).wait_send()

    send.finish()
    own[0].wait()


def gather(n_ctx, nf, tok, aq, ao, router, tile):
    R, X = n_ctx // G, nf // CORES
    lead = (G, R, X, CORES)
    sem = lambda *s: pltpu.SemaphoreType.DMA(s)
    qr, rows = aq.shape[0], ao.shape[0]
    return call(
        functools.partial(gather_body, n_ctx, nf),
        [
            sds((n_ctx,) + tok.shape, BF),
            sds(lead + (qr, GW), BF),
            sds(lead + (rows, D + 2 * E), BF),
            sds(lead + tile.shape, tile.dtype),
        ],
        [tok, aq, ao, router, tile],
        out_specs=[HB] * 4,
        scratch=[pltpu.VMEM((G, qr, GW), BF), pltpu.VMEM((rows, D + 2 * E), BF)]
        + [sem(2 * G)] * 2
        + [sem(2 * G, R)] * 2
        + [sem(4)]
        + Gather.scratch(R, X) * 3,
        cid=1,
        name="gather",
    )


def swap_body(n_ctx, nf, extra, *refs):
    p = Place(n_ctx, nf)
    src, more = refs[0], refs[1 : 1 + extra]
    dst, sums = refs[1 + extra], refs[2 + extra : 2 + 2 * extra]
    ss, rs, loc = refs[2 + 2 * extra : 5 + 2 * extra]
    rest = refs[5 + 2 * extra :]
    quad = [(er, ex) for er in range(p.R) for ex in range(p.X)]
    near = [p.dev(0, er, ex, 0) for er, ex in quad[1:]] + [p.dev(0, 0, 0, 1)]
    greet([p.dev(d, 0, 0, 0) for d in range(1, G)] + (near if extra else []))
    own = pltpu.make_async_copy(src.at[p.g], dst.at[p.g], loc)
    own.start()
    send = Sends()
    n = Scatter.COUNT
    scatters = [Scatter(p, send, m, rest[i * n : (i + 1) * n]) for i, m in enumerate(more)]
    for d in (2, 1, 3):
        send(src.at[p.up(p.g, d, G)], dst.at[p.g], ss.at[d], rs.at[d], p.dev(d, 0, 0, 0))
    for sc in scatters:
        sc.over_cores()
    for sc in scatters:
        sc.over_quad()
    for sc in scatters:
        sc.over_groups()
    for d in (1, 3, 2):
        got(dst.at[p.up(p.g, G - d, G)], ss.at[d], rs.at[d], p.dev(-d, 0, 0, 0))
    for sc, out in zip(scatters, sums):
        w = sc.pieces()
        out[...] = (w[0] + w[1]) + (w[2] + w[3])
    send.finish()
    own.wait()


def swap(n_ctx, nf, src, cid, name, more=()):
    sem = pltpu.SemaphoreType.DMA
    scratch = [sem((G,)), sem((G,)), sem]
    for m in more:
        scratch += Scatter.scratch(G, n_ctx // G, nf // CORES, m.shape[4:], m.dtype)
    return call(
        functools.partial(swap_body, n_ctx, nf, len(more)),
        [sds(src.shape, src.dtype)] + [sds(m.shape[4:]) for m in more],
        [src, *more],
        scratch=scratch,
        cid=cid,
        name=name,
    )


def dispatch_body(n_ctx, nf, packed, recv, ss, rs, xs, xr, ks, kr, loc):
    p = Place(n_ctx, nf)
    X = p.X
    greet(
        [(p.up(p.c, d, n_ctx), p.f) for d in range(1, n_ctx)]
        + [p.dev(0, 0, dx, 0) for dx in range(1, X)]
        + [p.dev(0, 0, 0, 1)]
    )
    own = pltpu.make_async_copy(packed.at[p.c], recv.at[:, p.f, p.c], loc)
    own.start()
    send = Sends()
    order = mixed_order(n_ctx)
    first = []

    def away(d):
        cc = mirror(p.c, d, n_ctx)
        first.append(send(packed.at[cc], recv.at[:, p.f, p.c], ss.at[d], rs.at[d], (cc, p.f)))

    def spread(d):
        cc = mirror(p.c, d, n_ctx)
        at = recv.at[:, p.f, cc]
        if d:
            got(at, ss.at[d], rs.at[d], (cc, p.f))
        src = packed.at[p.c] if d == 0 else at
        for dx in range(1, X):
            send(src, at, xs.at[d, dx], xr.at[d, dx], p.dev(0, 0, dx, 0))
        send(src, at, ks.at[d, 0], kr.at[d, 0], p.dev(0, 0, 0, 1))

    def relay(d):
        cc = mirror(p.c, d, n_ctx)
        for dx in range(1, X):
            at = recv.at[:, p.fs(-dx, 0), cc]
            got(at, xs.at[d, dx], xr.at[d, dx], p.dev(0, 0, -dx, 0))
            send(at, at, ks.at[d, dx], kr.at[d, dx], p.dev(0, 0, 0, 1))

    for d in order[:WINDOW]:
        away(d)
    spread(0)
    for i, d in enumerate(order):
        spread(d)
        if i + WINDOW < len(order):
            away(order[i + WINDOW])
        if i:
            relay(order[i - 1] if i > 1 else 0)
        if i == 1:
            relay(order[0])
    for d in order[max(1, len(order) - 1) :]:
        relay(d)
    for d in range(n_ctx):
        cc = mirror(p.c, d, n_ctx)
        for dx in range(X):
            at = recv.at[:, p.fs(-dx, 1), cc]
            got(at, ks.at[d, dx], kr.at[d, dx], p.dev(0, 0, 0, 1))
    send.finish()
    own.wait()


def dispatch(n_ctx, nf, packed):
    per_dev, width = packed.shape[1], packed.shape[3]
    X = nf // CORES
    sem = lambda *s: pltpu.SemaphoreType.DMA(s)
    return call(
        functools.partial(dispatch_body, n_ctx, nf),
        [sds((per_dev, nf, n_ctx, CAP, width), BF)],
        [packed],
        in_specs=[HB],
        out_specs=[HB],
        scratch=[sem(n_ctx)] * 2 + [sem(n_ctx, X)] * 4 + [pltpu.SemaphoreType.DMA],
        cid=3,
        name="dispatch",
    )[0]


def combine_body(n_ctx, nf, part, out, kept, cin, xsum, xin, fin, ss, rs, xs, xr, ks, kr, ls):
    p = Place(n_ctx, nf)
    X = p.X
    greet(
        [(p.up(p.c, d, n_ctx), p.f) for d in range(1, n_ctx)]
        + [p.dev(0, 0, dx, 0) for dx in range(1, X)]
        + [p.dev(0, 0, 0, 1)]
    )
    send = Sends()
    order = mixed_order(n_ctx) + [0]

    def keep(d, dx):
        return pltpu.make_async_copy(part.at[:, p.fs(dx, 0), mirror(p.c, d, n_ctx)], kept.at[dx, d], ls.at[d, dx])

    for d in order:
        cc = mirror(p.c, d, n_ctx)
        for dx in [*range(1, X), 0]:
            send(part.at[:, p.fs(dx, 1), cc], cin.at[dx, d], ks.at[d, dx], kr.at[d, dx], p.dev(0, 0, 0, 1))
            keep(d, dx).start()

    def across(d):
        for dx in range(1, X):
            got(cin.at[dx, d], ks.at[d, dx], kr.at[d, dx], p.dev(0, 0, 0, 1))
            keep(d, dx).wait()
            xsum[dx, d] = (kept[dx, d].astype(F32) + cin[dx, d].astype(F32)).astype(BF)
            send(xsum.at[dx, d], xin.at[dx, d], xs.at[d, dx], xr.at[d, dx], p.dev(0, 0, dx, 0))

    for d in order[:2]:
        across(d)
    for i, d in enumerate(order):
        if i + 2 < len(order):
            across(order[i + 2])
        cc = mirror(p.c, d, n_ctx)
        got(cin.at[0, d], ks.at[d, 0], kr.at[d, 0], p.dev(0, 0, 0, 1))
        keep(d, 0).wait()
        total = kept[0, d].astype(F32) + cin[0, d].astype(F32)
        for dx in range(1, X):
            got(xin.at[dx, d], xs.at[d, dx], xr.at[d, dx], p.dev(0, 0, -dx, 0))
            total = total + xin[dx, d].astype(F32)
        if d:
            fin[d] = total.astype(BF)
            send(fin.at[d], out.at[p.c], ss.at[d], rs.at[d], (cc, p.f))
        else:
            out[p.c] = total.astype(BF)
    for d in order[:-1]:
        cc = mirror(p.c, d, n_ctx)
        got(out.at[cc], ss.at[d], rs.at[d], (cc, p.f))
    send.finish()


def combine(n_ctx, nf, part):
    per_dev, width = part.shape[0], part.shape[-1]
    X = nf // CORES
    sem = lambda *s: pltpu.SemaphoreType.DMA(s)
    blk = (per_dev, CAP, width)
    return call(
        functools.partial(combine_body, n_ctx, nf),
        [sds((n_ctx,) + blk, BF)],
        [part],
        in_specs=[HB],
        scratch=[pltpu.VMEM((X, n_ctx) + blk, BF)] * 4
        + [pltpu.VMEM((n_ctx,) + blk, BF)]
        + [sem(n_ctx)] * 2
        + [sem(n_ctx, X)] * 5,
        cid=4,
        name="combine",
    )[0]


def reduce_body(n_ctx, nf, dx_ref, dw_ref, tail_ref, tok_ref, gain_ref, dtok_ref, dqkv_ref, dtail_ref, *refs):
    p = Place(n_ctx, nf)
    R, X = p.R, p.X
    rin, gsum, gin, a1, b1, a2, b2 = refs[:7]
    n = Scatter.COUNT
    quad = [(er, ex) for er in range(R) for ex in range(X)]
    greet(
        [p.dev(d, 0, 0, 0) for d in range(1, G)]
        + [p.dev(0, er, ex, 0) for er, ex in quad[1:]]
        + [p.dev(0, 0, 0, 1)]
    )
    send = Sends()
    wsum = Scatter(p, send, dw_ref, refs[7 : 7 + n])
    tsum = Scatter(p, send, tail_ref, refs[7 + n :])
    tsum.over_cores()
    wsum.over_cores()
    far = (2, 1, 3, 0)

    def near(dg):
        for er in range(1, R):
            send(dx_ref.at[p.ctx(dg, er)], rin.at[er, dg], a1.at[dg, er], b1.at[dg, er], p.dev(0, er, 0, 0))

    near(far[0])
    near(far[1])
    tsum.over_quad()
    wsum.over_quad()
    near(far[2])
    near(far[3])
    for dg in far:
        total = dx_ref[p.ctx(dg, 0)].astype(F32)
        for er in range(1, R):
            got(rin.at[er, dg], a1.at[dg, er], b1.at[dg, er], p.dev(0, -er, 0, 0))
            total = total + rin[er, dg].astype(F32)
        gsum[dg] = total.astype(BF)
        if dg:
            send(gsum.at[dg], gin.at[dg], a2.at[dg], b2.at[dg], p.dev(dg, 0, 0, 0))
        if dg == far[1]:
            tsum.over_groups()
            wsum.over_groups()
    grad = gsum[0].astype(F32)
    for dg in (1, 3, 2):
        got(gin.at[dg], a2.at[dg], b2.at[dg], p.dev(-dg, 0, 0, 0))
        grad = grad + gin[dg].astype(F32)
    rows = tok_ref[...].astype(F32)
    inv = lax.rsqrt(jnp.mean(rows * rows, axis=-1, keepdims=True) + EPS)
    hat = rows * inv
    grad = grad * gain_ref[...]
    dtok_ref[...] = inv * (grad - hat * jnp.mean(grad * hat, axis=-1, keepdims=True))
    w = tsum.pieces()
    dtail_ref[...] = (w[0] + w[1]) + (w[2] + w[3])
    dqkv_ref[...] = jnp.concatenate(wsum.pieces(), axis=1)
    send.finish()


def reduce_all(n_ctx, nf, dx, dw, tail, tok, gain):
    R, X = n_ctx // G, nf // CORES
    tb = dx.shape[1:]
    sem = lambda *n: pltpu.SemaphoreType.DMA(n)
    vm = lambda *n: pltpu.VMEM(n + tb, BF)
    return call(
        functools.partial(reduce_body, n_ctx, nf),
        [sds(tb), sds((dw.shape[4], D)), sds(tail.shape[4:])],
        [dx, dw, tail, tok, gain],
        scratch=[vm(R, G), vm(G), vm(G), sem(G, R), sem(G, R), sem(G), sem(G)]
        + Scatter.scratch(G, R, X, dw.shape[4:], BF)
        + Scatter.scratch(G, R, X, tail.shape[4:], F32),
        cid=6,
        name="reduce",
    )


def bias_tiles(tab_ref, tiles, g, R, nd):
    tok = tiles.shape[2]
    lane = lax.broadcasted_iota(jnp.int32, (8, 2 * tok), 1)
    apart = lax.broadcasted_iota(jnp.int32, (tok, tok), 0) - lax.broadcasted_iota(jnp.int32, (tok, tok), 1)
    for i in range(nd):
        d = i - (R - 1)
        least, most = (d - 1) * tok + 1, (d + 1) * tok - 1
        used = [b for b in range(NB) if STARTS[b] <= most and (b + 1 == NB or STARTS[b + 1] > least)]
        for hh in range(HG):
            base = (g * HG + hh) * NB
            few = len(used) <= 8
            off = apart + d * tok if few else d * tok + tok - lane
            first = tab_ref[base + used[0]] if used and least >= STARTS[used[0]] else NEG
            val = jnp.full(off.shape, first, F32)
            for b in used:
                if least < STARTS[b]:
                    val = jnp.where(off >= STARTS[b], tab_ref[base + b], val)
            if not few:
                wide = jnp.concatenate([val] * (tok // 8), axis=0)
                val = pltpu.roll(wide, tok, 1, stride=1, stride_axis=0)[:, :tok]
            tiles[hh, i] = val


def normed(x_ref, b):
    rows = x_ref[b].astype(F32)
    inv = lax.rsqrt(jnp.mean(rows * rows, axis=-1, keepdims=True) + EPS)
    return rows * inv


def scores(q, keys, tiles, hh, gq, r, R, n):
    s = dot(q, keys, 1, 1) * (1.0 / math.sqrt(DH))
    bias = jnp.concatenate([tiles[hh, gq * R + r - kb + R - 1] for kb in range(n)], axis=1)
    return s + bias


def attend_body(n_ctx, nf, x_ref, w_ref, tails_ref, tab_ref, att_ref, lse_ref, q_ref, k_ref, v_ref, tiles, gain1_ref, gain2_ref):
    p = Place(n_ctx, nf)
    R, tok = p.R, x_ref.shape[1]
    gw = D // (n_ctx * nf)
    for i in range(n_ctx * nf):
        gain1_ref[:, i * gw : (i + 1) * gw] = tails_ref[i, 0:1, :gw]
        gain2_ref[:, i * gw : (i + 1) * gw] = tails_ref[i, 0:1, gw : 2 * gw]
    gain = gain1_ref[...]
    bias_tiles(tab_ref, tiles, p.g, R, n_ctx + R - 1)

    def block(b, _):
        xn = (normed(x_ref, b) * gain).astype(BF)
        at = pl.ds(pl.multiple_of(b * tok, tok), tok)
        for m, ref in ((1, k_ref), (2, v_ref)):
            y = dot(xn, w_ref[pl.ds(m * D, D)]).astype(BF)
            for hh in range(HG):
                ref[hh, at] = y[:, hh * DH : (hh + 1) * DH]
        return 0

    lax.fori_loop(0, n_ctx, block, 0)
    for gq in range(G):
        xn = (normed(x_ref, gq * R + p.r) * gain).astype(BF)
        y = dot(xn, w_ref[pl.ds(0, D)]).astype(BF)
        for hh in range(HG):
            q_ref[hh, pl.ds(gq * tok, tok)] = y[:, hh * DH : (hh + 1) * DH]
    for gq in range(G):
        n = (gq + 1) * R
        outs = []
        for hh in range(HG):
            s = scores(q_ref[hh, pl.ds(gq * tok, tok)], k_ref[hh, pl.ds(0, n * tok)], tiles, hh, gq, p.r, R, n)
            top = jnp.max(s, axis=-1, keepdims=True)
            w = jnp.exp(s - top)
            total = jnp.sum(w, axis=-1, keepdims=True)
            acc = dot(w.astype(BF), v_ref[hh, pl.ds(0, n * tok)])
            outs.append((acc / total).astype(BF))
            lse_ref[gq, :, hh : hh + 1] = top + jnp.log(total)
        att_ref[gq] = jnp.concatenate(outs, axis=1)


def attend_back_body(
    n_ctx, nf, x_ref, w_ref, gain_ref, tiles, lse_ref, q_ref, k_ref, v_ref, att_ref, do_ref,
    dx_ref, dw_ref, dgain_ref, dtab_ref, dtiles, dk_acc, dv_acc, xn_s, dq_s, dkv_s, dw_acc,
):
    p = Place(n_ctx, nf)
    R, tok = p.R, x_ref.shape[1]
    scale = 1.0 / math.sqrt(DH)
    dtiles[...] = jnp.zeros_like(dtiles)
    dk_acc[...] = jnp.zeros_like(dk_acc)
    dv_acc[...] = jnp.zeros_like(dv_acc)
    for gq in range(G):
        n = (gq + 1) * R
        rows = pl.ds(gq * tok, tok)
        keys = pl.ds(0, n * tok)
        do_all = do_ref[gq]
        prod = do_all.astype(F32) * att_ref[gq].astype(F32)
        dqs = []
        for hh in range(HG):
            q, kk, vv = q_ref[hh, rows], k_ref[hh, keys], v_ref[hh, keys]
            do = do_all[:, hh * DH : (hh + 1) * DH]
            delta = jnp.sum(prod[:, hh * DH : (hh + 1) * DH], axis=-1, keepdims=True)
            s = scores(q, kk, tiles, hh, gq, p.r, R, n)
            w = jnp.exp(s - lse_ref[gq, :, hh : hh + 1])
            ds = w * (dot(do, vv, 1, 1) - delta)
            for kb in range(n):
                at = gq * R + p.r - kb + R - 1
                dtiles[hh, at] = dtiles[hh, at] + ds[:, kb * tok : (kb + 1) * tok]
            dsb = ds.astype(BF)
            dqs.append((dot(dsb, kk) * scale).astype(BF))
            dk_acc[hh, keys] = dk_acc[hh, keys] + dot(dsb, q, 0, 0)
            dv_acc[hh, keys] = dv_acc[hh, keys] + dot(w.astype(BF), do, 0, 0)
        dq_s[gq] = jnp.concatenate(dqs, axis=1)
    for hh in range(HG):
        sums = [None] * NB
        off0 = lax.broadcasted_iota(jnp.int32, (tok, tok), 0) - lax.broadcasted_iota(jnp.int32, (tok, tok), 1)
        for d in range(n_ctx):
            t = dtiles[hh, d + R - 1]
            off = off0 + d * tok
            for b in range(NB):
                low = STARTS[b]
                high = STARTS[b + 1] if b + 1 < NB else 1 << 30
                if high <= d * tok - tok + 1 or low > d * tok + tok - 1:
                    continue
                part = jnp.where((off >= low) & (off < high), t, 0.0)
                part = jnp.sum(part.reshape(tok // 8, 8, tok), axis=0)
                sums[b] = part if sums[b] is None else sums[b] + part
        for b in range(NB):
            dtab_ref[hh, b] = jnp.zeros((8, tok), F32) if sums[b] is None else sums[b]
    gain = gain_ref[...]
    xn_q = jnp.concatenate([(normed(x_ref, gq * R + p.r) * gain).astype(BF) for gq in range(G)], axis=0)
    dw_ref[pl.ds(0, D)] = dot(xn_q, dq_s[...].reshape(G * tok, GW), 0, 0).astype(BF)
    width = xn_s.shape[0]
    dgain = jnp.zeros((8, D), F32)
    for first in range(0, n_ctx, width):

        def block(i, dg):
            b = first + i
            hat = normed(x_ref, b)
            at = pl.ds(pl.multiple_of(b * tok, tok), tok)
            xn_s[i] = (hat * gain).astype(BF)
            dk = jnp.concatenate([(dk_acc[hh, at] * scale).astype(BF) for hh in range(HG)], axis=1)
            dv = jnp.concatenate([dv_acc[hh, at].astype(BF) for hh in range(HG)], axis=1)
            dkv_s[0, i] = dk
            dkv_s[1, i] = dv
            mine = lax.rem(b, R) == p.r
            dq = jnp.where(mine, dq_s[lax.div(b, R)], jnp.zeros((tok, GW), BF))
            dxn = (
                dot(dq, w_ref[pl.ds(0, D)], 1, 1)
                + dot(dk, w_ref[pl.ds(D, D)], 1, 1)
                + dot(dv, w_ref[pl.ds(2 * D, D)], 1, 1)
            )
            dx_ref[b] = dxn.astype(BF)
            return dg + jnp.sum((dxn * hat).reshape(tok // 8, 8, D), axis=0)

        dgain = lax.fori_loop(0, width, block, dgain)
        xn = xn_s[...].reshape(width * tok, D)
        for m in range(2):
            piece = dot(xn, dkv_s[m].reshape(width * tok, GW), 0, 0)
            if first:
                piece = piece + dw_acc[m]
            if first + width < n_ctx:
                dw_acc[m] = piece
            else:
                dw_ref[pl.ds((m + 1) * D, D)] = piece.astype(BF)
    dgain_ref[...] = dgain


def middle_body(
    att_ref, tok_ref, wo_ref, gain_ref, routes_ref, cot_ref,
    h1_ref, xn2_ref, gate_ref, disp_ref, packed_ref,
):
    tok = tok_ref.shape[0]
    att = jnp.concatenate([att_ref[i] for i in range(G)], axis=1)
    h1 = tok_ref[...].astype(F32) + dot(att, wo_ref[:, :D])
    h1_ref[...] = h1
    inv = lax.rsqrt(jnp.mean(h1 * h1, axis=-1, keepdims=True) + EPS)
    xn2 = (h1 * inv * gain_ref[...]).astype(BF)
    xn2_ref[...] = xn2
    logits = dot(xn2, wo_ref[:, D : D + E])
    experts = lax.broadcasted_iota(jnp.int32, (tok, E), 1)
    route = [routes_ref[:, k : k + 1] for k in range(2)]
    member = [(route[k] == experts).astype(F32) for k in range(2)]
    chosen = [jnp.sum(logits * member[k], axis=-1, keepdims=True) for k in range(2)]
    top = jnp.maximum(chosen[0], chosen[1])
    ex = [jnp.exp(chosen[k] - top) for k in range(2)]
    gate = [ex[k] / (ex[0] + ex[1]) for k in range(2)]
    gate_ref[...] = jnp.concatenate(gate, axis=1)
    before = lax.broadcasted_iota(jnp.int32, (tok, tok), 0) > lax.broadcasted_iota(jnp.int32, (tok, tok), 1)
    counts = dot(before.astype(F32).astype(BF), (member[0] + member[1]).astype(BF))
    slots = lax.broadcasted_iota(jnp.int32, (tok, E * CAP), 1)
    disp = []
    for k in range(2):
        slot = jnp.sum(counts * member[k], axis=-1, keepdims=True).astype(jnp.int32)
        disp.append((route[k] * CAP + slot == slots).astype(F32).astype(BF))
        disp_ref[k] = disp[k]
    cot = cot_ref[...].astype(F32)
    packed_ref[:, :D] = dot(disp[0] + disp[1], xn2, 0, 0).astype(BF)
    rows = dot(disp[0], (gate[0] * cot).astype(BF), 0, 0) + dot(disp[1], (gate[1] * cot).astype(BF), 0, 0)
    packed_ref[:, D:] = rows.astype(BF)


def expert_body(x_ref, win_ref, wout_ref, part_ref, dwin_ref, dwout_ref):
    x, dy = x_ref[0, :, :D], x_ref[0, :, D:]
    win, wout = win_ref[0], wout_ref[0]
    pre = dot(x, win)
    inner = GELU_C * (pre + 0.044715 * pre * pre * pre)
    th = jnp.tanh(inner)
    hid = (0.5 * pre * (1.0 + th)).astype(BF)
    slope = 0.5 * (1.0 + th) + 0.5 * pre * (1.0 - th * th) * GELU_C * (1.0 + 3.0 * 0.044715 * pre * pre)
    dpre = (dot(dy, wout, 1, 1) * slope).astype(BF)
    part_ref[0, :, :D] = dot(hid, wout).astype(BF)
    part_ref[0, :, D:] = dot(dpre, win, 1, 1).astype(BF)
    dwin_ref[0] = dot(x, dpre, 0, 0)
    dwout_ref[0] = dot(hid, dy, 0, 0)


def experts(x, w_in, w_out):
    n, rows = x.shape[:2]
    ff = w_in.shape[2]
    spec = lambda *s: pl.BlockSpec((1,) + s, lambda i: (i, 0, 0))
    return pl.pallas_call(
        expert_body,
        grid=(n,),
        in_specs=[spec(rows, 2 * D), spec(D, ff), spec(ff, D)],
        out_specs=[spec(rows, 2 * D), spec(D, ff), spec(ff, D)],
        out_shape=[sds(x.shape, BF), sds((n, D, ff)), sds((n, ff, D))],
        compiler_params=pltpu.CompilerParams(vmem_limit_bytes=LIMIT),
        name="experts",
    )(x, w_in, w_out)


def after_body(
    ret_ref, disp_ref, h1_ref, xn2_ref, gate_ref, cot_ref, routes_ref, wo_ref, att_ref, gain_ref,
    mixed_ref, dh1_ref, dat_ref, dout_ref, drouter_ref, dgain_ref,
):
    tok = h1_ref.shape[0]
    both = [dot(disp_ref[k], ret_ref[...]) for k in range(2)]
    gate = [gate_ref[:, k : k + 1] for k in range(2)]
    h1 = h1_ref[...]
    dy = cot_ref[...].astype(F32)
    picked = [both[k][:, :D] for k in range(2)]
    mixed_ref[...] = (h1 + (gate[0] * picked[0] + gate[1] * picked[1])).astype(BF)
    dgate = [jnp.sum(dy * picked[k], axis=-1, keepdims=True) for k in range(2)]
    mean = gate[0] * dgate[0] + gate[1] * dgate[1]
    lanes = lax.broadcasted_iota(jnp.int32, (tok, E), 1)
    dlog = jnp.zeros((tok, E), F32)
    for k in range(2):
        dlog = dlog + jnp.where(routes_ref[:, k : k + 1] == lanes, gate[k] * (dgate[k] - mean), 0.0)
    dlog = dlog.astype(BF)
    xn2 = xn2_ref[...]
    dxn = both[0][:, D:] + both[1][:, D:] + dot(dlog, wo_ref[:, D : D + E], 1, 1)
    drouter_ref[...] = dot(xn2, dlog, 0, 0).astype(BF)
    inv = lax.rsqrt(jnp.mean(h1 * h1, axis=-1, keepdims=True) + EPS)
    hat = h1 * inv
    dgain_ref[...] = jnp.sum((dxn * hat).reshape(tok // 8, 8, D), axis=0)
    cen = dxn * gain_ref[...]
    dh1 = dy + inv * (cen - hat * jnp.mean(cen * hat, axis=-1, keepdims=True))
    dh1_ref[...] = dh1
    dh1b = dh1.astype(BF)
    att = jnp.concatenate([att_ref[i] for i in range(G)], axis=1)
    dout_ref[...] = dot(att, dh1b, 0, 0).astype(BF)
    dat = dot(dh1b, wo_ref[:, :D], 1, 1).astype(BF)
    for i in range(G):
        dat_ref[i] = dat[:, i * GW : (i + 1) * GW]


def shards(tokens, routes, cotangent, gains, rel_bias, attn_qkv, attn_out, router, w_in, w_out):
    tok = tokens.shape[1]
    n_ctx, nf = lax.axis_size("ctx"), lax.axis_size("fsdp")
    n_dev = n_ctx * nf
    R, X = n_ctx // G, nf // CORES
    seq = tok * n_ctx
    per_dev = w_in.shape[0]
    qr, orows = attn_qkv.shape[0], attn_out.shape[0]
    x2, cot, route2 = tokens.reshape(tok, D), cotangent.reshape(tok, D), routes.reshape(tok, 2)

    n_gain, n_bias = gains.size, rel_bias.size
    tile = jnp.concatenate([gains.reshape(-1), rel_bias]).astype(F32)
    tile = jnp.broadcast_to(jnp.pad(tile, (0, 128 - n_gain - n_bias)), (8, 128))
    xall, wall, oall, tails = gather(n_ctx, nf, x2, attn_qkv, attn_out, router, tile)
    wall = wall.reshape(n_dev * qr, GW)
    wo = oall.reshape(D, D + 2 * E)
    tails = tails.reshape(n_dev, 8, 128)
    table = tails[:, 0, n_gain : n_gain + n_bias].reshape(H * NB)

    part = functools.partial
    width = math.gcd(n_ctx, 8)
    tiles_shape = (HG, n_ctx + R - 1, tok, tok)
    att, lse, q, k, v, tiles, gain1, gain2 = call(
        part(attend_body, n_ctx, nf),
        [sds((G, tok, GW), BF), sds((G, tok, 128)), sds((HG, G * tok, DH), BF)] + [sds((HG, seq, DH), BF)] * 2
        + [sds(tiles_shape), sds((1, D)), sds((1, D))],
        [xall, wall, tails, table],
        in_specs=[VM, VM, VM, SM],
        name="attend",
    )
    att_in = swap(n_ctx, nf, att, 2, "swap_att")[0]
    h1, xn2, gate, disp, packed = call(
        middle_body,
        [sds((tok, D)), sds((tok, D), BF), sds((tok, 2)), sds((2, tok, E * CAP), BF), sds((E * CAP, 2 * D), BF)],
        [att_in, x2, wo, gain2, route2, cot],
        name="middle",
    )
    recv = dispatch(n_ctx, nf, packed.reshape(n_ctx, per_dev, CAP, 2 * D))
    rows = nf * n_ctx * CAP
    part_rows, d_w_in, d_w_out = experts(recv.reshape(per_dev, rows, 2 * D), w_in, w_out)
    ret = combine(n_ctx, nf, part_rows.reshape(per_dev, nf, n_ctx, CAP, 2 * D))
    mixed, dh1, dat, d_out, d_router, dgain2 = call(
        after_body,
        [sds((tok, D), BF), sds((tok, D)), sds((G, tok, GW), BF), sds((D, D), BF), sds((D, E), BF), sds((8, D))],
        [ret.reshape(E * CAP, 2 * D), disp, h1, xn2, gate, cot, route2, wo, att_in, gain2],
        name="after",
    )
    lead = (G, R, X, CORES)
    more = (d_out.reshape(lead + (orows, D)), d_router.reshape(lead + router.shape))
    do, d_out_mine, d_router_mine = swap(n_ctx, nf, dat, 5, "swap_dat", more)
    dx, dw, dgain1, dtab = call(
        part(attend_back_body, n_ctx, nf),
        [sds((n_ctx, tok, D), BF), sds((3 * D, GW), BF), sds((8, D)), sds((HG, NB, 8, tok))],
        [xall, wall, gain1, tiles, lse, q, k, v, att, do],
        scratch=[
            pltpu.VMEM(tiles_shape, F32), pltpu.VMEM((HG, seq, DH), F32), pltpu.VMEM((HG, seq, DH), F32),
            pltpu.VMEM((width, tok, D), BF), pltpu.VMEM((G, tok, GW), BF), pltpu.VMEM((2, width, tok, GW), BF),
            pltpu.VMEM((2, D, GW) if width < n_ctx else (2, 8, GW), F32),
        ],
        name="attend_back",
        limit=LIMIT if width == n_ctx else 61 * 1024 * 1024,
    )
    dtab = jnp.sum(dtab, axis=(2, 3)).reshape(1, HG * NB)
    own_group = jnp.arange(G)[:, None] == lax.axis_index("ctx") // R
    dtab = jnp.where(own_group, dtab, 0.0).reshape(n_dev, n_bias)
    dgains = jnp.stack([jnp.sum(dgain1, axis=0), jnp.sum(dgain2, axis=0)])
    dgains = dgains.reshape(2, n_dev, -1).transpose(1, 0, 2).reshape(n_dev, n_gain)
    d_tail = jnp.pad(jnp.concatenate([dgains, dtab], axis=1), ((0, 0), (0, 128 - n_gain - n_bias)))
    d_tail = jnp.broadcast_to(d_tail[:, None, :], (n_dev, 8, 128)).reshape(lead + (8, 128))
    d_tokens, d_qkv, tail_mine = reduce_all(n_ctx, nf, dx, dw.reshape(lead + (qr, GW)), d_tail, x2, gain1)
    return (
        mixed.reshape(1, tok, D),
        (dh1 + d_tokens).reshape(1, tok, D),
        tail_mine[0, :n_gain].reshape(gains.shape),
        tail_mine[0, n_gain : n_gain + n_bias],
        d_qkv,
        d_out_mine,
        d_router_mine,
        d_w_in,
        d_w_out,
    )


def solution(mesh):
    return jax.shard_map(
        shards,
        mesh=mesh,
        in_specs=(
            P("fsdp", "ctx", None),
            P("fsdp", "ctx", None),
            P("fsdp", "ctx", None),
            P(None, ("ctx", "fsdp")),
            P(("ctx", "fsdp")),
            P(("ctx", "fsdp"), None),
            P(("ctx", "fsdp"), None),
            P(("ctx", "fsdp"), None),
            P("ctx", None, "fsdp"),
            P("ctx", "fsdp", None),
        ),
        out_specs=(
            P("fsdp", "ctx", None),
            P("fsdp", "ctx", None),
            P(None, ("ctx", "fsdp")),
            P(("ctx", "fsdp")),
            P(("ctx", "fsdp"), None),
            P(("ctx", "fsdp"), None),
            P(("ctx", "fsdp"), None),
            P("ctx", None, "fsdp"),
            P("ctx", "fsdp", None),
        ),
        check_vma=False,
    )
```

```python
import functools
import math

import jax
import jax.numpy as jnp
from jax import lax
from jax.experimental import pallas as pl
from jax.experimental.pallas import tpu as pltpu
from jax.sharding import PartitionSpec as P

D = 768
H = 12
DH = 64
E = 64
NB = 32
CAP = 8
G = 4
HG = H // G
GW = HG * DH
CORES = 2

EPS = 1e-06
EDGES = (16, 23, 32, 45, 64, 91, 128, 181, 256, 362, 512, 724, 1024, 1448, 2048, 2896)
STARTS = tuple(range(16)) + EDGES
GELU_C = 0.7978845608028654
NEG = -1e30
MESH = pl.DeviceIdType.MESH
F32 = jnp.float32
BF = jnp.bfloat16
VM = pl.BlockSpec(memory_space=pltpu.VMEM)
HB = pl.BlockSpec(memory_space=pl.ANY)
SM = pl.BlockSpec(memory_space=pltpu.SMEM)
WINDOW = 2
LIMIT = 56 * 1024 * 1024


def dot(a, b, ca=1, cb=0):
    return lax.dot_general(a, b, (((ca,), (cb,)), ((), ())), preferred_element_type=F32)


def call(body, outs, ins, out_specs=None, in_specs=None, scratch=(), cid=None, name=None, cost=None, limit=LIMIT, **kw):
    params = dict(vmem_limit_bytes=limit)
    if cid is not None:
        params.update(collective_id=cid, has_side_effects=True)
    return pl.pallas_call(
        body,
        out_shape=outs,
        in_specs=in_specs or [VM] * len(ins),
        out_specs=out_specs or [VM] * len(outs),
        scratch_shapes=list(scratch),
        compiler_params=pltpu.CompilerParams(**params),
        name=name,
        cost_estimate=cost,
        **kw,
    )(*ins)


def sds(shape, kind=F32):
    return jax.ShapeDtypeStruct(shape, kind)


class Place:
    def __init__(self, n_ctx, nf):
        self.n_ctx, self.nf = n_ctx, nf
        self.R, self.X = n_ctx // G, nf // CORES
        self.c, self.f = lax.axis_index("ctx"), lax.axis_index("fsdp")
        self.g, self.r = lax.div(self.c, self.R), lax.rem(self.c, self.R)
        self.x, self.k = lax.div(self.f, CORES), lax.rem(self.f, CORES)

    def up(self, v, d, n):
        return lax.rem(v + d, n)

    def ctx(self, dg, dr):
        return self.up(self.g, dg % G, G) * self.R + self.up(self.r, dr % self.R, self.R)

    def fs(self, dx, dk):
        return self.up(self.x, dx % self.X, self.X) * CORES + self.up(self.k, dk % CORES, CORES)

    def dev(self, dg, dr, dx, dk):
        return (self.ctx(dg, dr), self.fs(dx, dk))


def greet(targets):
    bar = pltpu.get_barrier_semaphore()
    for t in targets:
        pl.semaphore_signal(bar, inc=1, device_id=t, device_id_type=MESH)
    pl.semaphore_wait(bar, len(targets))


def mirror(c, d, n):
    out, bit = 0, 1
    while bit < n:
        out = out + lax.rem(lax.div(c, bit) + (d // bit) % 2, 2) * bit
        bit *= 2
    return out


def mixed_order(n):
    far, near = list(range(n // 2, n)), list(range(1, n // 2))
    out = []
    while far or near:
        if far:
            out.append(far.pop(0))
        if near:
            out.append(near.pop(0))
    return out


class Sends:
    def __init__(self):
        self.made = []

    def __call__(self, src, dst, ss, rs, dev):
        cp = rcopy(src, dst, ss, rs, dev)
        cp.start()
        self.made.append(cp)
        return cp

    def finish(self):
        for cp in self.made:
            cp.wait_send()


def got(at, s, r, dev):
    rcopy(at, at, s, r, dev).wait_recv()


class Scatter:
    COUNT = 11

    @staticmethod
    def scratch(G_, R, X, blk, kind):
        sem = lambda *n: pltpu.SemaphoreType.DMA(n)
        vm = lambda *n: pltpu.VMEM(n + blk, kind)
        return [vm(G_, R, X), vm(G_, R, X), vm(R * X, G_), vm(G_), vm(G_), sem(1), sem(1), sem(R * X), sem(R * X), sem(G_), sem(G_)]

    def __init__(self, p, send, src, refs):
        self.p, self.send, self.src = p, send, src
        self.cin, self.s1, self.qin, self.s2, self.win = refs[:5]
        self.c1, self.e1, self.c2, self.e2, self.c3, self.e3 = refs[5:]
        self.quad = [(er, ex) for er in range(p.R) for ex in range(p.X)]

    def over_cores(self):
        p = self.p
        self.send(self.src.at[:, :, :, 1 - p.k], self.cin, self.c1.at[0], self.e1.at[0], p.dev(0, 0, 0, 1))

    def over_quad(self):
        p = self.p
        got(self.cin, self.c1.at[0], self.e1.at[0], p.dev(0, 0, 0, 1))
        self.s1[...] = (self.src[:, :, :, p.k].astype(F32) + self.cin[...].astype(F32)).astype(self.s1.dtype)
        for i, (er, ex) in enumerate(self.quad):
            if i:
                at = self.s1.at[:, p.up(p.r, er, p.R), p.up(p.x, ex, p.X)]
                self.send(at, self.qin.at[i], self.c2.at[i], self.e2.at[i], p.dev(0, er, ex, 0))

    def over_groups(self):
        p = self.p
        total = self.s1[:, p.r, p.x].astype(F32)
        for i, (er, ex) in enumerate(self.quad):
            if i:
                got(self.qin.at[i], self.c2.at[i], self.e2.at[i], p.dev(0, -er, -ex, 0))
                total = total + self.qin[i].astype(F32)
        self.s2[...] = total.astype(self.s2.dtype)
        self.win[p.g] = self.s2[p.g]
        for dg in (2, 1, 3):
            self.send(self.s2.at[p.up(p.g, dg, G)], self.win.at[p.g], self.c3.at[dg], self.e3.at[dg], p.dev(dg, 0, 0, 0))

    def pieces(self):
        p = self.p
        for dg in (1, 3, 2):
            got(self.win.at[p.up(p.g, G - dg, G)], self.c3.at[dg], self.e3.at[dg], p.dev(-dg, 0, 0, 0))
        return [self.win[i].astype(F32) for i in range(G)]


def rcopy(src, dst, ss, rs, dev):
    return pltpu.make_async_remote_copy(
        src_ref=src, dst_ref=dst, send_sem=ss, recv_sem=rs, device_id=dev, device_id_type=MESH
    )


class Gather:
    COUNT = 8

    @staticmethod
    def scratch(R, X):
        sem = lambda *n: pltpu.SemaphoreType.DMA(n)
        return [sem(G)] * 2 + [sem(R)] * 2 + [sem(X)] * 2 + [sem(1)] * 2

    def __init__(self, p, send, piece, out, refs):
        self.p, self.send, self.piece, self.out = p, send, piece, out
        self.a, self.b = refs[0::2], refs[1::2]
        self.mine = out.at[p.g, p.r, p.x, p.k]

    def over_groups(self):
        p = self.p
        for d in (2, 1, 3):
            self.send(self.piece(d), self.mine, self.a[0].at[d], self.b[0].at[d], p.dev(d, 0, 0, 0))

    def over_rows(self):
        p = self.p
        for d in (1, 3, 2):
            at = self.out.at[p.up(p.g, G - d, G), p.r, p.x, p.k]
            got(at, self.a[0].at[d], self.b[0].at[d], p.dev(-d, 0, 0, 0))
        at = self.out.at[:, p.r, p.x, p.k]
        for er in range(1, p.R):
            self.send(at, at, self.a[1].at[er], self.b[1].at[er], p.dev(0, er, 0, 0))

    def over_x(self):
        p = self.p
        for er in range(1, p.R):
            at = self.out.at[:, p.up(p.r, p.R - er, p.R), p.x, p.k]
            got(at, self.a[1].at[er], self.b[1].at[er], p.dev(0, -er, 0, 0))
        at = self.out.at[:, :, p.x, p.k]
        for ex in range(1, p.X):
            self.send(at, at, self.a[2].at[ex], self.b[2].at[ex], p.dev(0, 0, ex, 0))

    def over_cores(self):
        p = self.p
        for ex in range(1, p.X):
            at = self.out.at[:, :, p.up(p.x, p.X - ex, p.X), p.k]
            got(at, self.a[2].at[ex], self.b[2].at[ex], p.dev(0, 0, -ex, 0))
        at = self.out.at[:, :, :, p.k]
        self.send(at, at, self.a[3].at[0], self.b[3].at[0], p.dev(0, 0, 0, 1))

    def settle(self):
        p = self.p
        got(self.out.at[:, :, :, 1 - p.k], self.a[3].at[0], self.b[3].at[0], p.dev(0, 0, 0, 1))


def gather_body(n_ctx, nf, tok, aq, ao, router, tile, xall, wall, oall, tiles, wq, wo, t1s, t1r, t2s, t2r, loc, *refs):
    p = Place(n_ctx, nf)
    R, X = p.R, p.X
    for i in range(G):
        wq[i] = aq[:, i * GW : (i + 1) * GW]
    wo[:, :D] = ao[...]
    wo[:, D : D + E] = router[...]
    wo[:, D + E :] = jnp.zeros((wo.shape[0], E), BF)
    greet(
        [p.dev(d, 0, 0, 0) for d in range(1, G)]
        + [p.dev(0, er, 0, 0) for er in range(1, R)]
        + [p.dev(0, 0, ex, 0) for ex in range(1, X)]
        + [p.dev(0, 0, 0, 1)]
    )
    send = Sends()
    n = Gather.COUNT
    items = [
        Gather(p, send, lambda d: tile, tiles, refs[:n]),
        Gather(p, send, lambda d: wq.at[p.up(p.g, d, G)], wall, refs[n : 2 * n]),
        Gather(p, send, lambda d: wo, oall, refs[2 * n :]),
    ]
    own = [
        pltpu.make_async_copy(src, dst, loc.at[i])
        for i, (src, dst) in enumerate([(tok, xall.at[p.c])] + [(it.piece(0), it.mine) for it in items])
    ]
    for cp in own:
        cp.start()
    sides = [(s, -1) for s in range(1, G)] + [(s, 1) for s in range(1, G)]

    def exists(at):
        return (p.g + at >= 0) & (p.g + at < G)

    def hop(s, way):
        at = way * (s - 1)
        src = tok if s == 1 else xall.at[p.ctx(at, 0)]
        i = s + (G if way > 0 else 0)
        return rcopy(src, xall.at[p.ctx(at, 0)], t1s.at[i], t1r.at[i], p.dev(-way, 0, 0, 0))

    def row(at, e):
        src = tok if at == 0 else xall.at[p.ctx(at, 0)]
        return rcopy(src, xall.at[p.ctx(at, 0)], t2s.at[at + G, e], t2r.at[at + G, e], p.dev(0, e, 0, 0))

    def step(s):
        for way in (-1, 1):

            @pl.when(exists(way * s))
            def _():
                i = s + (G if way > 0 else 0)
                got(xall.at[p.ctx(way * s, 0)], t1s.at[i], t1r.at[i], p.dev(way, 0, 0, 0))
                if s + 1 < G:

                    @pl.when(exists(-way))
                    def _():
                        hop(s + 1, way).start()

                for e in range(1, R):
                    row(way * s, e).start()

    for it in items[:2]:
        it.over_groups()
    for way in (-1, 1):

        @pl.when(exists(-way))
        def _():
            hop(1, way).start()

    for e in range(1, R):
        row(0, e).start()
    items[2].over_groups()
    for cp in own[1:]:
        cp.wait()
    items[0].over_rows()
    items[1].over_rows()
    step(1)
    items[2].over_rows()
    items[0].over_x()
    items[1].over_x()
    step(2)
    items[2].over_x()
    items[0].over_cores()
    items[1].over_cores()
    step(3)
    items[2].over_cores()
    for it in items:
        it.settle()
    for at in range(1 - G, G):

        @pl.when(exists(at))
        def _():
            for e in range(1, R):
                got(xall.at[p.ctx(at, -e)], t2s.at[at + G, e], t2r.at[at + G, e], p.dev(0, -e, 0, 0))
                row(at, e).wait_send()

    for s, way in sides:

        @pl.when(exists(-way) & exists(way * (s - 1)))
        def _():
            hop(s, way).wait_send()

    send.finish()
    own[0].wait()


def gather(n_ctx, nf, tok, aq, ao, router, tile):
    R, X = n_ctx // G, nf // CORES
    lead = (G, R, X, CORES)
    sem = lambda *s: pltpu.SemaphoreType.DMA(s)
    qr, rows = aq.shape[0], ao.shape[0]
    return call(
        functools.partial(gather_body, n_ctx, nf),
        [
            sds((n_ctx,) + tok.shape, BF),
            sds(lead + (qr, GW), BF),
            sds(lead + (rows, D + 2 * E), BF),
            sds(lead + tile.shape, tile.dtype),
        ],
        [tok, aq, ao, router, tile],
        out_specs=[HB] * 4,
        scratch=[pltpu.VMEM((G, qr, GW), BF), pltpu.VMEM((rows, D + 2 * E), BF)]
        + [sem(2 * G)] * 2
        + [sem(2 * G, R)] * 2
        + [sem(4)]
        + Gather.scratch(R, X) * 3,
        cid=1,
        name="gather",
    )


def swap_body(n_ctx, nf, extra, *refs):
    p = Place(n_ctx, nf)
    src, more = refs[0], refs[1 : 1 + extra]
    dst, sums = refs[1 + extra], refs[2 + extra : 2 + 2 * extra]
    ss, rs, loc = refs[2 + 2 * extra : 5 + 2 * extra]
    rest = refs[5 + 2 * extra :]
    quad = [(er, ex) for er in range(p.R) for ex in range(p.X)]
    near = [p.dev(0, er, ex, 0) for er, ex in quad[1:]] + [p.dev(0, 0, 0, 1)]
    greet([p.dev(d, 0, 0, 0) for d in range(1, G)] + (near if extra else []))
    own = pltpu.make_async_copy(src.at[p.g], dst.at[p.g], loc)
    own.start()
    send = Sends()
    n = Scatter.COUNT
    scatters = [Scatter(p, send, m, rest[i * n : (i + 1) * n]) for i, m in enumerate(more)]
    for d in (2, 1, 3):
        send(src.at[p.up(p.g, d, G)], dst.at[p.g], ss.at[d], rs.at[d], p.dev(d, 0, 0, 0))
    for sc in scatters:
        sc.over_cores()
    for sc in scatters:
        sc.over_quad()
    for sc in scatters:
        sc.over_groups()
    for d in (1, 3, 2):
        got(dst.at[p.up(p.g, G - d, G)], ss.at[d], rs.at[d], p.dev(-d, 0, 0, 0))
    for sc, out in zip(scatters, sums):
        w = sc.pieces()
        out[...] = (w[0] + w[1]) + (w[2] + w[3])
    send.finish()
    own.wait()


def swap(n_ctx, nf, src, cid, name, more=()):
    sem = pltpu.SemaphoreType.DMA
    scratch = [sem((G,)), sem((G,)), sem]
    for m in more:
        scratch += Scatter.scratch(G, n_ctx // G, nf // CORES, m.shape[4:], m.dtype)
    return call(
        functools.partial(swap_body, n_ctx, nf, len(more)),
        [sds(src.shape, src.dtype)] + [sds(m.shape[4:]) for m in more],
        [src, *more],
        scratch=scratch,
        cid=cid,
        name=name,
    )


def dispatch_body(n_ctx, nf, packed, recv, ss, rs, xs, xr, ks, kr, loc):
    p = Place(n_ctx, nf)
    X = p.X
    greet(
        [(p.up(p.c, d, n_ctx), p.f) for d in range(1, n_ctx)]
        + [p.dev(0, 0, dx, 0) for dx in range(1, X)]
        + [p.dev(0, 0, 0, 1)]
    )
    own = pltpu.make_async_copy(packed.at[p.c], recv.at[:, p.f, p.c], loc)
    own.start()
    send = Sends()
    order = mixed_order(n_ctx)
    first = []

    def away(d):
        cc = mirror(p.c, d, n_ctx)
        first.append(send(packed.at[cc], recv.at[:, p.f, p.c], ss.at[d], rs.at[d], (cc, p.f)))

    def spread(d):
        cc = mirror(p.c, d, n_ctx)
        at = recv.at[:, p.f, cc]
        if d:
            got(at, ss.at[d], rs.at[d], (cc, p.f))
        src = packed.at[p.c] if d == 0 else at
        for dx in range(1, X):
            send(src, at, xs.at[d, dx], xr.at[d, dx], p.dev(0, 0, dx, 0))
        send(src, at, ks.at[d, 0], kr.at[d, 0], p.dev(0, 0, 0, 1))

    def relay(d):
        cc = mirror(p.c, d, n_ctx)
        for dx in range(1, X):
            at = recv.at[:, p.fs(-dx, 0), cc]
            got(at, xs.at[d, dx], xr.at[d, dx], p.dev(0, 0, -dx, 0))
            send(at, at, ks.at[d, dx], kr.at[d, dx], p.dev(0, 0, 0, 1))

    for d in order[:WINDOW]:
        away(d)
    spread(0)
    for i, d in enumerate(order):
        spread(d)
        if i + WINDOW < len(order):
            away(order[i + WINDOW])
        if i:
            relay(order[i - 1] if i > 1 else 0)
        if i == 1:
            relay(order[0])
    for d in order[max(1, len(order) - 1) :]:
        relay(d)
    for d in range(n_ctx):
        cc = mirror(p.c, d, n_ctx)
        for dx in range(X):
            at = recv.at[:, p.fs(-dx, 1), cc]
            got(at, ks.at[d, dx], kr.at[d, dx], p.dev(0, 0, 0, 1))
    send.finish()
    own.wait()


def dispatch(n_ctx, nf, packed):
    per_dev, width = packed.shape[1], packed.shape[3]
    X = nf // CORES
    sem = lambda *s: pltpu.SemaphoreType.DMA(s)
    return call(
        functools.partial(dispatch_body, n_ctx, nf),
        [sds((per_dev, nf, n_ctx, CAP, width), BF)],
        [packed],
        in_specs=[HB],
        out_specs=[HB],
        scratch=[sem(n_ctx)] * 2 + [sem(n_ctx, X)] * 4 + [pltpu.SemaphoreType.DMA],
        cid=3,
        name="dispatch",
    )[0]


def combine_body(n_ctx, nf, part, out, kept, cin, xsum, xin, fin, ss, rs, xs, xr, ks, kr, ls):
    p = Place(n_ctx, nf)
    X = p.X
    greet(
        [(p.up(p.c, d, n_ctx), p.f) for d in range(1, n_ctx)]
        + [p.dev(0, 0, dx, 0) for dx in range(1, X)]
        + [p.dev(0, 0, 0, 1)]
    )
    send = Sends()
    order = mixed_order(n_ctx) + [0]

    def keep(d, dx):
        return pltpu.make_async_copy(part.at[:, p.fs(dx, 0), mirror(p.c, d, n_ctx)], kept.at[dx, d], ls.at[d, dx])

    for d in order:
        cc = mirror(p.c, d, n_ctx)
        for dx in [*range(1, X), 0]:
            send(part.at[:, p.fs(dx, 1), cc], cin.at[dx, d], ks.at[d, dx], kr.at[d, dx], p.dev(0, 0, 0, 1))
            keep(d, dx).start()

    def across(d):
        for dx in range(1, X):
            got(cin.at[dx, d], ks.at[d, dx], kr.at[d, dx], p.dev(0, 0, 0, 1))
            keep(d, dx).wait()
            xsum[dx, d] = (kept[dx, d].astype(F32) + cin[dx, d].astype(F32)).astype(BF)
            send(xsum.at[dx, d], xin.at[dx, d], xs.at[d, dx], xr.at[d, dx], p.dev(0, 0, dx, 0))

    for d in order[:2]:
        across(d)
    for i, d in enumerate(order):
        if i + 2 < len(order):
            across(order[i + 2])
        cc = mirror(p.c, d, n_ctx)
        got(cin.at[0, d], ks.at[d, 0], kr.at[d, 0], p.dev(0, 0, 0, 1))
        keep(d, 0).wait()
        total = kept[0, d].astype(F32) + cin[0, d].astype(F32)
        for dx in range(1, X):
            got(xin.at[dx, d], xs.at[d, dx], xr.at[d, dx], p.dev(0, 0, -dx, 0))
            total = total + xin[dx, d].astype(F32)
        if d:
            fin[d] = total.astype(BF)
            send(fin.at[d], out.at[p.c], ss.at[d], rs.at[d], (cc, p.f))
        else:
            out[p.c] = total.astype(BF)
    for d in order[:-1]:
        cc = mirror(p.c, d, n_ctx)
        got(out.at[cc], ss.at[d], rs.at[d], (cc, p.f))
    send.finish()


def combine(n_ctx, nf, part):
    per_dev, width = part.shape[0], part.shape[-1]
    X = nf // CORES
    sem = lambda *s: pltpu.SemaphoreType.DMA(s)
    blk = (per_dev, CAP, width)
    return call(
        functools.partial(combine_body, n_ctx, nf),
        [sds((n_ctx,) + blk, BF)],
        [part],
        in_specs=[HB],
        scratch=[pltpu.VMEM((X, n_ctx) + blk, BF)] * 4
        + [pltpu.VMEM((n_ctx,) + blk, BF)]
        + [sem(n_ctx)] * 2
        + [sem(n_ctx, X)] * 5,
        cid=4,
        name="combine",
    )[0]


def reduce_body(
    n_ctx, nf, dx_ref, dw_ref, tail_ref, out_ref, router_ref, tok_ref, gain_ref,
    dtok_ref, dqkv_ref, dtail_ref, dout_ref, drouter_ref, *refs,
):
    p = Place(n_ctx, nf)
    R, X = p.R, p.X
    rin, gsum, gin, a1, b1, a2, b2 = refs[:7]
    n = Scatter.COUNT
    quad = [(er, ex) for er in range(R) for ex in range(X)]
    greet(
        [p.dev(d, 0, 0, 0) for d in range(1, G)]
        + [p.dev(0, er, ex, 0) for er, ex in quad[1:]]
        + [p.dev(0, 0, 0, 1)]
    )
    send = Sends()
    wsum = Scatter(p, send, dw_ref, refs[7 : 7 + n])
    tsum = Scatter(p, send, tail_ref, refs[7 + n : 7 + 2 * n])
    osum = Scatter(p, send, out_ref, refs[7 + 2 * n : 7 + 3 * n])
    rsum = Scatter(p, send, router_ref, refs[7 + 3 * n :])
    every = (tsum, rsum, wsum, osum)
    for one in every:
        one.over_cores()
    far = (2, 1, 3, 0)

    def near(dg):
        for er in range(1, R):
            send(dx_ref.at[p.ctx(dg, er)], rin.at[er, dg], a1.at[dg, er], b1.at[dg, er], p.dev(0, er, 0, 0))

    near(far[0])
    near(far[1])
    for one in every:
        one.over_quad()
    near(far[2])
    near(far[3])
    for dg in far:
        total = dx_ref[p.ctx(dg, 0)].astype(F32)
        for er in range(1, R):
            got(rin.at[er, dg], a1.at[dg, er], b1.at[dg, er], p.dev(0, -er, 0, 0))
            total = total + rin[er, dg].astype(F32)
        gsum[dg] = total.astype(BF)
        if dg:
            send(gsum.at[dg], gin.at[dg], a2.at[dg], b2.at[dg], p.dev(dg, 0, 0, 0))
        if dg == far[1]:
            for one in every:
                one.over_groups()
    grad = gsum[0].astype(F32)
    for dg in (1, 3, 2):
        got(gin.at[dg], a2.at[dg], b2.at[dg], p.dev(-dg, 0, 0, 0))
        grad = grad + gin[dg].astype(F32)
    rows = tok_ref[...].astype(F32)
    inv = lax.rsqrt(jnp.mean(rows * rows, axis=-1, keepdims=True) + EPS)
    hat = rows * inv
    grad = grad * gain_ref[...]
    dtok_ref[...] = inv * (grad - hat * jnp.mean(grad * hat, axis=-1, keepdims=True))
    for one, ref in ((tsum, dtail_ref), (rsum, drouter_ref), (osum, dout_ref)):
        w = one.pieces()
        ref[...] = (w[0] + w[1]) + (w[2] + w[3])
    dqkv_ref[...] = jnp.concatenate(wsum.pieces(), axis=1)
    send.finish()


def reduce_all(n_ctx, nf, dx, dw, tail, out, router, tok, gain):
    R, X = n_ctx // G, nf // CORES
    tb = dx.shape[1:]
    sem = lambda *n: pltpu.SemaphoreType.DMA(n)
    vm = lambda *n: pltpu.VMEM(n + tb, BF)
    return call(
        functools.partial(reduce_body, n_ctx, nf),
        [sds(tb), sds((dw.shape[4], D))] + [sds(m.shape[4:]) for m in (tail, out, router)],
        [dx, dw, tail, out, router, tok, gain],
        scratch=[vm(R, G), vm(G), vm(G), sem(G, R), sem(G, R), sem(G), sem(G)]
        + Scatter.scratch(G, R, X, dw.shape[4:], BF)
        + Scatter.scratch(G, R, X, tail.shape[4:], F32)
        + Scatter.scratch(G, R, X, out.shape[4:], BF)
        + Scatter.scratch(G, R, X, router.shape[4:], BF),
        cid=6,
        name="reduce",
    )


def bias_tiles(tab_ref, tiles, g, R, nd):
    tok = tiles.shape[2]
    lane = lax.broadcasted_iota(jnp.int32, (8, 2 * tok), 1)
    apart = lax.broadcasted_iota(jnp.int32, (tok, tok), 0) - lax.broadcasted_iota(jnp.int32, (tok, tok), 1)
    for i in range(nd):
        d = i - (R - 1)
        least, most = (d - 1) * tok + 1, (d + 1) * tok - 1
        used = [b for b in range(NB) if STARTS[b] <= most and (b + 1 == NB or STARTS[b + 1] > least)]
        for hh in range(HG):
            base = (g * HG + hh) * NB
            few = len(used) <= 8
            off = apart + d * tok if few else d * tok + tok - lane
            first = tab_ref[base + used[0]] if used and least >= STARTS[used[0]] else NEG
            val = jnp.full(off.shape, first, F32)
            for b in used:
                if least < STARTS[b]:
                    val = jnp.where(off >= STARTS[b], tab_ref[base + b], val)
            if not few:
                wide = jnp.concatenate([val] * (tok // 8), axis=0)
                val = pltpu.roll(wide, tok, 1, stride=1, stride_axis=0)[:, :tok]
            tiles[hh, i] = val


def normed(x_ref, b):
    rows = x_ref[b].astype(F32)
    inv = lax.rsqrt(jnp.mean(rows * rows, axis=-1, keepdims=True) + EPS)
    return rows * inv


def scores(q, keys, tiles, hh, gq, r, R, n):
    s = dot(q, keys, 1, 1) * (1.0 / math.sqrt(DH))
    bias = jnp.concatenate([tiles[hh, gq * R + r - kb + R - 1] for kb in range(n)], axis=1)
    return s + bias


def attend_body(n_ctx, nf, x_ref, w_ref, tails_ref, tab_ref, att_ref, lse_ref, q_ref, k_ref, v_ref, tiles, gain1_ref, gain2_ref):
    p = Place(n_ctx, nf)
    R, tok = p.R, x_ref.shape[1]
    gw = D // (n_ctx * nf)
    for i in range(n_ctx * nf):
        gain1_ref[:, i * gw : (i + 1) * gw] = tails_ref[i, 0:1, :gw]
        gain2_ref[:, i * gw : (i + 1) * gw] = tails_ref[i, 0:1, gw : 2 * gw]
    gain = gain1_ref[...]
    bias_tiles(tab_ref, tiles, p.g, R, n_ctx + R - 1)

    def block(b, _):
        xn = (normed(x_ref, b) * gain).astype(BF)
        at = pl.ds(pl.multiple_of(b * tok, tok), tok)
        for m, ref in ((1, k_ref), (2, v_ref)):
            y = dot(xn, w_ref[pl.ds(m * D, D)]).astype(BF)
            for hh in range(HG):
                ref[hh, at] = y[:, hh * DH : (hh + 1) * DH]
        return 0

    lax.fori_loop(0, n_ctx, block, 0)
    for gq in range(G):
        xn = (normed(x_ref, gq * R + p.r) * gain).astype(BF)
        y = dot(xn, w_ref[pl.ds(0, D)]).astype(BF)
        for hh in range(HG):
            q_ref[hh, pl.ds(gq * tok, tok)] = y[:, hh * DH : (hh + 1) * DH]
    for gq in range(G):
        n = (gq + 1) * R
        outs = []
        for hh in range(HG):
            s = scores(q_ref[hh, pl.ds(gq * tok, tok)], k_ref[hh, pl.ds(0, n * tok)], tiles, hh, gq, p.r, R, n)
            top = jnp.max(s, axis=-1, keepdims=True)
            w = jnp.exp(s - top)
            total = jnp.sum(w, axis=-1, keepdims=True)
            acc = dot(w.astype(BF), v_ref[hh, pl.ds(0, n * tok)])
            outs.append((acc / total).astype(BF))
            lse_ref[gq, :, hh : hh + 1] = top + jnp.log(total)
        att_ref[gq] = jnp.concatenate(outs, axis=1)


def attend_back_body(
    n_ctx, nf, x_ref, w_ref, gain_ref, tiles, lse_ref, q_ref, k_ref, v_ref, att_ref, do_ref,
    dx_ref, dw_ref, dgain_ref, dtab_ref, dtiles, dk_acc, dv_acc, xn_s, dq_s, dkv_s, dw_acc,
):
    p = Place(n_ctx, nf)
    R, tok = p.R, x_ref.shape[1]
    scale = 1.0 / math.sqrt(DH)
    dtiles[...] = jnp.zeros_like(dtiles)
    dk_acc[...] = jnp.zeros_like(dk_acc)
    dv_acc[...] = jnp.zeros_like(dv_acc)
    for gq in range(G):
        n = (gq + 1) * R
        rows = pl.ds(gq * tok, tok)
        keys = pl.ds(0, n * tok)
        do_all = do_ref[gq]
        prod = do_all.astype(F32) * att_ref[gq].astype(F32)
        dqs = []
        for hh in range(HG):
            q, kk, vv = q_ref[hh, rows], k_ref[hh, keys], v_ref[hh, keys]
            do = do_all[:, hh * DH : (hh + 1) * DH]
            delta = jnp.sum(prod[:, hh * DH : (hh + 1) * DH], axis=-1, keepdims=True)
            s = scores(q, kk, tiles, hh, gq, p.r, R, n)
            w = jnp.exp(s - lse_ref[gq, :, hh : hh + 1])
            ds = w * (dot(do, vv, 1, 1) - delta)
            for kb in range(n):
                at = gq * R + p.r - kb + R - 1
                dtiles[hh, at] = dtiles[hh, at] + ds[:, kb * tok : (kb + 1) * tok]
            dsb = ds.astype(BF)
            dqs.append((dot(dsb, kk) * scale).astype(BF))
            dk_acc[hh, keys] = dk_acc[hh, keys] + dot(dsb, q, 0, 0)
            dv_acc[hh, keys] = dv_acc[hh, keys] + dot(w.astype(BF), do, 0, 0)
        dq_s[gq] = jnp.concatenate(dqs, axis=1)
    for hh in range(HG):
        sums = [None] * NB
        off0 = lax.broadcasted_iota(jnp.int32, (tok, tok), 0) - lax.broadcasted_iota(jnp.int32, (tok, tok), 1)
        for d in range(n_ctx):
            t = dtiles[hh, d + R - 1]
            off = off0 + d * tok
            for b in range(NB):
                low = STARTS[b]
                high = STARTS[b + 1] if b + 1 < NB else 1 << 30
                if high <= d * tok - tok + 1 or low > d * tok + tok - 1:
                    continue
                part = jnp.where((off >= low) & (off < high), t, 0.0)
                part = jnp.sum(part.reshape(tok // 8, 8, tok), axis=0)
                sums[b] = part if sums[b] is None else sums[b] + part
        for b in range(NB):
            dtab_ref[hh, b] = jnp.zeros((8, tok), F32) if sums[b] is None else sums[b]
    gain = gain_ref[...]
    xn_q = jnp.concatenate([(normed(x_ref, gq * R + p.r) * gain).astype(BF) for gq in range(G)], axis=0)
    dw_ref[pl.ds(0, D)] = dot(xn_q, dq_s[...].reshape(G * tok, GW), 0, 0).astype(BF)
    width = xn_s.shape[0]
    dgain = jnp.zeros((8, D), F32)
    for first in range(0, n_ctx, width):

        def block(i, dg):
            b = first + i
            hat = normed(x_ref, b)
            at = pl.ds(pl.multiple_of(b * tok, tok), tok)
            xn_s[i] = (hat * gain).astype(BF)
            dk = jnp.concatenate([(dk_acc[hh, at] * scale).astype(BF) for hh in range(HG)], axis=1)
            dv = jnp.concatenate([dv_acc[hh, at].astype(BF) for hh in range(HG)], axis=1)
            dkv_s[0, i] = dk
            dkv_s[1, i] = dv
            mine = lax.rem(b, R) == p.r
            dq = jnp.where(mine, dq_s[lax.div(b, R)], jnp.zeros((tok, GW), BF))
            dxn = (
                dot(dq, w_ref[pl.ds(0, D)], 1, 1)
                + dot(dk, w_ref[pl.ds(D, D)], 1, 1)
                + dot(dv, w_ref[pl.ds(2 * D, D)], 1, 1)
            )
            dx_ref[b] = dxn.astype(BF)
            return dg + jnp.sum((dxn * hat).reshape(tok // 8, 8, D), axis=0)

        dgain = lax.fori_loop(0, width, block, dgain)
        xn = xn_s[...].reshape(width * tok, D)
        for m in range(2):
            piece = dot(xn, dkv_s[m].reshape(width * tok, GW), 0, 0)
            if first:
                piece = piece + dw_acc[m]
            if first + width < n_ctx:
                dw_acc[m] = piece
            else:
                dw_ref[pl.ds((m + 1) * D, D)] = piece.astype(BF)
    dgain_ref[...] = dgain


def middle_body(
    att_ref, tok_ref, wo_ref, gain_ref, routes_ref, cot_ref,
    h1_ref, xn2_ref, gate_ref, disp_ref, packed_ref,
):
    tok = tok_ref.shape[0]
    att = jnp.concatenate([att_ref[i] for i in range(G)], axis=1)
    h1 = tok_ref[...].astype(F32) + dot(att, wo_ref[:, :D])
    h1_ref[...] = h1
    inv = lax.rsqrt(jnp.mean(h1 * h1, axis=-1, keepdims=True) + EPS)
    xn2 = (h1 * inv * gain_ref[...]).astype(BF)
    xn2_ref[...] = xn2
    logits = dot(xn2, wo_ref[:, D : D + E])
    experts = lax.broadcasted_iota(jnp.int32, (tok, E), 1)
    route = [routes_ref[:, k : k + 1] for k in range(2)]
    member = [(route[k] == experts).astype(F32) for k in range(2)]
    chosen = [jnp.sum(logits * member[k], axis=-1, keepdims=True) for k in range(2)]
    top = jnp.maximum(chosen[0], chosen[1])
    ex = [jnp.exp(chosen[k] - top) for k in range(2)]
    gate = [ex[k] / (ex[0] + ex[1]) for k in range(2)]
    gate_ref[...] = jnp.concatenate(gate, axis=1)
    before = lax.broadcasted_iota(jnp.int32, (tok, tok), 0) > lax.broadcasted_iota(jnp.int32, (tok, tok), 1)
    counts = dot(before.astype(F32).astype(BF), (member[0] + member[1]).astype(BF))
    slots = lax.broadcasted_iota(jnp.int32, (tok, E * CAP), 1)
    disp = []
    for k in range(2):
        slot = jnp.sum(counts * member[k], axis=-1, keepdims=True).astype(jnp.int32)
        disp.append((route[k] * CAP + slot == slots).astype(F32).astype(BF))
        disp_ref[k] = disp[k]
    cot = cot_ref[...].astype(F32)
    packed_ref[:, :D] = dot(disp[0] + disp[1], xn2, 0, 0).astype(BF)
    rows = dot(disp[0], (gate[0] * cot).astype(BF), 0, 0) + dot(disp[1], (gate[1] * cot).astype(BF), 0, 0)
    packed_ref[:, D:] = rows.astype(BF)


def expert_body(x_ref, win_ref, wout_ref, part_ref, dwin_ref, dwout_ref):
    x, dy = x_ref[0, :, :D], x_ref[0, :, D:]
    win, wout = win_ref[0], wout_ref[0]
    pre = dot(x, win)
    inner = GELU_C * (pre + 0.044715 * pre * pre * pre)
    th = jnp.tanh(inner)
    hid = (0.5 * pre * (1.0 + th)).astype(BF)
    slope = 0.5 * (1.0 + th) + 0.5 * pre * (1.0 - th * th) * GELU_C * (1.0 + 3.0 * 0.044715 * pre * pre)
    dpre = (dot(dy, wout, 1, 1) * slope).astype(BF)
    part_ref[0, :, :D] = dot(hid, wout).astype(BF)
    part_ref[0, :, D:] = dot(dpre, win, 1, 1).astype(BF)
    dwin_ref[0] = dot(x, dpre, 0, 0)
    dwout_ref[0] = dot(hid, dy, 0, 0)


def experts(x, w_in, w_out):
    n, rows = x.shape[:2]
    ff = w_in.shape[2]
    spec = lambda *s: pl.BlockSpec((1,) + s, lambda i: (i, 0, 0))
    return pl.pallas_call(
        expert_body,
        grid=(n,),
        in_specs=[spec(rows, 2 * D), spec(D, ff), spec(ff, D)],
        out_specs=[spec(rows, 2 * D), spec(D, ff), spec(ff, D)],
        out_shape=[sds(x.shape, BF), sds((n, D, ff)), sds((n, ff, D))],
        compiler_params=pltpu.CompilerParams(vmem_limit_bytes=LIMIT),
        name="experts",
    )(x, w_in, w_out)


def after_body(
    ret_ref, disp_ref, h1_ref, xn2_ref, gate_ref, cot_ref, routes_ref, wo_ref, att_ref, gain_ref,
    mixed_ref, dh1_ref, dat_ref, dout_ref, drouter_ref, dgain_ref,
):
    tok = h1_ref.shape[0]
    both = [dot(disp_ref[k], ret_ref[...]) for k in range(2)]
    gate = [gate_ref[:, k : k + 1] for k in range(2)]
    h1 = h1_ref[...]
    dy = cot_ref[...].astype(F32)
    picked = [both[k][:, :D] for k in range(2)]
    mixed_ref[...] = (h1 + (gate[0] * picked[0] + gate[1] * picked[1])).astype(BF)
    dgate = [jnp.sum(dy * picked[k], axis=-1, keepdims=True) for k in range(2)]
    mean = gate[0] * dgate[0] + gate[1] * dgate[1]
    lanes = lax.broadcasted_iota(jnp.int32, (tok, E), 1)
    dlog = jnp.zeros((tok, E), F32)
    for k in range(2):
        dlog = dlog + jnp.where(routes_ref[:, k : k + 1] == lanes, gate[k] * (dgate[k] - mean), 0.0)
    dlog = dlog.astype(BF)
    xn2 = xn2_ref[...]
    dxn = both[0][:, D:] + both[1][:, D:] + dot(dlog, wo_ref[:, D : D + E], 1, 1)
    drouter_ref[...] = dot(xn2, dlog, 0, 0).astype(BF)
    inv = lax.rsqrt(jnp.mean(h1 * h1, axis=-1, keepdims=True) + EPS)
    hat = h1 * inv
    dgain_ref[...] = jnp.sum((dxn * hat).reshape(tok // 8, 8, D), axis=0)
    cen = dxn * gain_ref[...]
    dh1 = dy + inv * (cen - hat * jnp.mean(cen * hat, axis=-1, keepdims=True))
    dh1_ref[...] = dh1
    dh1b = dh1.astype(BF)
    att = jnp.concatenate([att_ref[i] for i in range(G)], axis=1)
    dout_ref[...] = dot(att, dh1b, 0, 0).astype(BF)
    dat = dot(dh1b, wo_ref[:, :D], 1, 1).astype(BF)
    for i in range(G):
        dat_ref[i] = dat[:, i * GW : (i + 1) * GW]


def shards(tokens, routes, cotangent, gains, rel_bias, attn_qkv, attn_out, router, w_in, w_out):
    tok = tokens.shape[1]
    n_ctx, nf = lax.axis_size("ctx"), lax.axis_size("fsdp")
    n_dev = n_ctx * nf
    R, X = n_ctx // G, nf // CORES
    seq = tok * n_ctx
    per_dev = w_in.shape[0]
    qr, orows = attn_qkv.shape[0], attn_out.shape[0]
    x2, cot, route2 = tokens.reshape(tok, D), cotangent.reshape(tok, D), routes.reshape(tok, 2)

    n_gain, n_bias = gains.size, rel_bias.size
    tile = jnp.concatenate([gains.reshape(-1), rel_bias]).astype(F32)
    tile = jnp.broadcast_to(jnp.pad(tile, (0, 128 - n_gain - n_bias)), (8, 128))
    xall, wall, oall, tails = gather(n_ctx, nf, x2, attn_qkv, attn_out, router, tile)
    wall = wall.reshape(n_dev * qr, GW)
    wo = oall.reshape(D, D + 2 * E)
    tails = tails.reshape(n_dev, 8, 128)
    table = tails[:, 0, n_gain : n_gain + n_bias].reshape(H * NB)

    part = functools.partial
    width = math.gcd(n_ctx, 8)
    tiles_shape = (HG, n_ctx + R - 1, tok, tok)
    att, lse, q, k, v, tiles, gain1, gain2 = call(
        part(attend_body, n_ctx, nf),
        [sds((G, tok, GW), BF), sds((G, tok, 128)), sds((HG, G * tok, DH), BF)] + [sds((HG, seq, DH), BF)] * 2
        + [sds(tiles_shape), sds((1, D)), sds((1, D))],
        [xall, wall, tails, table],
        in_specs=[VM, VM, VM, SM],
        name="attend",
    )
    att_in = swap(n_ctx, nf, att, 2, "swap_att")[0]
    h1, xn2, gate, disp, packed = call(
        middle_body,
        [sds((tok, D)), sds((tok, D), BF), sds((tok, 2)), sds((2, tok, E * CAP), BF), sds((E * CAP, 2 * D), BF)],
        [att_in, x2, wo, gain2, route2, cot],
        name="middle",
    )
    recv = dispatch(n_ctx, nf, packed.reshape(n_ctx, per_dev, CAP, 2 * D))
    rows = nf * n_ctx * CAP
    part_rows, d_w_in, d_w_out = experts(recv.reshape(per_dev, rows, 2 * D), w_in, w_out)
    ret = combine(n_ctx, nf, part_rows.reshape(per_dev, nf, n_ctx, CAP, 2 * D))
    mixed, dh1, dat, d_out, d_router, dgain2 = call(
        after_body,
        [sds((tok, D), BF), sds((tok, D)), sds((G, tok, GW), BF), sds((D, D), BF), sds((D, E), BF), sds((8, D))],
        [ret.reshape(E * CAP, 2 * D), disp, h1, xn2, gate, cot, route2, wo, att_in, gain2],
        name="after",
    )
    lead = (G, R, X, CORES)
    more = (d_out.reshape(lead + (orows, D)), d_router.reshape(lead + router.shape))
    do = swap(n_ctx, nf, dat, 5, "swap_dat")[0]
    dx, dw, dgain1, dtab = call(
        part(attend_back_body, n_ctx, nf),
        [sds((n_ctx, tok, D), BF), sds((3 * D, GW), BF), sds((8, D)), sds((HG, NB, 8, tok))],
        [xall, wall, gain1, tiles, lse, q, k, v, att, do],
        scratch=[
            pltpu.VMEM(tiles_shape, F32), pltpu.VMEM((HG, seq, DH), F32), pltpu.VMEM((HG, seq, DH), F32),
            pltpu.VMEM((width, tok, D), BF), pltpu.VMEM((G, tok, GW), BF), pltpu.VMEM((2, width, tok, GW), BF),
            pltpu.VMEM((2, D, GW) if width < n_ctx else (2, 8, GW), F32),
        ],
        name="attend_back",
        limit=LIMIT if width == n_ctx else 61 * 1024 * 1024,
    )
    dtab = jnp.sum(dtab, axis=(2, 3)).reshape(1, HG * NB)
    own_group = jnp.arange(G)[:, None] == lax.axis_index("ctx") // R
    dtab = jnp.where(own_group, dtab, 0.0).reshape(n_dev, n_bias)
    dgains = jnp.stack([jnp.sum(dgain1, axis=0), jnp.sum(dgain2, axis=0)])
    dgains = dgains.reshape(2, n_dev, -1).transpose(1, 0, 2).reshape(n_dev, n_gain)
    d_tail = jnp.pad(jnp.concatenate([dgains, dtab], axis=1), ((0, 0), (0, 128 - n_gain - n_bias)))
    d_tail = jnp.broadcast_to(d_tail[:, None, :], (n_dev, 8, 128)).reshape(lead + (8, 128))
    d_tokens, d_qkv, tail_mine, d_out_mine, d_router_mine = reduce_all(
        n_ctx, nf, dx, dw.reshape(lead + (qr, GW)), d_tail, *more, x2, gain1
    )
    return (
        mixed.reshape(1, tok, D),
        (dh1 + d_tokens).reshape(1, tok, D),
        tail_mine[0, :n_gain].reshape(gains.shape),
        tail_mine[0, n_gain : n_gain + n_bias],
        d_qkv,
        d_out_mine,
        d_router_mine,
        d_w_in,
        d_w_out,
    )


def solution(mesh):
    return jax.shard_map(
        shards,
        mesh=mesh,
        in_specs=(
            P("fsdp", "ctx", None),
            P("fsdp", "ctx", None),
            P("fsdp", "ctx", None),
            P(None, ("ctx", "fsdp")),
            P(("ctx", "fsdp")),
            P(("ctx", "fsdp"), None),
            P(("ctx", "fsdp"), None),
            P(("ctx", "fsdp"), None),
            P("ctx", None, "fsdp"),
            P("ctx", "fsdp", None),
        ),
        out_specs=(
            P("fsdp", "ctx", None),
            P("fsdp", "ctx", None),
            P(None, ("ctx", "fsdp")),
            P(("ctx", "fsdp")),
            P(("ctx", "fsdp"), None),
            P(("ctx", "fsdp"), None),
            P(("ctx", "fsdp"), None),
            P("ctx", None, "fsdp"),
            P("ctx", "fsdp", None),
        ),
        check_vma=False,
    )
```
